32 devices in a mesh: blk: 8 (over z, x), map: 4 (over y, core).
Axes of the slice: x: 2, y: 2, z: 4, core: 2. Of those that a mesh axis runs over, the one named last changes fastest.
Arguments:
- sky_maps: bfloat16 [32, 10, 32768], P(('blk', 'map')), may hold values from -6 to 6
- cycle_number: int32 [32], replicated, may hold values from 8192 to 24576
- legendre_starts: float32 [2, 512, 64, 32], P(None, 'blk', 'map'), may hold values from -6 to 6
Outputs:
- harmonics: bfloat16 [512, 20, 8192], P('blk', None, 'map')
- spectra: float32 [4, 10, 10, 2048], P('map', None, None, 'blk')
The draws below stay inside these ranges and needn't reach their ends.
All inputs are finite; a program needn't handle non-finite values.
Results may differ from the reference program's by a relative error of at most 0.0071.
Values may be sent and summed in bfloat16 or wider, within the bound.
A program may use at most 128 MiB of HBM per device.

```python
import math
import jax
import jax.numpy as jnp
from jax import lax

NSIDE = 8192
CYCLE_LEN = 32768
NMAPS = 10
RES = 128
MGRP = 4
MSTART = 4096
LSTART = 8192
L = 8192
LBLK = 128
CYCLES = 32
N_MAP = 4


def place_ends(values, rng, low, top_value):
    extent = values.shape
    index_at = [jax.random.randint(jax.random.fold_in(rng, axis), (), 0, extent[axis]) for axis in range(len(extent))]
    values = values.at[tuple(index_at)].set(low)
    longest = extent.index(max(extent))
    index_at[longest] = (index_at[longest] + 1) % extent[longest]
    return values.at[tuple(index_at)].set(top_value)


def block_scale(rng, extent, pieces, least, largest):
    loudness, own = 1.0, jax.random.fold_in(rng, 6)
    for position, blocks in pieces:
        steps = jnp.exp(jax.random.uniform(jax.random.fold_in(own, position), (blocks,), jnp.float32, least / len(pieces), largest / len(pieces)))
        loudness = loudness * jnp.repeat(steps, extent[position] // blocks).reshape([-1 if axis == position else 1 for axis in range(len(extent))])
    return loudness


def gaussian(key, shape, scale, limit, cuts=(), kind=jnp.bfloat16):
    level = block_scale(key, shape, cuts, -0.22, 0.18) if cuts else 1.0
    values = jax.random.normal(key, shape, jnp.float32) * scale * level
    return jnp.minimum(jnp.maximum(values, -limit), limit).astype(kind)


def setup_inputs(seed: int = 0) -> dict:
    keys = jax.random.split(jax.random.key(seed), 4)
    sky_maps = gaussian(keys[0], (CYCLES, NMAPS, CYCLE_LEN), 1.0, 6.0, ((0, 32),))
    cycle_number = place_ends(jax.random.randint(keys[1], (CYCLES,), NSIDE, 3 * NSIDE + 1), jax.random.fold_in(keys[1], 1), NSIDE, 3 * NSIDE).astype(jnp.int32)
    legendre_starts = gaussian(keys[2], (2, MGRP * RES, L // LBLK, CYCLES), 1.0, 6.0, ((1, 8), (2, 4)), jnp.float32)
    return {"sky_maps": sky_maps, "cycle_number": cycle_number, "legendre_starts": legendre_starts}


def cycle_height(cycle_ids):
    return (4.0 * NSIDE - 2.0 * cycle_ids.astype(jnp.float32)) / (3.0 * NSIDE)

def dft_tables(cycle_len):
    low_len = cycle_len // RES
    residue = jnp.arange(RES, dtype=jnp.int32)
    turn_one = residue[:, None] * residue[None, :] % RES
    angle_one = 2.0 * math.pi / RES * turn_one.astype(jnp.float32)
    first_table = jnp.concatenate([jnp.cos(angle_one), -jnp.sin(angle_one)], axis=1).astype(jnp.bfloat16)
    column_group = jnp.arange(MGRP, dtype=jnp.int32)
    sample = jnp.arange(low_len, dtype=jnp.int32)
    m_value = MSTART + RES * column_group[:, None, None] + residue[None, None, :]
    turn_two = m_value * sample[None, :, None] % cycle_len
    angle_two = 2.0 * math.pi / cycle_len * turn_two.astype(jnp.float32)
    twiddle_re = jnp.cos(angle_two).astype(jnp.bfloat16)
    twiddle_im = (-jnp.sin(angle_two)).astype(jnp.bfloat16)
    return (first_table, twiddle_re, twiddle_im)

def cycle_transform(cycle_rows, parity, tables):
    first_table, twiddle_re, twiddle_im = tables
    cycle_count, maps_count, cycle_len = cycle_rows.shape
    low_len = cycle_len // RES
    folded = cycle_rows.reshape(cycle_count, maps_count, RES, low_len).astype(jnp.float32)
    section_one = jnp.einsum('rnaj,ak->rnjk', folded, first_table.astype(jnp.float32))
    section_one = lax.optimization_barrier(section_one.astype(jnp.bfloat16)).astype(jnp.float32)
    part_re = section_one[..., :RES]
    part_im = section_one[..., RES:]
    wave_re = twiddle_re.astype(jnp.float32)
    wave_im = twiddle_im.astype(jnp.float32)
    real_sum = jnp.einsum('rnjk,cjk->rnck', part_re, wave_re) - jnp.einsum('rnjk,cjk->rnck', part_im, wave_im)
    imag_sum = jnp.einsum('rnjk,cjk->rnck', part_im, wave_re) + jnp.einsum('rnjk,cjk->rnck', part_re, wave_im)
    column_group = jnp.arange(MGRP, dtype=jnp.int32)
    residue = jnp.arange(RES, dtype=jnp.int32)
    m_value = MSTART + RES * column_group[:, None] + residue[None, :]
    shifted = m_value[None, :, :] * parity[:, None, None] % (2 * cycle_len)
    phase_angle = math.pi / cycle_len * shifted.astype(jnp.float32)
    cos_part = jnp.cos(phase_angle)[:, None]
    sin_part = jnp.sin(phase_angle)[:, None]
    factor = 1.0 / math.sqrt(cycle_len)
    out_re = factor * (cos_part * real_sum + sin_part * imag_sum)
    out_im = factor * (cos_part * imag_sum - sin_part * real_sum)
    return jnp.stack([out_re, out_im], axis=1).astype(jnp.bfloat16)

def legendre_rows(start_pair, height, m_float, first_l):
    m_column = m_float[:, None]

    def recur_coef(degree):
        return jnp.sqrt((4.0 * degree * degree - 1.0) / ((degree - m_column) * (degree + m_column)))
    base_l = first_l.astype(jnp.float32)
    value_older = start_pair[0]
    value_newer = start_pair[1]
    prior_coef = recur_coef(base_l - 1.0)
    height_row = height[None, :]
    stacked_rows = []
    for offset in range(LBLK):
        present_coef = recur_coef(base_l + offset)
        value_now = present_coef * (height_row * value_newer - value_older / prior_coef)
        stacked_rows.append(value_now)
        value_older = value_newer
        value_newer = value_now
        prior_coef = present_coef
    return jnp.stack(stacked_rows, axis=1)

def reference(sky_maps, cycle_number, legendre_starts):
    cycle_count, maps_count, cycle_len = sky_maps.shape
    tables = dft_tables(cycle_len)
    parity = (cycle_number - NSIDE + 1) % 2
    block_rows = 8
    folded_maps = sky_maps.reshape(cycle_count // block_rows, block_rows, maps_count, cycle_len)
    folded_parity = parity.reshape(cycle_count // block_rows, block_rows)

    def transform_block(inputs):
        return cycle_transform(inputs[0], inputs[1], tables)
    cycle_modes = lax.map(transform_block, (folded_maps, folded_parity))
    cycle_modes = cycle_modes.reshape(cycle_count, 2, maps_count, MGRP, RES)
    total_cols = MGRP * RES
    ordered = jnp.transpose(cycle_modes, (4, 3, 1, 2, 0)).reshape(total_cols, 2 * maps_count, cycle_count)
    modes_wide = ordered.astype(jnp.float32)
    heights = cycle_height(cycle_number)
    column = jnp.arange(total_cols, dtype=jnp.int32)
    m_float = (MSTART + RES * (column % MGRP) + column // MGRP).astype(jnp.float32)
    cycle_scale = 1.0 / math.sqrt(cycle_count)

    def one_block(block_index):
        start_pair = lax.dynamic_index_in_dim(legendre_starts, block_index, 2, keepdims=False)
        first_l = LSTART + block_index * LBLK
        legendre_tile = legendre_rows(start_pair, heights, m_float, first_l)
        legendre_tile = lax.optimization_barrier(legendre_tile.astype(jnp.bfloat16)).astype(jnp.float32)
        projected = jnp.einsum('qlr,qnr->qnl', legendre_tile, modes_wide) * cycle_scale
        return projected.astype(jnp.bfloat16)
    blocks_out = lax.map(one_block, jnp.arange(L // LBLK, dtype=jnp.int32))
    harmonics = jnp.transpose(blocks_out, (1, 2, 0, 3)).reshape(total_cols, 2 * maps_count, L)
    split_harm = harmonics.astype(jnp.float32).reshape(total_cols, 2, maps_count, L)
    cross_sum = jnp.einsum('qcil,qcjl->ijl', split_harm, split_harm) / total_cols
    spectra = jnp.transpose(cross_sum.reshape(maps_count, maps_count, N_MAP, L // N_MAP), (2, 0, 1, 3))
    return (harmonics, spectra)
```

```python
import functools
import math

import jax
import jax.numpy as jnp
import numpy as np
from jax import lax
from jax.experimental import pallas as pl
from jax.experimental.pallas import tpu as pltpu
from jax.sharding import PartitionSpec as P

NSIDE = 8192
RES = 128
MGRP = 4
MSTART = 4096
LSTART = 8192
LBLK = 128


def shortened(array):

    def short(part):
        return part.astype(jnp.bfloat16) if part.dtype == jnp.float32 else part

    return jax.tree.map(short, array)


def cycle_height(cycle_ids):
    return (4.0 * NSIDE - 2.0 * cycle_ids.astype(jnp.float32)) / (3.0 * NSIDE)


def dft_tables(cycle_len):
    low_len = cycle_len // RES
    residue = jnp.arange(RES, dtype=jnp.int32)
    turn_one = residue[:, None] * residue[None, :] % RES
    angle_one = 2.0 * math.pi / RES * turn_one.astype(jnp.float32)
    first_table = jnp.concatenate([jnp.cos(angle_one), -jnp.sin(angle_one)], axis=1).astype(
        jnp.bfloat16
    )
    column_group = jnp.arange(MGRP, dtype=jnp.int32)
    sample = jnp.arange(low_len, dtype=jnp.int32)
    m_value = MSTART + RES * column_group[:, None, None] + residue[None, None, :]
    turn_two = m_value * sample[None, :, None] % cycle_len
    angle_two = 2.0 * math.pi / cycle_len * turn_two.astype(jnp.float32)
    twiddle_re = jnp.cos(angle_two).astype(jnp.bfloat16)
    twiddle_im = (-jnp.sin(angle_two)).astype(jnp.bfloat16)
    return (first_table, twiddle_re, twiddle_im)


def cycle_transform(cycle_rows, parity, tables):
    first_table, twiddle_re, twiddle_im = tables
    cycle_count, maps_count, cycle_len = cycle_rows.shape
    low_len = cycle_len // RES
    folded = cycle_rows.reshape(cycle_count, maps_count, RES, low_len)
    section_one = jnp.einsum(
        "rnaj,ak->rnjk", folded, first_table, preferred_element_type=jnp.float32
    )
    section_one = section_one.astype(jnp.bfloat16)
    part_re = section_one[..., :RES]
    part_im = section_one[..., RES:]
    real_sum = jnp.einsum(
        "rnjk,cjk->rnck", part_re, twiddle_re, preferred_element_type=jnp.float32
    ) - jnp.einsum("rnjk,cjk->rnck", part_im, twiddle_im, preferred_element_type=jnp.float32)
    imag_sum = jnp.einsum(
        "rnjk,cjk->rnck", part_im, twiddle_re, preferred_element_type=jnp.float32
    ) + jnp.einsum("rnjk,cjk->rnck", part_re, twiddle_im, preferred_element_type=jnp.float32)
    column_group = jnp.arange(MGRP, dtype=jnp.int32)
    residue = jnp.arange(RES, dtype=jnp.int32)
    m_value = MSTART + RES * column_group[:, None] + residue[None, :]
    shifted = m_value[None, :, :] * parity[:, None, None] % (2 * cycle_len)
    phase_angle = math.pi / cycle_len * shifted.astype(jnp.float32)
    cos_part = jnp.cos(phase_angle)[:, None]
    sin_part = jnp.sin(phase_angle)[:, None]
    factor = 1.0 / math.sqrt(cycle_len)
    out_re = factor * (cos_part * real_sum + sin_part * imag_sum)
    out_im = factor * (cos_part * imag_sum - sin_part * real_sum)
    return jnp.stack([out_re, out_im], axis=1).astype(jnp.bfloat16)


def legendre_rows(start_pair, height, m_float, first_l):
    m_column = m_float[:, None]

    def recur_coef(degree):
        return jnp.sqrt((4.0 * degree * degree - 1.0) / ((degree - m_column) * (degree + m_column)))

    base_l = first_l.astype(jnp.float32)
    value_older = start_pair[0]
    value_newer = start_pair[1]
    prior_coef = recur_coef(base_l - 1.0)
    height_row = height[None, :]
    stacked_rows = []
    for offset in range(LBLK):
        present_coef = recur_coef(base_l + offset)
        value_now = present_coef * (height_row * value_newer - value_older / prior_coef)
        stacked_rows.append(value_now)
        value_older = value_newer
        value_newer = value_now
        prior_coef = present_coef
    return jnp.stack(stacked_rows, axis=1)


STEP_LANES = 1024
KDIM = 256
GAP = 8
RUN = 16
PACK = 16


def project_kernel(dims, starts_ref, z_ref, turned_ref, pieces_ref, modes_ref, harm_ref, leg_ref):
    blocks, cycles, maps, q_group, scale = dims
    step = pl.program_id(0)
    groups = STEP_LANES // KDIM
    halves = STEP_LANES // 128
    parts = 2 * maps

    q_row = lax.broadcasted_iota(jnp.int32, (256, STEP_LANES), 0)
    q_lane = lax.broadcasted_iota(jnp.int32, (256, STEP_LANES), 1) // cycles + step * (
        STEP_LANES // cycles
    )
    spread = jnp.where((q_row % 64 == q_lane) & (q_row < 192), 1.0, 0.0).astype(jnp.bfloat16)

    run = RUN

    def recur(i, carry):
        older, newer = carry
        rows = pl.ds(pl.multiple_of(i * run * blocks, run * blocks), run * blocks)
        kap = jnp.dot(pieces_ref[rows, :], spread, preferred_element_type=jnp.float32)
        for j in range(run):
            now = (kap[j * blocks : (j + 1) * blocks] * z_ref[...]) * newer - older
            for half in range(blocks // 8):
                at = pl.ds(half * 8 * (LBLK + GAP) + i * run + j, 8, stride=LBLK + GAP)
                for g in range(halves):
                    leg_ref[g, at, :] = now[half * 8 : half * 8 + 8, g * 128 : g * 128 + 128]
            older, newer = newer, now
        return older, newer

    lax.fori_loop(0, LBLK // run, recur, (starts_ref[0], starts_ref[1]))

    rows_all = parts * q_group
    row = lax.broadcasted_iota(jnp.int32, (rows_all, 128), 0)
    lane = lax.broadcasted_iota(jnp.int32, (rows_all, 128), 1)
    picked = (row % MGRP) * parts + row // q_group == lane
    row = lax.broadcasted_iota(jnp.int32, (rows_all, KDIM), 0)
    lane = lax.broadcasted_iota(jnp.int32, (rows_all, KDIM), 1)
    same_q = row % q_group == lane // cycles
    cyc = lax.broadcasted_iota(jnp.int32, (cycles, KDIM), 0)
    lane_c = lax.broadcasted_iota(jnp.int32, (cycles, KDIM), 1) % cycles
    tile = jnp.where(cyc == lane_c, 1.0, 0.0).astype(jnp.bfloat16)
    row_k = lax.broadcasted_iota(jnp.int32, (rows_all, 128), 0) % q_group // MGRP
    per_group = q_group // MGRP
    weights = []
    for g in range(groups):
        narrow = jnp.zeros((rows_all, cycles), jnp.float32)
        for k in range(per_group):
            pick = jnp.where(picked & (row_k == k), 1.0, 0.0).astype(jnp.bfloat16)
            narrow = narrow + lax.dot_general(
                pick, modes_ref[g * per_group + k], (((1,), (1,)), ((), ())),
                preferred_element_type=jnp.float32,
            )
        wide = jnp.dot(narrow.astype(jnp.bfloat16), tile, preferred_element_type=jnp.float32)
        weights.append(jnp.where(same_q, wide, 0.0).astype(jnp.bfloat16))

    def project(u, _):
        cols = pl.ds(pl.multiple_of(u * 2 * LBLK, 2 * LBLK), 2 * LBLK)
        sources = [
            pl.ds(pl.multiple_of((2 * u + x) * (LBLK + GAP), 8), LBLK) for x in range(2)
        ]
        for g in range(groups):
            first = pl.multiple_of((step * groups + g) * q_group, 8)
            p_rows = jnp.concatenate(
                [turned_ref[2 * u + x, pl.ds(first, q_group), :] for x in range(2)], axis=1
            ) * scale
            leg = jnp.concatenate(
                [
                    jnp.concatenate(
                        [leg_ref[g * (KDIM // 128) + h, src, :] for h in range(KDIM // 128)],
                        axis=1,
                    )
                    for src in sources
                ],
                axis=0,
            ).astype(jnp.bfloat16)
            out = lax.dot_general(
                weights[g], leg, (((1,), (1,)), ((), ())), preferred_element_type=jnp.float32
            )
            crossed = out.reshape(parts, q_group, 2 * LBLK) * p_rows[None]
            harm_ref[:, g * q_group : (g + 1) * q_group, cols] = crossed.astype(jnp.bfloat16)
        return 0

    lax.fori_loop(0, blocks // 2, project, 0)


def project_blocks(legendre_starts, m_float, first_l, prepared, maps_count, cycle_scale):
    modes, pieces, turned, z_row = prepared
    local_cols, block_count, cycles = legendre_starts.shape[1:]
    local_len = block_count * LBLK
    q_group = KDIM // cycles
    parts = 2 * maps_count
    base_l = first_l.astype(jnp.float32) + LBLK * jnp.arange(block_count, dtype=jnp.float32)
    degree = base_l[None, :] - 1.0
    m_col = m_float[:, None]
    coef = jnp.sqrt((4.0 * degree * degree - 1.0) / ((degree - m_col) * (degree + m_col)))
    starts = jnp.stack([legendre_starts[0] / coef[:, :, None], legendre_starts[1]])
    starts = jnp.transpose(starts, (0, 2, 1, 3)).reshape(2, block_count, local_cols * cycles)
    groups = STEP_LANES // KDIM
    step_cols = groups * q_group
    dims = (block_count, cycles, maps_count, q_group, cycle_scale)
    whole = lambda shape: pl.BlockSpec(shape, lambda i: (0,) * len(shape))
    return pl.pallas_call(
        functools.partial(project_kernel, dims),
        grid=(local_cols // step_cols,),
        out_shape=jax.ShapeDtypeStruct((parts, local_cols, local_len), jnp.bfloat16),
        in_specs=[
            pl.BlockSpec((2, block_count, STEP_LANES), lambda i: (0, 0, i)),
            whole((1, STEP_LANES)),
            whole(turned.shape),
            whole(pieces.shape),
            pl.BlockSpec((step_cols // MGRP, cycles, 128), lambda i: (i, 0, 0)),
        ],
        out_specs=pl.BlockSpec((parts, step_cols, local_len), lambda i: (0, i, 0)),
        scratch_shapes=[
            pltpu.VMEM((STEP_LANES // 128, block_count * (LBLK + GAP), 128), jnp.float32),
        ],
        compiler_params=pltpu.CompilerParams(vmem_limit_bytes=60 * 1024 * 1024),
    )(starts, z_row, turned, pieces, modes)


def modes_kernel(
    totals, number_ref, sky_ref, first_ref, wr_ref, wi_ref, phase_ref,
    out_ref, pieces_ref, scales_ref, z_ref, rows_ref, turned_ref, held_ref, p_ref,
    send_sem, recv_sem,
):
    blk_total, map_total, factor = totals
    maps = sky_ref.shape[0]
    count = blk_total * map_total
    me_blk, me_map = lax.axis_index("blk"), lax.axis_index("map")
    me = me_blk * map_total + me_map
    share = RES // blk_total
    barrier = pltpu.get_barrier_semaphore()
    for i in range(1, count):
        peer = lax.rem(me + i, count)
        pl.semaphore_signal(
            barrier, inc=1,
            device_id={"blk": peer // map_total, "map": lax.rem(peer, map_total)},
            device_id_type=pl.DeviceIdType.MESH,
        )
    rows_ref[...] = jnp.zeros_like(rows_ref)
    first = first_ref[...]
    parity = (number_ref[me] - NSIDE + 1) % 2
    odd = jnp.full((MGRP, RES), parity, jnp.int32) == 1
    cosines = jnp.where(odd, phase_ref[:MGRP], 1.0)
    sines = jnp.where(odd, phase_ref[MGRP:], 0.0)
    for n in range(maps):
        section = lax.dot_general(
            sky_ref[n], first, (((0,), (0,)), ((), ())), preferred_element_type=jnp.float32
        )
        section = section.astype(jnp.bfloat16).astype(jnp.float32)
        part_re, part_im = section[:, :RES], section[:, RES:]
        for c in range(MGRP):
            wave_re = wr_ref[c].astype(jnp.float32)
            wave_im = wi_ref[c].astype(jnp.float32)
            real = jnp.sum(wave_re * part_re - wave_im * part_im, axis=0, keepdims=True)
            imag = jnp.sum(wave_re * part_im + wave_im * part_re, axis=0, keepdims=True)
            cos, sin = cosines[c : c + 1], sines[c : c + 1]
            row = c * 2 * maps + n
            rows_ref[row : row + 1, :] = factor * (cos * real + sin * imag)
            rows_ref[row + maps : row + maps + 1, :] = factor * (cos * imag - sin * real)
    turned_ref[...] = rows_ref[...].T.astype(jnp.bfloat16)
    pl.semaphore_wait(barrier, count - 1)

    def copy_to(peer, source):
        target_blk = peer // map_total
        return pltpu.make_async_remote_copy(
            src_ref=turned_ref.at[pl.ds(pl.multiple_of(target_blk * share, share), share)],
            dst_ref=held_ref.at[source],
            send_sem=send_sem.at[peer],
            recv_sem=recv_sem.at[source],
            device_id={"blk": target_blk, "map": lax.rem(peer, map_total)},
            device_id_type=pl.DeviceIdType.MESH,
        )

    for i in range(1, count):
        copy_to(lax.rem(me + i, count), me).start()
    held_ref[me] = turned_ref[pl.ds(pl.multiple_of(me_blk * share, share), share), :]
    prepare(blk_total, number_ref, pieces_ref, scales_ref, z_ref, p_ref)
    for i in range(1, count):
        peer = lax.rem(me + i, count)
        copy_to(peer, peer).wait_recv()
    for i in range(1, count):
        copy_to(lax.rem(me + i, count), me).wait_send()
    gathered = held_ref[...].astype(jnp.float32)
    out_ref[...] = jnp.swapaxes(gathered, 0, 1).astype(jnp.bfloat16)


def prepare(blk_total, number_ref, pieces_ref, scales_ref, z_ref, p_ref):
    blocks = scales_ref.shape[0]
    local_cols = MGRP * RES // blk_total
    lane = lax.broadcasted_iota(jnp.int32, z_ref.shape, 1) % number_ref.shape[0]
    numbers = jnp.zeros(z_ref.shape, jnp.int32)
    for r in range(number_ref.shape[0]):
        numbers = jnp.where(lane == r, number_ref[r], numbers)
    z_ref[...] = cycle_height(numbers)
    lane = lax.broadcasted_iota(jnp.int32, (blocks, 256), 1)
    piece = lane // local_cols
    column = lax.axis_index("blk") * local_cols + lane % local_cols
    m_row = (MSTART + RES * (column % MGRP) + column // MGRP).astype(jnp.float32)
    block = lax.broadcasted_iota(jnp.int32, (blocks, 256), 0)
    base = LSTART + (lax.axis_index("map") * blocks + block) * LBLK

    def setup(j, carry):
        p_prev, q_prev = carry
        degree = (base + j).astype(jnp.float32)
        num = 4.0 * degree * degree - 1.0
        den = (degree - m_row) * (degree + m_row)
        root = lax.rsqrt(num * den)
        kappa = p_prev * p_prev
        high = kappa.astype(jnp.bfloat16).astype(jnp.float32)
        rest = kappa - high
        mid = rest.astype(jnp.bfloat16).astype(jnp.float32)
        low = rest - mid
        pieces = jnp.where(piece == 0, high, jnp.where(piece == 1, mid, low))
        pieces_ref[pl.ds(pl.multiple_of(j * blocks, blocks), blocks), :] = pieces.astype(
            jnp.bfloat16
        )
        p_now = num * root * q_prev
        q_now = den * root * p_prev
        for half in range(blocks // 8):
            p_ref[pl.ds(half * 8 * (LBLK + GAP) + j, 8, stride=LBLK + GAP), :] = p_now[
                half * 8 : half * 8 + 8, :128
            ]
        return p_now, q_now

    one = jnp.ones((blocks, 256), jnp.float32)
    lax.fori_loop(0, LBLK, setup, (one, one), unroll=4)

    def turn(t, _):
        turned = p_ref[pl.ds(pl.multiple_of(t * (LBLK + GAP), 8), LBLK), :].T
        scales_ref[t] = turned[:local_cols]
        return 0

    lax.fori_loop(0, blocks, turn, 0)


def exchange_modes(sky_maps, cycle_number, block_count, blk_total, map_total):
    _, maps, cycle_len = sky_maps.shape
    first_table, wave_re, wave_im = constant_tables(cycle_len)
    m_value = MSTART + np.arange(MGRP)[:, None] * RES + np.arange(RES)[None, :]
    angle = np.float32(math.pi / cycle_len) * (m_value % (2 * cycle_len)).astype(np.float32)
    phase = jnp.asarray(np.concatenate([np.cos(angle), np.sin(angle)], axis=0))
    count = blk_total * map_total
    return pl.pallas_call(
        functools.partial(modes_kernel, (blk_total, map_total, 1.0 / math.sqrt(cycle_len))),
        out_shape=(
            jax.ShapeDtypeStruct((RES // blk_total, count, 128), jnp.bfloat16),
            jax.ShapeDtypeStruct((block_count * LBLK, 256), jnp.bfloat16),
            jax.ShapeDtypeStruct((block_count, MGRP * RES // blk_total, LBLK), jnp.float32),
            jax.ShapeDtypeStruct((1, STEP_LANES), jnp.float32),
        ),
        in_specs=[pl.BlockSpec(memory_space=pltpu.SMEM)]
        + [pl.BlockSpec(memory_space=pltpu.VMEM)] * 5,
        out_specs=(pl.BlockSpec(memory_space=pltpu.VMEM),) * 4,
        scratch_shapes=[
            pltpu.VMEM((128, RES), jnp.float32),
            pltpu.VMEM((RES, 128), jnp.bfloat16),
            pltpu.VMEM((count, RES // blk_total, 128), jnp.bfloat16),
            pltpu.VMEM((block_count * (LBLK + GAP), 128), jnp.float32),
            pltpu.SemaphoreType.DMA((count,)),
            pltpu.SemaphoreType.DMA((count,)),
        ],
        compiler_params=pltpu.CompilerParams(collective_id=0, has_side_effects=True),
    )(cycle_number, sky_maps.reshape(maps, RES, cycle_len // RES), first_table, wave_re, wave_im, phase)


def constant_tables(cycle_len):
    low_len = cycle_len // RES
    residue = np.arange(RES)
    angle = np.float32(2.0 * math.pi / RES) * (
        residue[:, None] * residue[None, :] % RES
    ).astype(np.float32)
    first = np.concatenate([np.cos(angle), -np.sin(angle)], axis=1)
    m_value = MSTART + RES * np.arange(MGRP)[:, None, None] + residue[None, None, :]
    turn = m_value * np.arange(low_len)[None, :, None] % cycle_len
    angle = np.float32(2.0 * math.pi / cycle_len) * turn.astype(np.float32)
    short = lambda table: jnp.asarray(table.astype(jnp.bfloat16))
    return short(first), short(np.cos(angle)), short(-np.sin(angle))


def cross_kernel(
    dims, harm_ref, out_ref, share_ref, sums_ref, part_ref, held_ref, load_sem, send_sem, recv_sem
):
    blk_total, maps = dims
    me = lax.axis_index("blk")
    _, parts, local_cols, share = share_ref.shape
    pair_rows = part_ref.shape[1]
    pairs = [(i, k) for i in range(maps) for k in range(i, maps)]

    def load(s):
        peer = lax.rem(me + s, blk_total)
        return pltpu.make_async_copy(
            harm_ref.at[:, :, pl.ds(pl.multiple_of(peer * share, share), share)],
            share_ref.at[s - 1],
            load_sem.at[s - 1],
        )

    for s in range(1, blk_total + 1):
        load(s).start()
    barrier = pltpu.get_barrier_semaphore()
    for i in range(1, blk_total):
        pl.semaphore_signal(
            barrier, inc=1, device_id={"blk": lax.rem(me + i, blk_total)},
            device_id_type=pl.DeviceIdType.MESH,
        )

    row = lax.broadcasted_iota(jnp.int32, (pair_rows, pair_rows * PACK), 0)
    lane = lax.broadcasted_iota(jnp.int32, (pair_rows, pair_rows * PACK), 1)
    gather = jnp.where(lane // PACK == row, 1.0, 0.0).astype(jnp.bfloat16)
    for p in range(len(pairs), pair_rows):
        sums_ref[p * PACK : (p + 1) * PACK, :] = jnp.zeros((PACK, share), jnp.bfloat16)

    def products(s):
        load(s).wait()

        def one(half, _):
            cols = pl.ds(pl.multiple_of(half * 128, 128), 128)
            middle = (len(pairs) + 1) // 2
            for first, last in ((0, middle), (middle, len(pairs))):
                total = [None] * (last - first)
                for h in range(2):
                    for t in range(local_cols // PACK):
                        x = {}
                        for n in sorted({v for pair in pairs[first:last] for v in pair}):
                            x[n] = share_ref[s - 1, h * maps + n, t * PACK : (t + 1) * PACK, cols]
                        for p in range(first, last):
                            i, k = pairs[p]
                            term = x[i] * x[k]
                            had = total[p - first]
                            total[p - first] = term if had is None else had + term
                for p in range(first, last):
                    sums_ref[p * PACK : (p + 1) * PACK, cols] = total[p - first]
            return 0

        lax.fori_loop(0, share // 128, one, 0)
        peer = lax.rem(me + s, blk_total)
        part_ref[peer] = jnp.dot(
            gather, sums_ref[...], preferred_element_type=jnp.float32
        ).astype(jnp.bfloat16)

    def copy_to(peer, source):
        return pltpu.make_async_remote_copy(
            src_ref=part_ref.at[peer],
            dst_ref=held_ref.at[source],
            send_sem=send_sem.at[peer],
            recv_sem=recv_sem.at[source],
            device_id={"blk": peer},
            device_id_type=pl.DeviceIdType.MESH,
        )

    products(1)
    pl.semaphore_wait(barrier, blk_total - 1)
    copy_to(lax.rem(me + 1, blk_total), me).start()

    def send_next(s, _):
        products(s)
        copy_to(lax.rem(me + s, blk_total), me).start()
        return 0

    lax.fori_loop(2, blk_total, send_next, 0)
    products(blk_total)
    out_rows = maps * maps
    row = lax.broadcasted_iota(jnp.int32, (out_rows, pair_rows), 0)
    lane = lax.broadcasted_iota(jnp.int32, (out_rows, pair_rows), 1)
    low = jnp.minimum(row // maps, row % maps)
    high = jnp.maximum(row // maps, row % maps)
    pair_at = low * maps - low * (low - 1) // 2 + high - low
    unfold = jnp.where(lane == pair_at, 1.0, 0.0).astype(jnp.bfloat16)
    spread = lambda x: jnp.dot(unfold, x, preferred_element_type=jnp.float32)
    total = spread(part_ref[me])
    for i in range(1, blk_total):
        peer = lax.rem(me + blk_total - i, blk_total)
        copy_to(peer, peer).wait_recv()
        total = total + spread(held_ref[peer])
    out_ref[...] = total * (1.0 / (MGRP * RES))
    for i in range(1, blk_total):
        copy_to(lax.rem(me + i, blk_total), me).wait_send()


def total_cross(harmonics, maps, blk_total):
    parts, local_cols, local_len = harmonics.shape
    share = local_len // blk_total
    pair_rows = -(-(maps * (maps + 1) // 2) // 8) * 8
    held = pltpu.VMEM((blk_total, pair_rows, share), jnp.bfloat16)
    return pl.pallas_call(
        functools.partial(cross_kernel, (blk_total, maps)),
        out_shape=jax.ShapeDtypeStruct((maps * maps, share), jnp.float32),
        in_specs=[pl.BlockSpec(memory_space=pl.ANY)],
        out_specs=pl.BlockSpec(memory_space=pltpu.VMEM),
        scratch_shapes=[
            pltpu.VMEM((blk_total, parts, local_cols, share), jnp.bfloat16),
            pltpu.VMEM((pair_rows * PACK, share), jnp.bfloat16),
            held,
            held,
            pltpu.SemaphoreType.DMA((blk_total,)),
            pltpu.SemaphoreType.DMA((blk_total,)),
            pltpu.SemaphoreType.DMA((blk_total,)),
        ],
        compiler_params=pltpu.CompilerParams(
            collective_id=1, has_side_effects=True, vmem_limit_bytes=32 * 1024 * 1024
        ),
    )(harmonics)


def kernel_fits(own_cycles, blk_total, cycles, maps_count, block_count):
    local_cols = MGRP * RES // blk_total
    return (
        own_cycles == 1
        and local_cols == 64
        and KDIM % cycles == 0
        and KDIM // cycles == 8
        and 2 * maps_count * MGRP <= 128
        and block_count % 8 == 0
        and block_count % blk_total == 0
        and (block_count * LBLK // blk_total) % 128 == 0
    )


def fast_body(sky_maps, cycle_number, legendre_starts):
    _, maps_count, _ = sky_maps.shape
    map_total = lax.axis_size("map")
    blk_total = lax.axis_size("blk")
    local_cols, block_count, cycles = legendre_starts.shape[1:]
    prepared = exchange_modes(sky_maps, cycle_number, block_count, blk_total, map_total)
    column = lax.axis_index("blk") * local_cols + jnp.arange(local_cols, dtype=jnp.int32)
    m_float = (MSTART + RES * (column % MGRP) + column // MGRP).astype(jnp.float32)
    first_l = LSTART + lax.axis_index("map") * block_count * LBLK
    cycle_scale = 1.0 / math.sqrt(cycles)
    harmonics = project_blocks(
        legendre_starts, m_float, first_l, prepared, maps_count, cycle_scale
    )
    spectra = total_cross(harmonics, maps_count, blk_total)
    spectra = spectra.reshape(1, maps_count, maps_count, spectra.shape[1])
    return (jnp.transpose(harmonics, (1, 0, 2)), spectra)


def body(sky_maps, cycle_number, legendre_starts):
    own_cycles, maps_count, cycle_len = sky_maps.shape
    map_total = lax.axis_size("map")
    blk_total = lax.axis_size("blk")
    cycles, block_count = cycle_number.shape[0], legendre_starts.shape[2]
    if kernel_fits(own_cycles, blk_total, cycles, maps_count, block_count):
        return fast_body(sky_maps, cycle_number, legendre_starts)
    tables = dft_tables(cycle_len)
    first_row = (lax.axis_index("blk") * map_total + lax.axis_index("map")) * own_cycles
    own_numbers = lax.dynamic_slice_in_dim(cycle_number, first_row, own_cycles)
    parity = (own_numbers - NSIDE + 1) % 2
    local_modes = cycle_transform(sky_maps, parity, tables)
    grouped = lax.all_gather(local_modes, "map", axis=0, tiled=True)
    regrouped = lax.all_to_all(grouped, "blk", split_axis=4, concat_axis=0, tiled=True)
    ordered = jnp.transpose(regrouped, (4, 3, 1, 2, 0))
    local_cols = ordered.shape[0] * ordered.shape[1]
    cycle_modes = ordered.reshape(local_cols, 2 * maps_count, -1)
    heights = cycle_height(cycle_number)
    column = lax.axis_index("blk") * local_cols + jnp.arange(local_cols, dtype=jnp.int32)
    m_float = (MSTART + RES * (column % MGRP) + column // MGRP).astype(jnp.float32)
    block_count = legendre_starts.shape[2]
    local_len = block_count * LBLK
    first_l = LSTART + lax.axis_index("map") * local_len
    cycle_scale = 1.0 / math.sqrt(cycle_modes.shape[-1])

    def one_block(block_index):
        start_pair = lax.dynamic_index_in_dim(legendre_starts, block_index, 2, keepdims=False)
        legendre_tile = legendre_rows(
            start_pair, heights, m_float, first_l + block_index * LBLK
        ).astype(jnp.bfloat16)
        projected = (
            jnp.einsum(
                "qlr,qnr->qnl", legendre_tile, cycle_modes, preferred_element_type=jnp.float32
            )
            * cycle_scale
        )
        return projected.astype(jnp.bfloat16)

    blocks_out = lax.map(one_block, jnp.arange(block_count, dtype=jnp.int32))
    harmonics = jnp.transpose(blocks_out, (1, 2, 0, 3)).reshape(
        local_cols, 2 * maps_count, local_len
    )
    total_cols = MGRP * RES
    spread = harmonics.reshape(local_cols, 2 * maps_count, blk_total, local_len // blk_total)
    spread = jnp.transpose(spread, (2, 3, 1, 0))
    received = lax.all_to_all(
        shortened(spread), "blk", split_axis=0, concat_axis=3, tiled=True
    ).astype(spread.dtype)
    item_count = received.shape[1]
    split_piece = received.reshape(item_count, 2, maps_count, received.shape[3])
    cross_sum = jnp.einsum(
        "gciq,gcjq->ijg", split_piece, split_piece, preferred_element_type=jnp.float32
    )
    owned = (cross_sum / total_cols)[None]
    return (harmonics, owned)


def solution(mesh):
    return jax.shard_map(
        body,
        mesh=mesh,
        in_specs=(P(("blk", "map"), None, None), P(), P(None, "blk", "map", None)),
        out_specs=(P("blk", None, "map"), P("map", None, None, "blk")),
        check_vma=False,
    )
```

```python
import functools
import math

import jax
import jax.numpy as jnp
import numpy as np
from jax import lax
from jax.experimental import pallas as pl
from jax.experimental.pallas import tpu as pltpu
from jax.sharding import PartitionSpec as P

NSIDE = 8192
RES = 128
MGRP = 4
MSTART = 4096
LSTART = 8192
LBLK = 128


def shortened(array):

    def short(part):
        return part.astype(jnp.bfloat16) if part.dtype == jnp.float32 else part

    return jax.tree.map(short, array)


def cycle_height(cycle_ids):
    return (4.0 * NSIDE - 2.0 * cycle_ids.astype(jnp.float32)) / (3.0 * NSIDE)


def dft_tables(cycle_len):
    low_len = cycle_len // RES
    residue = jnp.arange(RES, dtype=jnp.int32)
    turn_one = residue[:, None] * residue[None, :] % RES
    angle_one = 2.0 * math.pi / RES * turn_one.astype(jnp.float32)
    first_table = jnp.concatenate([jnp.cos(angle_one), -jnp.sin(angle_one)], axis=1).astype(
        jnp.bfloat16
    )
    column_group = jnp.arange(MGRP, dtype=jnp.int32)
    sample = jnp.arange(low_len, dtype=jnp.int32)
    m_value = MSTART + RES * column_group[:, None, None] + residue[None, None, :]
    turn_two = m_value * sample[None, :, None] % cycle_len
    angle_two = 2.0 * math.pi / cycle_len * turn_two.astype(jnp.float32)
    twiddle_re = jnp.cos(angle_two).astype(jnp.bfloat16)
    twiddle_im = (-jnp.sin(angle_two)).astype(jnp.bfloat16)
    return (first_table, twiddle_re, twiddle_im)


def cycle_transform(cycle_rows, parity, tables):
    first_table, twiddle_re, twiddle_im = tables
    cycle_count, maps_count, cycle_len = cycle_rows.shape
    low_len = cycle_len // RES
    folded = cycle_rows.reshape(cycle_count, maps_count, RES, low_len)
    section_one = jnp.einsum(
        "rnaj,ak->rnjk", folded, first_table, preferred_element_type=jnp.float32
    )
    section_one = section_one.astype(jnp.bfloat16)
    part_re = section_one[..., :RES]
    part_im = section_one[..., RES:]
    real_sum = jnp.einsum(
        "rnjk,cjk->rnck", part_re, twiddle_re, preferred_element_type=jnp.float32
    ) - jnp.einsum("rnjk,cjk->rnck", part_im, twiddle_im, preferred_element_type=jnp.float32)
    imag_sum = jnp.einsum(
        "rnjk,cjk->rnck", part_im, twiddle_re, preferred_element_type=jnp.float32
    ) + jnp.einsum("rnjk,cjk->rnck", part_re, twiddle_im, preferred_element_type=jnp.float32)
    column_group = jnp.arange(MGRP, dtype=jnp.int32)
    residue = jnp.arange(RES, dtype=jnp.int32)
    m_value = MSTART + RES * column_group[:, None] + residue[None, :]
    shifted = m_value[None, :, :] * parity[:, None, None] % (2 * cycle_len)
    phase_angle = math.pi / cycle_len * shifted.astype(jnp.float32)
    cos_part = jnp.cos(phase_angle)[:, None]
    sin_part = jnp.sin(phase_angle)[:, None]
    factor = 1.0 / math.sqrt(cycle_len)
    out_re = factor * (cos_part * real_sum + sin_part * imag_sum)
    out_im = factor * (cos_part * imag_sum - sin_part * real_sum)
    return jnp.stack([out_re, out_im], axis=1).astype(jnp.bfloat16)


def legendre_rows(start_pair, height, m_float, first_l):
    m_column = m_float[:, None]

    def recur_coef(degree):
        return jnp.sqrt((4.0 * degree * degree - 1.0) / ((degree - m_column) * (degree + m_column)))

    base_l = first_l.astype(jnp.float32)
    value_older = start_pair[0]
    value_newer = start_pair[1]
    prior_coef = recur_coef(base_l - 1.0)
    height_row = height[None, :]
    stacked_rows = []
    for offset in range(LBLK):
        present_coef = recur_coef(base_l + offset)
        value_now = present_coef * (height_row * value_newer - value_older / prior_coef)
        stacked_rows.append(value_now)
        value_older = value_newer
        value_newer = value_now
        prior_coef = present_coef
    return jnp.stack(stacked_rows, axis=1)


STEP_LANES = 1024
KDIM = 256
GAP = 8
RUN = 64
PACK = 16


def project_kernel(dims, starts_ref, z_ref, turned_ref, pieces_ref, modes_ref, harm_ref, leg_ref):
    blocks, cycles, maps, q_group, scale = dims
    step = pl.program_id(0)
    groups = STEP_LANES // KDIM
    halves = STEP_LANES // 128
    parts = 2 * maps

    q_row = lax.broadcasted_iota(jnp.int32, (256, STEP_LANES), 0)
    q_lane = lax.broadcasted_iota(jnp.int32, (256, STEP_LANES), 1) // cycles + step * (
        STEP_LANES // cycles
    )
    spread = jnp.where((q_row % 64 == q_lane) & (q_row < 192), 1.0, 0.0).astype(jnp.bfloat16)

    run = RUN

    def recur(i, carry):
        older, newer = carry
        rows = pl.ds(pl.multiple_of(i * run * blocks, run * blocks), run * blocks)
        kap = jnp.dot(pieces_ref[rows, :], spread, preferred_element_type=jnp.float32)
        for j in range(run):
            now = (kap[j * blocks : (j + 1) * blocks] * z_ref[...]) * newer - older
            for half in range(blocks // 8):
                at = pl.ds(half * 8 * (LBLK + GAP) + i * run + j, 8, stride=LBLK + GAP)
                for g in range(halves):
                    leg_ref[g, at, :] = now[half * 8 : half * 8 + 8, g * 128 : g * 128 + 128]
            older, newer = newer, now
        return older, newer

    lax.fori_loop(0, LBLK // run, recur, (starts_ref[0], starts_ref[1]))

    rows_all = parts * q_group
    row = lax.broadcasted_iota(jnp.int32, (rows_all, 128), 0)
    lane = lax.broadcasted_iota(jnp.int32, (rows_all, 128), 1)
    picked = (row % MGRP) * parts + row // q_group == lane
    row = lax.broadcasted_iota(jnp.int32, (rows_all, KDIM), 0)
    lane = lax.broadcasted_iota(jnp.int32, (rows_all, KDIM), 1)
    same_q = row % q_group == lane // cycles
    cyc = lax.broadcasted_iota(jnp.int32, (cycles, KDIM), 0)
    lane_c = lax.broadcasted_iota(jnp.int32, (cycles, KDIM), 1) % cycles
    tile = jnp.where(cyc == lane_c, 1.0, 0.0).astype(jnp.bfloat16)
    row_k = lax.broadcasted_iota(jnp.int32, (rows_all, 128), 0) % q_group // MGRP
    per_group = q_group // MGRP
    weights = []
    for g in range(groups):
        narrow = jnp.zeros((rows_all, cycles), jnp.float32)
        for k in range(per_group):
            pick = jnp.where(picked & (row_k == k), 1.0, 0.0).astype(jnp.bfloat16)
            narrow = narrow + lax.dot_general(
                pick, modes_ref[g * per_group + k], (((1,), (1,)), ((), ())),
                preferred_element_type=jnp.float32,
            )
        wide = jnp.dot(narrow.astype(jnp.bfloat16), tile, preferred_element_type=jnp.float32)
        weights.append(jnp.where(same_q, wide, 0.0).astype(jnp.bfloat16))

    def project_two(i, _):
        project(2 * i)
        project(2 * i + 1)
        return 0

    def project(u):
        cols = pl.ds(pl.multiple_of(u * 2 * LBLK, 2 * LBLK), 2 * LBLK)
        sources = [
            pl.ds(pl.multiple_of((2 * u + x) * (LBLK + GAP), 8), LBLK) for x in range(2)
        ]
        for g in range(groups):
            first = pl.multiple_of((step * groups + g) * q_group, 8)
            p_rows = jnp.concatenate(
                [turned_ref[2 * u + x, pl.ds(first, q_group), :] for x in range(2)], axis=1
            ) * scale
            leg = jnp.concatenate(
                [
                    jnp.concatenate(
                        [leg_ref[g * (KDIM // 128) + h, src, :] for h in range(KDIM // 128)],
                        axis=1,
                    )
                    for src in sources
                ],
                axis=0,
            ).astype(jnp.bfloat16)
            out = lax.dot_general(
                weights[g], leg, (((1,), (1,)), ((), ())), preferred_element_type=jnp.float32
            )
            crossed = out.reshape(parts, q_group, 2 * LBLK) * p_rows[None]
            harm_ref[:, g * q_group : (g + 1) * q_group, cols] = crossed.astype(jnp.bfloat16)

    lax.fori_loop(0, blocks // 4, project_two, 0)


def project_blocks(legendre_starts, m_float, first_l, prepared, maps_count, cycle_scale):
    modes, pieces, turned, z_row = prepared
    local_cols, block_count, cycles = legendre_starts.shape[1:]
    local_len = block_count * LBLK
    q_group = KDIM // cycles
    parts = 2 * maps_count
    base_l = first_l.astype(jnp.float32) + LBLK * jnp.arange(block_count, dtype=jnp.float32)
    degree = base_l[None, :] - 1.0
    m_col = m_float[:, None]
    coef = jnp.sqrt((4.0 * degree * degree - 1.0) / ((degree - m_col) * (degree + m_col)))
    starts = jnp.stack([legendre_starts[0] / coef[:, :, None], legendre_starts[1]])
    starts = jnp.transpose(starts, (0, 2, 1, 3)).reshape(2, block_count, local_cols * cycles)
    groups = STEP_LANES // KDIM
    step_cols = groups * q_group
    dims = (block_count, cycles, maps_count, q_group, cycle_scale)
    whole = lambda shape: pl.BlockSpec(shape, lambda i: (0,) * len(shape))
    return pl.pallas_call(
        functools.partial(project_kernel, dims),
        grid=(local_cols // step_cols,),
        out_shape=jax.ShapeDtypeStruct((parts, local_cols, local_len), jnp.bfloat16),
        in_specs=[
            pl.BlockSpec((2, block_count, STEP_LANES), lambda i: (0, 0, i)),
            whole((1, STEP_LANES)),
            whole(turned.shape),
            whole(pieces.shape),
            pl.BlockSpec((step_cols // MGRP, cycles, 128), lambda i: (i, 0, 0)),
        ],
        out_specs=pl.BlockSpec((parts, step_cols, local_len), lambda i: (0, i, 0)),
        scratch_shapes=[
            pltpu.VMEM((STEP_LANES // 128, block_count * (LBLK + GAP), 128), jnp.float32),
        ],
        compiler_params=pltpu.CompilerParams(vmem_limit_bytes=60 * 1024 * 1024),
    )(starts, z_row, turned, pieces, modes)


def modes_kernel(
    totals, number_ref, sky_ref, first_ref, wr_ref, wi_ref, phase_ref,
    out_ref, pieces_ref, scales_ref, z_ref, rows_ref, turned_ref, held_ref, p_ref,
    send_sem, recv_sem,
):
    blk_total, map_total, factor = totals
    maps = sky_ref.shape[0]
    count = blk_total * map_total
    me_blk, me_map = lax.axis_index("blk"), lax.axis_index("map")
    me = me_blk * map_total + me_map
    share = RES // blk_total
    barrier = pltpu.get_barrier_semaphore()
    for i in range(1, count):
        peer = lax.rem(me + i, count)
        pl.semaphore_signal(
            barrier, inc=1,
            device_id={"blk": peer // map_total, "map": lax.rem(peer, map_total)},
            device_id_type=pl.DeviceIdType.MESH,
        )
    rows_ref[...] = jnp.zeros_like(rows_ref)
    first = first_ref[...]
    parity = (number_ref[me] - NSIDE + 1) % 2
    odd = jnp.full((MGRP, RES), parity, jnp.int32) == 1
    cosines = jnp.where(odd, phase_ref[:MGRP], 1.0)
    sines = jnp.where(odd, phase_ref[MGRP:], 0.0)
    for n in range(maps):
        section = lax.dot_general(
            sky_ref[n], first, (((0,), (0,)), ((), ())), preferred_element_type=jnp.float32
        )
        section = section.astype(jnp.bfloat16).astype(jnp.float32)
        part_re, part_im = section[:, :RES], section[:, RES:]
        for c in range(MGRP):
            wave_re = wr_ref[c].astype(jnp.float32)
            wave_im = wi_ref[c].astype(jnp.float32)
            real = jnp.sum(wave_re * part_re - wave_im * part_im, axis=0, keepdims=True)
            imag = jnp.sum(wave_re * part_im + wave_im * part_re, axis=0, keepdims=True)
            cos, sin = cosines[c : c + 1], sines[c : c + 1]
            row = c * 2 * maps + n
            rows_ref[row : row + 1, :] = factor * (cos * real + sin * imag)
            rows_ref[row + maps : row + maps + 1, :] = factor * (cos * imag - sin * real)
    turned_ref[...] = rows_ref[...].T.astype(jnp.bfloat16)
    pl.semaphore_wait(barrier, count - 1)

    def copy_to(peer, source):
        target_blk = peer // map_total
        return pltpu.make_async_remote_copy(
            src_ref=turned_ref.at[pl.ds(pl.multiple_of(target_blk * share, share), share)],
            dst_ref=held_ref.at[source],
            send_sem=send_sem.at[peer],
            recv_sem=recv_sem.at[source],
            device_id={"blk": target_blk, "map": lax.rem(peer, map_total)},
            device_id_type=pl.DeviceIdType.MESH,
        )

    for i in range(1, count):
        copy_to(lax.rem(me + i, count), me).start()
    held_ref[me] = turned_ref[pl.ds(pl.multiple_of(me_blk * share, share), share), :]
    prepare(blk_total, number_ref, pieces_ref, scales_ref, z_ref, p_ref)
    for i in range(1, count):
        peer = lax.rem(me + i, count)
        copy_to(peer, peer).wait_recv()
    for i in range(1, count):
        copy_to(lax.rem(me + i, count), me).wait_send()
    gathered = held_ref[...].astype(jnp.float32)
    out_ref[...] = jnp.swapaxes(gathered, 0, 1).astype(jnp.bfloat16)


def prepare(blk_total, number_ref, pieces_ref, scales_ref, z_ref, p_ref):
    blocks = scales_ref.shape[0]
    local_cols = MGRP * RES // blk_total
    lane = lax.broadcasted_iota(jnp.int32, z_ref.shape, 1) % number_ref.shape[0]
    numbers = jnp.zeros(z_ref.shape, jnp.int32)
    for r in range(number_ref.shape[0]):
        numbers = jnp.where(lane == r, number_ref[r], numbers)
    z_ref[...] = cycle_height(numbers)
    lane = lax.broadcasted_iota(jnp.int32, (blocks, 256), 1)
    piece = lane // local_cols
    column = lax.axis_index("blk") * local_cols + lane % local_cols
    m_row = (MSTART + RES * (column % MGRP) + column // MGRP).astype(jnp.float32)
    block = lax.broadcasted_iota(jnp.int32, (blocks, 256), 0)
    base = LSTART + (lax.axis_index("map") * blocks + block) * LBLK

    def setup(j, carry):
        p_prev, q_prev = carry
        degree = (base + j).astype(jnp.float32)
        num = 4.0 * degree * degree - 1.0
        den = (degree - m_row) * (degree + m_row)
        root = lax.rsqrt(num * den)
        kappa = p_prev * p_prev
        high = kappa.astype(jnp.bfloat16).astype(jnp.float32)
        rest = kappa - high
        mid = rest.astype(jnp.bfloat16).astype(jnp.float32)
        low = rest - mid
        pieces = jnp.where(piece == 0, high, jnp.where(piece == 1, mid, low))
        pieces_ref[pl.ds(pl.multiple_of(j * blocks, blocks), blocks), :] = pieces.astype(
            jnp.bfloat16
        )
        p_now = num * root * q_prev
        q_now = den * root * p_prev
        for half in range(blocks // 8):
            p_ref[pl.ds(half * 8 * (LBLK + GAP) + j, 8, stride=LBLK + GAP), :] = p_now[
                half * 8 : half * 8 + 8, :128
            ]
        return p_now, q_now

    one = jnp.ones((blocks, 256), jnp.float32)
    lax.fori_loop(0, LBLK, setup, (one, one), unroll=4)

    def turn(t, _):
        turned = p_ref[pl.ds(pl.multiple_of(t * (LBLK + GAP), 8), LBLK), :].T
        scales_ref[t] = turned[:local_cols]
        return 0

    lax.fori_loop(0, blocks, turn, 0)


def exchange_modes(sky_maps, cycle_number, block_count, blk_total, map_total):
    _, maps, cycle_len = sky_maps.shape
    first_table, wave_re, wave_im = constant_tables(cycle_len)
    m_value = MSTART + np.arange(MGRP)[:, None] * RES + np.arange(RES)[None, :]
    angle = np.float32(math.pi / cycle_len) * (m_value % (2 * cycle_len)).astype(np.float32)
    phase = jnp.asarray(np.concatenate([np.cos(angle), np.sin(angle)], axis=0))
    count = blk_total * map_total
    return pl.pallas_call(
        functools.partial(modes_kernel, (blk_total, map_total, 1.0 / math.sqrt(cycle_len))),
        out_shape=(
            jax.ShapeDtypeStruct((RES // blk_total, count, 128), jnp.bfloat16),
            jax.ShapeDtypeStruct((block_count * LBLK, 256), jnp.bfloat16),
            jax.ShapeDtypeStruct((block_count, MGRP * RES // blk_total, LBLK), jnp.float32),
            jax.ShapeDtypeStruct((1, STEP_LANES), jnp.float32),
        ),
        in_specs=[pl.BlockSpec(memory_space=pltpu.SMEM)]
        + [pl.BlockSpec(memory_space=pltpu.VMEM)] * 5,
        out_specs=(pl.BlockSpec(memory_space=pltpu.VMEM),) * 4,
        scratch_shapes=[
            pltpu.VMEM((128, RES), jnp.float32),
            pltpu.VMEM((RES, 128), jnp.bfloat16),
            pltpu.VMEM((count, RES // blk_total, 128), jnp.bfloat16),
            pltpu.VMEM((block_count * (LBLK + GAP), 128), jnp.float32),
            pltpu.SemaphoreType.DMA((count,)),
            pltpu.SemaphoreType.DMA((count,)),
        ],
        compiler_params=pltpu.CompilerParams(collective_id=0, has_side_effects=True),
    )(cycle_number, sky_maps.reshape(maps, RES, cycle_len // RES), first_table, wave_re, wave_im, phase)


def constant_tables(cycle_len):
    low_len = cycle_len // RES
    residue = np.arange(RES)
    angle = np.float32(2.0 * math.pi / RES) * (
        residue[:, None] * residue[None, :] % RES
    ).astype(np.float32)
    first = np.concatenate([np.cos(angle), -np.sin(angle)], axis=1)
    m_value = MSTART + RES * np.arange(MGRP)[:, None, None] + residue[None, None, :]
    turn = m_value * np.arange(low_len)[None, :, None] % cycle_len
    angle = np.float32(2.0 * math.pi / cycle_len) * turn.astype(np.float32)
    short = lambda table: jnp.asarray(table.astype(jnp.bfloat16))
    return short(first), short(np.cos(angle)), short(-np.sin(angle))


def cross_kernel(
    dims, harm_ref, out_ref, share_ref, sums_ref, part_ref, held_ref, load_sem, send_sem, recv_sem
):
    blk_total, maps = dims
    me = lax.axis_index("blk")
    _, parts, local_cols, share = share_ref.shape
    pair_rows = part_ref.shape[1]
    pairs = [(i, k) for i in range(maps) for k in range(i, maps)]

    def load(s):
        peer = lax.rem(me + s, blk_total)
        return pltpu.make_async_copy(
            harm_ref.at[:, :, pl.ds(pl.multiple_of(peer * share, share), share)],
            share_ref.at[s - 1],
            load_sem.at[s - 1],
        )

    for s in range(1, blk_total + 1):
        load(s).start()
    barrier = pltpu.get_barrier_semaphore()
    for i in range(1, blk_total):
        pl.semaphore_signal(
            barrier, inc=1, device_id={"blk": lax.rem(me + i, blk_total)},
            device_id_type=pl.DeviceIdType.MESH,
        )

    row = lax.broadcasted_iota(jnp.int32, (pair_rows, pair_rows * PACK), 0)
    lane = lax.broadcasted_iota(jnp.int32, (pair_rows, pair_rows * PACK), 1)
    gather = jnp.where(lane // PACK == row, 1.0, 0.0).astype(jnp.bfloat16)
    for p in range(len(pairs), pair_rows):
        sums_ref[p * PACK : (p + 1) * PACK, :] = jnp.zeros((PACK, share), jnp.bfloat16)

    def products(s):
        load(s).wait()

        def one(half, _):
            cols = pl.ds(pl.multiple_of(half * 128, 128), 128)
            middle = (len(pairs) + 1) // 2
            for first, last in ((0, middle), (middle, len(pairs))):
                total = [None] * (last - first)
                for h in range(2):
                    for t in range(local_cols // PACK):
                        x = {}
                        for n in sorted({v for pair in pairs[first:last] for v in pair}):
                            x[n] = share_ref[s - 1, h * maps + n, t * PACK : (t + 1) * PACK, cols]
                        for p in range(first, last):
                            i, k = pairs[p]
                            term = x[i] * x[k]
                            had = total[p - first]
                            total[p - first] = term if had is None else had + term
                for p in range(first, last):
                    sums_ref[p * PACK : (p + 1) * PACK, cols] = total[p - first]
            return 0

        lax.fori_loop(0, share // 128, one, 0)
        peer = lax.rem(me + s, blk_total)
        part_ref[peer] = jnp.dot(
            gather, sums_ref[...], preferred_element_type=jnp.float32
        ).astype(jnp.bfloat16)

    def copy_to(peer, source):
        return pltpu.make_async_remote_copy(
            src_ref=part_ref.at[peer],
            dst_ref=held_ref.at[source],
            send_sem=send_sem.at[peer],
            recv_sem=recv_sem.at[source],
            device_id={"blk": peer},
            device_id_type=pl.DeviceIdType.MESH,
        )

    products(1)
    pl.semaphore_wait(barrier, blk_total - 1)
    copy_to(lax.rem(me + 1, blk_total), me).start()

    def send_next(s, _):
        products(s)
        copy_to(lax.rem(me + s, blk_total), me).start()
        return 0

    lax.fori_loop(2, blk_total, send_next, 0)
    products(blk_total)
    out_rows = maps * maps
    row = lax.broadcasted_iota(jnp.int32, (out_rows, pair_rows), 0)
    lane = lax.broadcasted_iota(jnp.int32, (out_rows, pair_rows), 1)
    low = jnp.minimum(row // maps, row % maps)
    high = jnp.maximum(row // maps, row % maps)
    pair_at = low * maps - low * (low - 1) // 2 + high - low
    unfold = jnp.where(lane == pair_at, 1.0, 0.0).astype(jnp.bfloat16)
    spread = lambda x: jnp.dot(unfold, x, preferred_element_type=jnp.float32)
    total = spread(part_ref[me])
    for i in range(1, blk_total):
        peer = lax.rem(me + blk_total - i, blk_total)
        copy_to(peer, peer).wait_recv()
        total = total + spread(held_ref[peer])
    out_ref[...] = total * (1.0 / (MGRP * RES))
    for i in range(1, blk_total):
        copy_to(lax.rem(me + i, blk_total), me).wait_send()


def total_cross(harmonics, maps, blk_total):
    parts, local_cols, local_len = harmonics.shape
    share = local_len // blk_total
    pair_rows = -(-(maps * (maps + 1) // 2) // 8) * 8
    held = pltpu.VMEM((blk_total, pair_rows, share), jnp.bfloat16)
    return pl.pallas_call(
        functools.partial(cross_kernel, (blk_total, maps)),
        out_shape=jax.ShapeDtypeStruct((maps * maps, share), jnp.float32),
        in_specs=[pl.BlockSpec(memory_space=pl.ANY)],
        out_specs=pl.BlockSpec(memory_space=pltpu.VMEM),
        scratch_shapes=[
            pltpu.VMEM((blk_total, parts, local_cols, share), jnp.bfloat16),
            pltpu.VMEM((pair_rows * PACK, share), jnp.bfloat16),
            held,
            held,
            pltpu.SemaphoreType.DMA((blk_total,)),
            pltpu.SemaphoreType.DMA((blk_total,)),
            pltpu.SemaphoreType.DMA((blk_total,)),
        ],
        compiler_params=pltpu.CompilerParams(
            collective_id=1, has_side_effects=True, vmem_limit_bytes=60 * 1024 * 1024
        ),
    )(harmonics)


def kernel_fits(own_cycles, blk_total, cycles, maps_count, block_count):
    local_cols = MGRP * RES // blk_total
    return (
        own_cycles == 1
        and local_cols == 64
        and KDIM % cycles == 0
        and KDIM // cycles == 8
        and 2 * maps_count * MGRP <= 128
        and block_count % 8 == 0
        and block_count % blk_total == 0
        and (block_count * LBLK // blk_total) % 128 == 0
    )


def fast_body(sky_maps, cycle_number, legendre_starts):
    _, maps_count, _ = sky_maps.shape
    map_total = lax.axis_size("map")
    blk_total = lax.axis_size("blk")
    local_cols, block_count, cycles = legendre_starts.shape[1:]
    prepared = exchange_modes(sky_maps, cycle_number, block_count, blk_total, map_total)
    column = lax.axis_index("blk") * local_cols + jnp.arange(local_cols, dtype=jnp.int32)
    m_float = (MSTART + RES * (column % MGRP) + column // MGRP).astype(jnp.float32)
    first_l = LSTART + lax.axis_index("map") * block_count * LBLK
    cycle_scale = 1.0 / math.sqrt(cycles)
    harmonics = project_blocks(
        legendre_starts, m_float, first_l, prepared, maps_count, cycle_scale
    )
    spectra = total_cross(harmonics, maps_count, blk_total)
    spectra = spectra.reshape(1, maps_count, maps_count, spectra.shape[1])
    return (jnp.transpose(harmonics, (1, 0, 2)), spectra)


def body(sky_maps, cycle_number, legendre_starts):
    own_cycles, maps_count, cycle_len = sky_maps.shape
    map_total = lax.axis_size("map")
    blk_total = lax.axis_size("blk")
    cycles, block_count = cycle_number.shape[0], legendre_starts.shape[2]
    if kernel_fits(own_cycles, blk_total, cycles, maps_count, block_count):
        return fast_body(sky_maps, cycle_number, legendre_starts)
    tables = dft_tables(cycle_len)
    first_row = (lax.axis_index("blk") * map_total + lax.axis_index("map")) * own_cycles
    own_numbers = lax.dynamic_slice_in_dim(cycle_number, first_row, own_cycles)
    parity = (own_numbers - NSIDE + 1) % 2
    local_modes = cycle_transform(sky_maps, parity, tables)
    grouped = lax.all_gather(local_modes, "map", axis=0, tiled=True)
    regrouped = lax.all_to_all(grouped, "blk", split_axis=4, concat_axis=0, tiled=True)
    ordered = jnp.transpose(regrouped, (4, 3, 1, 2, 0))
    local_cols = ordered.shape[0] * ordered.shape[1]
    cycle_modes = ordered.reshape(local_cols, 2 * maps_count, -1)
    heights = cycle_height(cycle_number)
    column = lax.axis_index("blk") * local_cols + jnp.arange(local_cols, dtype=jnp.int32)
    m_float = (MSTART + RES * (column % MGRP) + column // MGRP).astype(jnp.float32)
    block_count = legendre_starts.shape[2]
    local_len = block_count * LBLK
    first_l = LSTART + lax.axis_index("map") * local_len
    cycle_scale = 1.0 / math.sqrt(cycle_modes.shape[-1])

    def one_block(block_index):
        start_pair = lax.dynamic_index_in_dim(legendre_starts, block_index, 2, keepdims=False)
        legendre_tile = legendre_rows(
            start_pair, heights, m_float, first_l + block_index * LBLK
        ).astype(jnp.bfloat16)
        projected = (
            jnp.einsum(
                "qlr,qnr->qnl", legendre_tile, cycle_modes, preferred_element_type=jnp.float32
            )
            * cycle_scale
        )
        return projected.astype(jnp.bfloat16)

    blocks_out = lax.map(one_block, jnp.arange(block_count, dtype=jnp.int32))
    harmonics = jnp.transpose(blocks_out, (1, 2, 0, 3)).reshape(
        local_cols, 2 * maps_count, local_len
    )
    total_cols = MGRP * RES
    spread = harmonics.reshape(local_cols, 2 * maps_count, blk_total, local_len // blk_total)
    spread = jnp.transpose(spread, (2, 3, 1, 0))
    received = lax.all_to_all(
        shortened(spread), "blk", split_axis=0, concat_axis=3, tiled=True
    ).astype(spread.dtype)
    item_count = received.shape[1]
    split_piece = received.reshape(item_count, 2, maps_count, received.shape[3])
    cross_sum = jnp.einsum(
        "gciq,gcjq->ijg", split_piece, split_piece, preferred_element_type=jnp.float32
    )
    owned = (cross_sum / total_cols)[None]
    return (harmonics, owned)


def solution(mesh):
    return jax.shard_map(
        body,
        mesh=mesh,
        in_specs=(P(("blk", "map"), None, None), P(), P(None, "blk", "map", None)),
        out_specs=(P("blk", None, "map"), P("map", None, None, "blk")),
        check_vma=False,
    )
```

```python
import functools
import math

import jax
import jax.numpy as jnp
import numpy as np
from jax import lax
from jax.experimental import pallas as pl
from jax.experimental.pallas import tpu as pltpu
from jax.sharding import PartitionSpec as P

NSIDE = 8192
RES = 128
MGRP = 4
MSTART = 4096
LSTART = 8192
LBLK = 128


def shortened(array):

    def short(part):
        return part.astype(jnp.bfloat16) if part.dtype == jnp.float32 else part

    return jax.tree.map(short, array)


def cycle_height(cycle_ids):
    return (4.0 * NSIDE - 2.0 * cycle_ids.astype(jnp.float32)) / (3.0 * NSIDE)


def dft_tables(cycle_len):
    low_len = cycle_len // RES
    residue = jnp.arange(RES, dtype=jnp.int32)
    turn_one = residue[:, None] * residue[None, :] % RES
    angle_one = 2.0 * math.pi / RES * turn_one.astype(jnp.float32)
    first_table = jnp.concatenate([jnp.cos(angle_one), -jnp.sin(angle_one)], axis=1).astype(
        jnp.bfloat16
    )
    column_group = jnp.arange(MGRP, dtype=jnp.int32)
    sample = jnp.arange(low_len, dtype=jnp.int32)
    m_value = MSTART + RES * column_group[:, None, None] + residue[None, None, :]
    turn_two = m_value * sample[None, :, None] % cycle_len
    angle_two = 2.0 * math.pi / cycle_len * turn_two.astype(jnp.float32)
    twiddle_re = jnp.cos(angle_two).astype(jnp.bfloat16)
    twiddle_im = (-jnp.sin(angle_two)).astype(jnp.bfloat16)
    return (first_table, twiddle_re, twiddle_im)


def cycle_transform(cycle_rows, parity, tables):
    first_table, twiddle_re, twiddle_im = tables
    cycle_count, maps_count, cycle_len = cycle_rows.shape
    low_len = cycle_len // RES
    folded = cycle_rows.reshape(cycle_count, maps_count, RES, low_len)
    section_one = jnp.einsum(
        "rnaj,ak->rnjk", folded, first_table, preferred_element_type=jnp.float32
    )
    section_one = section_one.astype(jnp.bfloat16)
    part_re = section_one[..., :RES]
    part_im = section_one[..., RES:]
    real_sum = jnp.einsum(
        "rnjk,cjk->rnck", part_re, twiddle_re, preferred_element_type=jnp.float32
    ) - jnp.einsum("rnjk,cjk->rnck", part_im, twiddle_im, preferred_element_type=jnp.float32)
    imag_sum = jnp.einsum(
        "rnjk,cjk->rnck", part_im, twiddle_re, preferred_element_type=jnp.float32
    ) + jnp.einsum("rnjk,cjk->rnck", part_re, twiddle_im, preferred_element_type=jnp.float32)
    column_group = jnp.arange(MGRP, dtype=jnp.int32)
    residue = jnp.arange(RES, dtype=jnp.int32)
    m_value = MSTART + RES * column_group[:, None] + residue[None, :]
    shifted = m_value[None, :, :] * parity[:, None, None] % (2 * cycle_len)
    phase_angle = math.pi / cycle_len * shifted.astype(jnp.float32)
    cos_part = jnp.cos(phase_angle)[:, None]
    sin_part = jnp.sin(phase_angle)[:, None]
    factor = 1.0 / math.sqrt(cycle_len)
    out_re = factor * (cos_part * real_sum + sin_part * imag_sum)
    out_im = factor * (cos_part * imag_sum - sin_part * real_sum)
    return jnp.stack([out_re, out_im], axis=1).astype(jnp.bfloat16)


def legendre_rows(start_pair, height, m_float, first_l):
    m_column = m_float[:, None]

    def recur_coef(degree):
        return jnp.sqrt((4.0 * degree * degree - 1.0) / ((degree - m_column) * (degree + m_column)))

    base_l = first_l.astype(jnp.float32)
    value_older = start_pair[0]
    value_newer = start_pair[1]
    prior_coef = recur_coef(base_l - 1.0)
    height_row = height[None, :]
    stacked_rows = []
    for offset in range(LBLK):
        present_coef = recur_coef(base_l + offset)
        value_now = present_coef * (height_row * value_newer - value_older / prior_coef)
        stacked_rows.append(value_now)
        value_older = value_newer
        value_newer = value_now
        prior_coef = present_coef
    return jnp.stack(stacked_rows, axis=1)


STEP_LANES = 1024
KDIM = 256
GAP = 8
RUN = 64
PACK = 16
START_GAP = 8


def sky_modes(totals, number_ref, sky_ref, first_ref, wave_ref, phase_ref, lhs_ref, rows_ref, me):
    maps, factor = totals
    low_len = wave_ref.shape[1]
    for a in range(RES):
        lhs_ref[a * PACK : a * PACK + maps, :] = sky_ref[0, :, a * low_len : (a + 1) * low_len]
    rows_ref[...] = jnp.zeros_like(rows_ref)
    parity = (number_ref[me] - NSIDE + 1) % 2
    odd = jnp.full((MGRP, RES), parity, jnp.int32) == 1
    cosines = jnp.where(odd, phase_ref[:MGRP], 1.0)
    sines = jnp.where(odd, phase_ref[MGRP:], 0.0)
    for c in range(MGRP):
        out = jnp.dot(lhs_ref[...], wave_ref[c], preferred_element_type=jnp.float32)
        real = jnp.zeros((PACK, RES), jnp.float32)
        imag = real
        for a in range(RES):
            e_re, e_im = first_ref[a : a + 1, :RES], first_ref[a : a + 1, RES:]
            w_re = out[a * PACK : (a + 1) * PACK, :RES]
            w_im = out[a * PACK : (a + 1) * PACK, RES:]
            real = real + (e_re * w_re - e_im * w_im)
            imag = imag + (e_re * w_im + e_im * w_re)
        cos, sin = cosines[c : c + 1], sines[c : c + 1]
        row = c * 2 * maps
        rows_ref[row : row + maps, :] = (factor * (cos * real + sin * imag))[:maps]
        rows_ref[row + maps : row + 2 * maps, :] = (factor * (cos * imag - sin * real))[:maps]


def prepare(blk_total, scale, number_ref, pieces_ref, scales_ref, z_ref, p_ref):
    blocks = scales_ref.shape[0]
    local_cols = MGRP * RES // blk_total
    lane = lax.broadcasted_iota(jnp.int32, z_ref.shape, 1) % number_ref.shape[0]
    numbers = jnp.zeros(z_ref.shape, jnp.int32)
    for r in range(number_ref.shape[0]):
        numbers = jnp.where(lane == r, number_ref[r], numbers)
    z_ref[...] = cycle_height(numbers)
    lane = lax.broadcasted_iota(jnp.int32, (blocks, 256), 1)
    piece = lane // local_cols
    column = lax.axis_index("blk") * local_cols + lane % local_cols
    m_row = (MSTART + RES * (column % MGRP) + column // MGRP).astype(jnp.float32)
    block = lax.broadcasted_iota(jnp.int32, (blocks, 256), 0)
    base = LSTART + (lax.axis_index("map") * blocks + block) * LBLK

    def setup(j, carry):
        p_prev, q_prev = carry
        degree = (base + j).astype(jnp.float32)
        num = 4.0 * degree * degree - 1.0
        den = (degree - m_row) * (degree + m_row)
        root = lax.rsqrt(num * den)
        kappa = p_prev * p_prev
        high = kappa.astype(jnp.bfloat16).astype(jnp.float32)
        rest = kappa - high
        mid = rest.astype(jnp.bfloat16).astype(jnp.float32)
        low = rest - mid
        pieces = jnp.where(piece == 0, high, jnp.where(piece == 1, mid, low))
        pieces_ref[pl.ds(pl.multiple_of(j * blocks, blocks), blocks), :] = pieces.astype(
            jnp.bfloat16
        )
        p_now = num * root * q_prev
        q_now = den * root * p_prev
        for half in range(blocks // 8):
            p_ref[pl.ds(half * 8 * (LBLK + GAP) + j, 8, stride=LBLK + GAP), :] = p_now[
                half * 8 : half * 8 + 8, :128
            ]
        return p_now, q_now

    one = jnp.ones((blocks, 256), jnp.float32)
    lax.fori_loop(0, LBLK, setup, (one, one), unroll=4)

    def turn(t, _):
        turned = p_ref[pl.ds(pl.multiple_of(t * (LBLK + GAP), 8), LBLK), :].T
        scales_ref[t] = turned[:local_cols] * scale
        return 0

    lax.fori_loop(0, blocks, turn, 0)


def start_values(starts_ref, turn_ref, init_ref):
    _, blocks, cycles, local_cols = starts_ref.shape
    lane = lax.broadcasted_iota(jnp.int32, (blocks, local_cols), 1)
    column = lax.axis_index("blk") * local_cols + lane
    m_row = (MSTART + RES * (column % MGRP) + column // MGRP).astype(jnp.float32)
    block = lax.broadcasted_iota(jnp.int32, (blocks, local_cols), 0)
    degree = (LSTART + (lax.axis_index("map") * blocks + block) * LBLK - 1).astype(jnp.float32)
    inverse = jnp.sqrt(((degree - m_row) * (degree + m_row)) / (4.0 * degree * degree - 1.0))
    pitch = local_cols + START_GAP
    for kind in range(2):
        for t in range(blocks):
            values = starts_ref[kind, t]
            if kind == 0:
                values = values * inverse[t : t + 1]
            turn_ref[kind, t * pitch : t * pitch + local_cols, :cycles] = values.T
    per_tile = 128 // cycles
    slot = lax.broadcasted_iota(jnp.int32, (8, 128), 1) // cycles
    for kind in range(2):
        for half in range(blocks // 8):
            for tile in range(local_cols // per_tile):
                row = None
                for i in range(per_tile):
                    first = half * 8 * pitch + tile * per_tile + i
                    part = turn_ref[kind, pl.ds(first, 8, stride=pitch), :]
                    if i == 0:
                        row = part
                    else:
                        row = jnp.where(slot == i, pltpu.roll(part, i * cycles, 1), row)
                init_ref[kind, half * 8 : half * 8 + 8, tile * 128 : tile * 128 + 128] = row


def recurrence(part, cycles, z_ref, pieces_ref, init_ref, leg_ref):
    blocks = init_ref.shape[1]
    halves = STEP_LANES // 128
    q_row = lax.broadcasted_iota(jnp.int32, (256, STEP_LANES), 0)
    q_lane = lax.broadcasted_iota(jnp.int32, (256, STEP_LANES), 1) // cycles + part * (
        STEP_LANES // cycles
    )
    spread = jnp.where((q_row % 64 == q_lane) & (q_row < 192), 1.0, 0.0).astype(jnp.bfloat16)

    def recur(i, carry):
        older, newer = carry
        rows = pl.ds(pl.multiple_of(i * RUN * blocks, RUN * blocks), RUN * blocks)
        kap = jnp.dot(pieces_ref[rows, :], spread, preferred_element_type=jnp.float32)
        for j in range(RUN):
            now = (kap[j * blocks : (j + 1) * blocks] * z_ref[...]) * newer - older
            for half in range(blocks // 8):
                at = pl.ds(half * 8 * (LBLK + GAP) + i * RUN + j, 8, stride=LBLK + GAP)
                for g in range(halves):
                    leg_ref[part * halves + g, at, :] = now[
                        half * 8 : half * 8 + 8, g * 128 : g * 128 + 128
                    ]
            older, newer = newer, now
        return older, newer

    lanes = slice(part * STEP_LANES, (part + 1) * STEP_LANES)
    lax.fori_loop(0, LBLK // RUN, recur, (init_ref[0, :, lanes], init_ref[1, :, lanes]))


def block_weights(maps, held_ref, weight_ref):
    groups, rows_all, _ = weight_ref.shape
    cycles, _, _ = held_ref.shape
    parts = 2 * maps
    q_group = rows_all // parts
    per_group = q_group // MGRP
    row = lax.broadcasted_iota(jnp.int32, (rows_all, per_group * 128), 0)
    lane = lax.broadcasted_iota(jnp.int32, (rows_all, per_group * 128), 1)
    q = row % q_group
    wanted = q // MGRP * 128 + (q % MGRP) * parts + row // q_group
    pick = jnp.where(lane == wanted, 1.0, 0.0).astype(jnp.bfloat16)
    row = lax.broadcasted_iota(jnp.int32, (rows_all, KDIM), 0)
    lane = lax.broadcasted_iota(jnp.int32, (rows_all, KDIM), 1)
    same_q = row % q_group == lane // cycles
    modes = jnp.swapaxes(held_ref[...].astype(jnp.float32), 0, 1).astype(jnp.bfloat16)
    for g in range(groups):
        own = jnp.concatenate([modes[g * per_group + k] for k in range(per_group)], axis=1)
        wide = lax.dot_general(
            pick, jnp.concatenate([own] * q_group, axis=0), (((1,), (1,)), ((), ())),
            preferred_element_type=jnp.float32,
        )
        weight_ref[g] = jnp.where(same_q, wide, 0.0).astype(jnp.bfloat16)


def project_share(u, maps, share, leg_ref, scales_ref, weight_ref, harm_ref):
    groups, rows_all, _ = weight_ref.shape
    parts = 2 * maps
    q_group = rows_all // parts
    width = 2 * LBLK
    for piece in range(share // width):
        first_t = u * (share // LBLK) + 2 * piece
        cols = pl.ds(pl.multiple_of(u * share + piece * width, width), width)
        sources = [
            pl.ds(pl.multiple_of((first_t + x) * (LBLK + GAP), 8), LBLK) for x in range(2)
        ]
        for g in range(groups):
            p_rows = jnp.concatenate(
                [scales_ref[first_t + x, g * q_group : (g + 1) * q_group, :] for x in range(2)],
                axis=1,
            )
            leg = jnp.concatenate(
                [
                    jnp.concatenate(
                        [leg_ref[g * (KDIM // 128) + h, src, :] for h in range(KDIM // 128)],
                        axis=1,
                    )
                    for src in sources
                ],
                axis=0,
            ).astype(jnp.bfloat16)
            out = lax.dot_general(
                weight_ref[g], leg, (((1,), (1,)), ((), ())), preferred_element_type=jnp.float32
            )
            crossed = out.reshape(parts, q_group, width) * p_rows[None]
            harm_ref[:, g * q_group : (g + 1) * q_group, cols] = crossed.astype(jnp.bfloat16)


def cross_share(u, maps, share, gather, harm_ref, sums_ref, part_ref):
    local_cols = harm_ref.shape[1]
    pairs = [(i, k) for i in range(maps) for k in range(i, maps)]

    def one(half, _):
        cols = pl.ds(pl.multiple_of(half * 128, 128), 128)
        lanes = pl.ds(pl.multiple_of(u * share + half * 128, 128), 128)
        middle = (len(pairs) + 1) // 2
        for first, last in ((0, middle), (middle, len(pairs))):
            total = [None] * (last - first)
            for h in range(2):
                for t in range(local_cols // PACK):
                    x = {}
                    for n in sorted({v for pair in pairs[first:last] for v in pair}):
                        x[n] = harm_ref[h * maps + n, t * PACK : (t + 1) * PACK, lanes]
                    for p in range(first, last):
                        i, k = pairs[p]
                        term = x[i] * x[k]
                        had = total[p - first]
                        total[p - first] = term if had is None else had + term
            for p in range(first, last):
                sums_ref[p * PACK : (p + 1) * PACK, cols] = total[p - first]
        return 0

    lax.fori_loop(0, share // 128, one, 0)
    part_ref[u] = jnp.dot(gather, sums_ref[...], preferred_element_type=jnp.float32).astype(
        jnp.bfloat16
    )


def whole_kernel(
    dims, number_ref, sky_ref, starts_ref, first_ref, wave_ref, phase_ref,
    harm_ref, out_ref,
    lhs_ref, rows_ref, turned_ref, held_ref, pieces_ref, scales_ref, z_ref, p_ref,
    turn_ref, init_ref, leg_ref, weight_ref, sums_ref, part_ref, other_ref,
    send_sem, recv_sem, part_send, part_recv,
):
    blk_total, map_total, maps, factor, scale = dims
    count = blk_total * map_total
    cycles = number_ref.shape[0]
    share = out_ref.shape[1]
    me_blk, me_map = lax.axis_index("blk"), lax.axis_index("map")
    me = me_blk * map_total + me_map
    k_share = RES // blk_total
    barrier = pltpu.get_barrier_semaphore()
    for i in range(1, count):
        peer = lax.rem(me + i, count)
        pl.semaphore_signal(
            barrier, inc=1,
            device_id={"blk": peer // map_total, "map": lax.rem(peer, map_total)},
            device_id_type=pl.DeviceIdType.MESH,
        )
    sky_modes(
        (maps, factor), number_ref, sky_ref, first_ref, wave_ref, phase_ref, lhs_ref, rows_ref, me
    )
    turned_ref[...] = rows_ref[...].T.astype(jnp.bfloat16)
    pl.semaphore_wait(barrier, count - 1)

    def modes_to(peer, source):
        target_blk = peer // map_total
        return pltpu.make_async_remote_copy(
            src_ref=turned_ref.at[pl.ds(pl.multiple_of(target_blk * k_share, k_share), k_share)],
            dst_ref=held_ref.at[source],
            send_sem=send_sem.at[peer],
            recv_sem=recv_sem.at[source],
            device_id={"blk": target_blk, "map": lax.rem(peer, map_total)},
            device_id_type=pl.DeviceIdType.MESH,
        )

    for i in range(1, count):
        modes_to(lax.rem(me + i, count), me).start()
    held_ref[me] = turned_ref[pl.ds(pl.multiple_of(me_blk * k_share, k_share), k_share), :]

    prepare(blk_total, scale, number_ref, pieces_ref, scales_ref, z_ref, p_ref)
    start_values(starts_ref, turn_ref, init_ref)
    for part in range(init_ref.shape[2] // STEP_LANES):
        recurrence(part, cycles, z_ref, pieces_ref, init_ref, leg_ref)

    for i in range(1, count):
        peer = lax.rem(me + i, count)
        modes_to(peer, peer).wait_recv()
    block_weights(maps, held_ref, weight_ref)

    pairs = maps * (maps + 1) // 2
    pair_rows = part_ref.shape[1]
    row = lax.broadcasted_iota(jnp.int32, (pair_rows, pair_rows * PACK), 0)
    lane = lax.broadcasted_iota(jnp.int32, (pair_rows, pair_rows * PACK), 1)
    gather = jnp.where(lane // PACK == row, 1.0, 0.0).astype(jnp.bfloat16)
    for p in range(pairs, pair_rows):
        sums_ref[p * PACK : (p + 1) * PACK, :] = jnp.zeros((PACK, share), jnp.bfloat16)

    def part_to(peer, source):
        return pltpu.make_async_remote_copy(
            src_ref=part_ref.at[peer],
            dst_ref=other_ref.at[source],
            send_sem=part_send.at[peer],
            recv_sem=part_recv.at[source],
            device_id={"blk": peer},
            device_id_type=pl.DeviceIdType.MESH,
        )

    def one_share(s, _):
        u = lax.rem(me_blk + s, blk_total)
        project_share(u, maps, share, leg_ref, scales_ref, weight_ref, harm_ref)
        cross_share(u, maps, share, gather, harm_ref, sums_ref, part_ref)

        @pl.when(s < blk_total)
        def _():
            part_to(u, me_blk).start()

        return 0

    lax.fori_loop(1, blk_total + 1, one_share, 0)
    out_rows = maps * maps
    row = lax.broadcasted_iota(jnp.int32, (out_rows, pair_rows), 0)
    lane = lax.broadcasted_iota(jnp.int32, (out_rows, pair_rows), 1)
    low = jnp.minimum(row // maps, row % maps)
    high = jnp.maximum(row // maps, row % maps)
    pair_at = low * maps - low * (low - 1) // 2 + high - low
    unfold = jnp.where(lane == pair_at, 1.0, 0.0).astype(jnp.bfloat16)
    unfolded = lambda x: jnp.dot(unfold, x, preferred_element_type=jnp.float32)
    total = unfolded(part_ref[me_blk])
    for i in range(1, blk_total):
        peer = lax.rem(me_blk + blk_total - i, blk_total)
        part_to(peer, peer).wait_recv()
        total = total + unfolded(other_ref[peer])
    out_ref[...] = total * (1.0 / (MGRP * RES))
    for i in range(1, count):
        modes_to(lax.rem(me + i, count), me).wait_send()
    for i in range(1, blk_total):
        part_to(lax.rem(me_blk + i, blk_total), me_blk).wait_send()


def constant_tables(cycle_len):
    low_len = cycle_len // RES
    residue = np.arange(RES)
    angle = np.float32(2.0 * math.pi / RES) * (
        residue[:, None] * residue[None, :] % RES
    ).astype(np.float32)
    first = np.concatenate([np.cos(angle), -np.sin(angle)], axis=1)
    first = first.astype(jnp.bfloat16).astype(np.float32)
    m_value = MSTART + RES * np.arange(MGRP)[:, None, None] + residue[None, None, :]
    turn = m_value * np.arange(low_len)[None, :, None] % cycle_len
    angle = np.float32(2.0 * math.pi / cycle_len) * turn.astype(np.float32)
    wave = np.concatenate([np.cos(angle), -np.sin(angle)], axis=2).astype(jnp.bfloat16)
    m_value = MSTART + np.arange(MGRP)[:, None] * RES + np.arange(RES)[None, :]
    angle = np.float32(math.pi / cycle_len) * (m_value % (2 * cycle_len)).astype(np.float32)
    phase = np.concatenate([np.cos(angle), np.sin(angle)], axis=0)
    return jnp.asarray(first), jnp.asarray(wave), jnp.asarray(phase)


def kernel_fits(own_cycles, blk_total, cycles, maps_count, block_count):
    local_cols = MGRP * RES // blk_total
    return (
        own_cycles == 1
        and local_cols == 64
        and KDIM % cycles == 0
        and KDIM // cycles == 8
        and 2 * maps_count * MGRP <= 128
        and block_count % 8 == 0
        and block_count % blk_total == 0
        and (block_count * LBLK // blk_total) % (2 * LBLK) == 0
    )


def fast_body(sky_maps, cycle_number, legendre_starts):
    _, maps, cycle_len = sky_maps.shape
    map_total = lax.axis_size("map")
    blk_total = lax.axis_size("blk")
    local_cols, blocks, cycles = legendre_starts.shape[1:]
    count = blk_total * map_total
    local_len = blocks * LBLK
    share = local_len // blk_total
    parts = 2 * maps
    q_group = KDIM // cycles
    lanes = local_cols * cycles
    pair_rows = -(-(maps * (maps + 1) // 2) // 8) * 8
    tables = constant_tables(cycle_len)
    starts = jnp.transpose(legendre_starts, (0, 2, 3, 1))
    dims = (blk_total, map_total, maps, 1.0 / math.sqrt(cycle_len), 1.0 / math.sqrt(cycles))
    vmem = pl.BlockSpec(memory_space=pltpu.VMEM)
    pitch = LBLK + GAP
    harmonics, spectra = pl.pallas_call(
        functools.partial(whole_kernel, dims),
        out_shape=(
            jax.ShapeDtypeStruct((parts, local_cols, local_len), jnp.bfloat16),
            jax.ShapeDtypeStruct((maps * maps, share), jnp.float32),
        ),
        in_specs=[pl.BlockSpec(memory_space=pltpu.SMEM)] + [vmem] * 5,
        out_specs=(vmem, vmem),
        scratch_shapes=[
            pltpu.VMEM((RES * PACK, cycle_len // RES), jnp.bfloat16),
            pltpu.VMEM((128, RES), jnp.float32),
            pltpu.VMEM((RES, 128), jnp.bfloat16),
            pltpu.VMEM((count, RES // blk_total, 128), jnp.bfloat16),
            pltpu.VMEM((local_len, 256), jnp.bfloat16),
            pltpu.VMEM((blocks, local_cols, LBLK), jnp.float32),
            pltpu.VMEM((1, STEP_LANES), jnp.float32),
            pltpu.VMEM((blocks * pitch, 128), jnp.float32),
            pltpu.VMEM((2, blocks * (local_cols + START_GAP), 128), jnp.float32),
            pltpu.VMEM((2, blocks, lanes), jnp.float32),
            pltpu.VMEM((lanes // 128, blocks * pitch, 128), jnp.float32),
            pltpu.VMEM((local_cols // q_group, parts * q_group, KDIM), jnp.bfloat16),
            pltpu.VMEM((pair_rows * PACK, share), jnp.bfloat16),
            pltpu.VMEM((blk_total, pair_rows, share), jnp.bfloat16),
            pltpu.VMEM((blk_total, pair_rows, share), jnp.bfloat16),
            pltpu.SemaphoreType.DMA((count,)),
            pltpu.SemaphoreType.DMA((count,)),
            pltpu.SemaphoreType.DMA((blk_total,)),
            pltpu.SemaphoreType.DMA((blk_total,)),
        ],
        compiler_params=pltpu.CompilerParams(
            collective_id=0, has_side_effects=True, vmem_limit_bytes=40 * 1024 * 1024
        ),
    )(cycle_number, sky_maps, starts, *tables)
    spectra = spectra.reshape(1, maps, maps, share)
    return (jnp.transpose(harmonics, (1, 0, 2)), spectra)


def body(sky_maps, cycle_number, legendre_starts):
    own_cycles, maps_count, cycle_len = sky_maps.shape
    map_total = lax.axis_size("map")
    blk_total = lax.axis_size("blk")
    cycles, block_count = cycle_number.shape[0], legendre_starts.shape[2]
    if kernel_fits(own_cycles, blk_total, cycles, maps_count, block_count):
        return fast_body(sky_maps, cycle_number, legendre_starts)
    tables = dft_tables(cycle_len)
    first_row = (lax.axis_index("blk") * map_total + lax.axis_index("map")) * own_cycles
    own_numbers = lax.dynamic_slice_in_dim(cycle_number, first_row, own_cycles)
    parity = (own_numbers - NSIDE + 1) % 2
    local_modes = cycle_transform(sky_maps, parity, tables)
    grouped = lax.all_gather(local_modes, "map", axis=0, tiled=True)
    regrouped = lax.all_to_all(grouped, "blk", split_axis=4, concat_axis=0, tiled=True)
    ordered = jnp.transpose(regrouped, (4, 3, 1, 2, 0))
    local_cols = ordered.shape[0] * ordered.shape[1]
    cycle_modes = ordered.reshape(local_cols, 2 * maps_count, -1)
    heights = cycle_height(cycle_number)
    column = lax.axis_index("blk") * local_cols + jnp.arange(local_cols, dtype=jnp.int32)
    m_float = (MSTART + RES * (column % MGRP) + column // MGRP).astype(jnp.float32)
    block_count = legendre_starts.shape[2]
    local_len = block_count * LBLK
    first_l = LSTART + lax.axis_index("map") * local_len
    cycle_scale = 1.0 / math.sqrt(cycle_modes.shape[-1])

    def one_block(block_index):
        start_pair = lax.dynamic_index_in_dim(legendre_starts, block_index, 2, keepdims=False)
        legendre_tile = legendre_rows(
            start_pair, heights, m_float, first_l + block_index * LBLK
        ).astype(jnp.bfloat16)
        projected = (
            jnp.einsum(
                "qlr,qnr->qnl", legendre_tile, cycle_modes, preferred_element_type=jnp.float32
            )
            * cycle_scale
        )
        return projected.astype(jnp.bfloat16)

    blocks_out = lax.map(one_block, jnp.arange(block_count, dtype=jnp.int32))
    harmonics = jnp.transpose(blocks_out, (1, 2, 0, 3)).reshape(
        local_cols, 2 * maps_count, local_len
    )
    total_cols = MGRP * RES
    spread = harmonics.reshape(local_cols, 2 * maps_count, blk_total, local_len // blk_total)
    spread = jnp.transpose(spread, (2, 3, 1, 0))
    received = lax.all_to_all(
        shortened(spread), "blk", split_axis=0, concat_axis=3, tiled=True
    ).astype(spread.dtype)
    item_count = received.shape[1]
    split_piece = received.reshape(item_count, 2, maps_count, received.shape[3])
    cross_sum = jnp.einsum(
        "gciq,gcjq->ijg", split_piece, split_piece, preferred_element_type=jnp.float32
    )
    owned = (cross_sum / total_cols)[None]
    return (harmonics, owned)


def solution(mesh):
    return jax.shard_map(
        body,
        mesh=mesh,
        in_specs=(P(("blk", "map"), None, None), P(), P(None, "blk", "map", None)),
        out_specs=(P("blk", None, "map"), P("map", None, None, "blk")),
        check_vma=False,
    )
```

```python
import functools
import math

import jax
import jax.numpy as jnp
import numpy as np
from jax import lax
from jax.experimental import pallas as pl
from jax.experimental.pallas import tpu as pltpu
from jax.sharding import PartitionSpec as P

NSIDE = 8192
RES = 128
MGRP = 4
MSTART = 4096
LSTART = 8192
LBLK = 128


def shortened(array):

    def short(part):
        return part.astype(jnp.bfloat16) if part.dtype == jnp.float32 else part

    return jax.tree.map(short, array)


def cycle_height(cycle_ids):
    return (4.0 * NSIDE - 2.0 * cycle_ids.astype(jnp.float32)) / (3.0 * NSIDE)


def dft_tables(cycle_len):
    low_len = cycle_len // RES
    residue = jnp.arange(RES, dtype=jnp.int32)
    turn_one = residue[:, None] * residue[None, :] % RES
    angle_one = 2.0 * math.pi / RES * turn_one.astype(jnp.float32)
    first_table = jnp.concatenate([jnp.cos(angle_one), -jnp.sin(angle_one)], axis=1).astype(
        jnp.bfloat16
    )
    column_group = jnp.arange(MGRP, dtype=jnp.int32)
    sample = jnp.arange(low_len, dtype=jnp.int32)
    m_value = MSTART + RES * column_group[:, None, None] + residue[None, None, :]
    turn_two = m_value * sample[None, :, None] % cycle_len
    angle_two = 2.0 * math.pi / cycle_len * turn_two.astype(jnp.float32)
    twiddle_re = jnp.cos(angle_two).astype(jnp.bfloat16)
    twiddle_im = (-jnp.sin(angle_two)).astype(jnp.bfloat16)
    return (first_table, twiddle_re, twiddle_im)


def cycle_transform(cycle_rows, parity, tables):
    first_table, twiddle_re, twiddle_im = tables
    cycle_count, maps_count, cycle_len = cycle_rows.shape
    low_len = cycle_len // RES
    folded = cycle_rows.reshape(cycle_count, maps_count, RES, low_len)
    section_one = jnp.einsum(
        "rnaj,ak->rnjk", folded, first_table, preferred_element_type=jnp.float32
    )
    section_one = section_one.astype(jnp.bfloat16)
    part_re = section_one[..., :RES]
    part_im = section_one[..., RES:]
    real_sum = jnp.einsum(
        "rnjk,cjk->rnck", part_re, twiddle_re, preferred_element_type=jnp.float32
    ) - jnp.einsum("rnjk,cjk->rnck", part_im, twiddle_im, preferred_element_type=jnp.float32)
    imag_sum = jnp.einsum(
        "rnjk,cjk->rnck", part_im, twiddle_re, preferred_element_type=jnp.float32
    ) + jnp.einsum("rnjk,cjk->rnck", part_re, twiddle_im, preferred_element_type=jnp.float32)
    column_group = jnp.arange(MGRP, dtype=jnp.int32)
    residue = jnp.arange(RES, dtype=jnp.int32)
    m_value = MSTART + RES * column_group[:, None] + residue[None, :]
    shifted = m_value[None, :, :] * parity[:, None, None] % (2 * cycle_len)
    phase_angle = math.pi / cycle_len * shifted.astype(jnp.float32)
    cos_part = jnp.cos(phase_angle)[:, None]
    sin_part = jnp.sin(phase_angle)[:, None]
    factor = 1.0 / math.sqrt(cycle_len)
    out_re = factor * (cos_part * real_sum + sin_part * imag_sum)
    out_im = factor * (cos_part * imag_sum - sin_part * real_sum)
    return jnp.stack([out_re, out_im], axis=1).astype(jnp.bfloat16)


def legendre_rows(start_pair, height, m_float, first_l):
    m_column = m_float[:, None]

    def recur_coef(degree):
        return jnp.sqrt((4.0 * degree * degree - 1.0) / ((degree - m_column) * (degree + m_column)))

    base_l = first_l.astype(jnp.float32)
    value_older = start_pair[0]
    value_newer = start_pair[1]
    prior_coef = recur_coef(base_l - 1.0)
    height_row = height[None, :]
    stacked_rows = []
    for offset in range(LBLK):
        present_coef = recur_coef(base_l + offset)
        value_now = present_coef * (height_row * value_newer - value_older / prior_coef)
        stacked_rows.append(value_now)
        value_older = value_newer
        value_newer = value_now
        prior_coef = present_coef
    return jnp.stack(stacked_rows, axis=1)


STEP_LANES = 1024
KDIM = 256
GAP = 8
RUN = 64
PACK = 16
START_GAP = 8
PAIR_GROUPS = 2


def sky_modes(totals, number_ref, sky_ref, first_ref, wave_ref, phase_ref, lhs_ref, rows_ref, me):
    maps, factor = totals
    low_len = wave_ref.shape[1]
    for a in range(RES):
        lhs_ref[a * PACK : a * PACK + maps, :] = sky_ref[0, :, a * low_len : (a + 1) * low_len]
    rows_ref[...] = jnp.zeros_like(rows_ref)
    parity = (number_ref[me] - NSIDE + 1) % 2
    odd = jnp.full((MGRP, RES), parity, jnp.int32) == 1
    cosines = jnp.where(odd, phase_ref[:MGRP], 1.0)
    sines = jnp.where(odd, phase_ref[MGRP:], 0.0)
    for c in range(MGRP):
        out = jnp.dot(lhs_ref[...], wave_ref[c], preferred_element_type=jnp.float32)
        real = jnp.zeros((PACK, RES), jnp.float32)
        imag = real
        for a in range(RES):
            e_re, e_im = first_ref[a : a + 1, :RES], first_ref[a : a + 1, RES:]
            w_re = out[a * PACK : (a + 1) * PACK, :RES]
            w_im = out[a * PACK : (a + 1) * PACK, RES:]
            real = real + (e_re * w_re - e_im * w_im)
            imag = imag + (e_re * w_im + e_im * w_re)
        cos, sin = cosines[c : c + 1], sines[c : c + 1]
        row = c * 2 * maps
        rows_ref[row : row + maps, :] = (factor * (cos * real + sin * imag))[:maps]
        rows_ref[row + maps : row + 2 * maps, :] = (factor * (cos * imag - sin * real))[:maps]


def prepare(blk_total, scale, number_ref, pieces_ref, scales_ref, z_ref, p_ref):
    blocks = scales_ref.shape[0]
    local_cols = MGRP * RES // blk_total
    lane = lax.broadcasted_iota(jnp.int32, z_ref.shape, 1) % number_ref.shape[0]
    numbers = jnp.zeros(z_ref.shape, jnp.int32)
    for r in range(number_ref.shape[0]):
        numbers = jnp.where(lane == r, number_ref[r], numbers)
    z_ref[...] = cycle_height(numbers)
    lane = lax.broadcasted_iota(jnp.int32, (blocks, 256), 1)
    piece = lane // local_cols
    column = lax.axis_index("blk") * local_cols + lane % local_cols
    m_row = (MSTART + RES * (column % MGRP) + column // MGRP).astype(jnp.float32)
    block = lax.broadcasted_iota(jnp.int32, (blocks, 256), 0)
    base = LSTART + (lax.axis_index("map") * blocks + block) * LBLK

    def setup(j, carry):
        p_prev, q_prev = carry
        degree = (base + j).astype(jnp.float32)
        num = 4.0 * degree * degree - 1.0
        den = (degree - m_row) * (degree + m_row)
        root = lax.rsqrt(num * den)
        kappa = p_prev * p_prev
        high = kappa.astype(jnp.bfloat16).astype(jnp.float32)
        rest = kappa - high
        mid = rest.astype(jnp.bfloat16).astype(jnp.float32)
        low = rest - mid
        pieces = jnp.where(piece == 0, high, jnp.where(piece == 1, mid, low))
        pieces_ref[pl.ds(pl.multiple_of(j * blocks, blocks), blocks), :] = pieces.astype(
            jnp.bfloat16
        )
        p_now = num * root * q_prev
        q_now = den * root * p_prev
        for half in range(blocks // 8):
            p_ref[pl.ds(half * 8 * (LBLK + GAP) + j, 8, stride=LBLK + GAP), :] = p_now[
                half * 8 : half * 8 + 8, :128
            ]
        return p_now, q_now

    one = jnp.ones((blocks, 256), jnp.float32)
    lax.fori_loop(0, LBLK, setup, (one, one), unroll=4)

    def turn(t, _):
        turned = p_ref[pl.ds(pl.multiple_of(t * (LBLK + GAP), 8), LBLK), :].T
        scales_ref[t] = turned[:local_cols] * scale
        return 0

    lax.fori_loop(0, blocks, turn, 0)


def start_values(starts_ref, turn_ref, init_ref):
    _, blocks, cycles, local_cols = starts_ref.shape
    lane = lax.broadcasted_iota(jnp.int32, (blocks, local_cols), 1)
    column = lax.axis_index("blk") * local_cols + lane
    m_row = (MSTART + RES * (column % MGRP) + column // MGRP).astype(jnp.float32)
    block = lax.broadcasted_iota(jnp.int32, (blocks, local_cols), 0)
    degree = (LSTART + (lax.axis_index("map") * blocks + block) * LBLK - 1).astype(jnp.float32)
    inverse = jnp.sqrt(((degree - m_row) * (degree + m_row)) / (4.0 * degree * degree - 1.0))
    pitch = local_cols + START_GAP
    for kind in range(2):
        for t in range(blocks):
            values = starts_ref[kind, t]
            if kind == 0:
                values = values * inverse[t : t + 1]
            turn_ref[kind, t * pitch : t * pitch + local_cols, :cycles] = values.T
    per_tile = 128 // cycles
    slot = lax.broadcasted_iota(jnp.int32, (8, 128), 1) // cycles
    for kind in range(2):
        for half in range(blocks // 8):
            for tile in range(local_cols // per_tile):
                row = None
                for i in range(per_tile):
                    first = half * 8 * pitch + tile * per_tile + i
                    part = turn_ref[kind, pl.ds(first, 8, stride=pitch), :]
                    if i == 0:
                        row = part
                    else:
                        row = jnp.where(slot == i, pltpu.roll(part, i * cycles, 1), row)
                init_ref[kind, half * 8 : half * 8 + 8, tile * 128 : tile * 128 + 128] = row


def recurrence(part, cycles, z_ref, pieces_ref, init_ref, leg_ref):
    blocks = init_ref.shape[1]
    halves = STEP_LANES // 128
    q_row = lax.broadcasted_iota(jnp.int32, (256, STEP_LANES), 0)
    q_lane = lax.broadcasted_iota(jnp.int32, (256, STEP_LANES), 1) // cycles + part * (
        STEP_LANES // cycles
    )
    spread = jnp.where((q_row % 64 == q_lane) & (q_row < 192), 1.0, 0.0).astype(jnp.bfloat16)

    def recur(i, carry):
        older, newer = carry
        rows = pl.ds(pl.multiple_of(i * RUN * blocks, RUN * blocks), RUN * blocks)
        kap = jnp.dot(pieces_ref[rows, :], spread, preferred_element_type=jnp.float32)
        for j in range(RUN):
            now = (kap[j * blocks : (j + 1) * blocks] * z_ref[...]) * newer - older
            for half in range(blocks // 8):
                at = pl.ds(half * 8 * (LBLK + GAP) + i * RUN + j, 8, stride=LBLK + GAP)
                for g in range(halves):
                    leg_ref[part * halves + g, at, :] = now[
                        half * 8 : half * 8 + 8, g * 128 : g * 128 + 128
                    ]
            older, newer = newer, now
        return older, newer

    lanes = slice(part * STEP_LANES, (part + 1) * STEP_LANES)
    lax.fori_loop(0, LBLK // RUN, recur, (init_ref[0, :, lanes], init_ref[1, :, lanes]))


def block_weights(maps, held_ref, weight_ref):
    groups, rows_all, _ = weight_ref.shape
    cycles, _, _ = held_ref.shape
    parts = 2 * maps
    q_group = rows_all // parts
    per_group = q_group // MGRP
    row = lax.broadcasted_iota(jnp.int32, (rows_all, per_group * 128), 0)
    lane = lax.broadcasted_iota(jnp.int32, (rows_all, per_group * 128), 1)
    q = row % q_group
    wanted = q // MGRP * 128 + (q % MGRP) * parts + row // q_group
    pick = jnp.where(lane == wanted, 1.0, 0.0).astype(jnp.bfloat16)
    row = lax.broadcasted_iota(jnp.int32, (rows_all, KDIM), 0)
    lane = lax.broadcasted_iota(jnp.int32, (rows_all, KDIM), 1)
    same_q = row % q_group == lane // cycles
    modes = jnp.swapaxes(held_ref[...].astype(jnp.float32), 0, 1).astype(jnp.bfloat16)
    for g in range(groups):
        own = jnp.concatenate([modes[g * per_group + k] for k in range(per_group)], axis=1)
        wide = lax.dot_general(
            pick, jnp.concatenate([own] * q_group, axis=0), (((1,), (1,)), ((), ())),
            preferred_element_type=jnp.float32,
        )
        weight_ref[g] = jnp.where(same_q, wide, 0.0).astype(jnp.bfloat16)


def project_tiles(u, maps, share, leg_ref, scales_ref, weight_ref, harm_ref, near_ref):
    groups, rows_all, _ = weight_ref.shape
    parts = 2 * maps
    q_group = rows_all // parts
    width = 2 * LBLK

    def tile(piece, g):
        first_t = u * (share // LBLK) + 2 * piece
        cols = pl.ds(pl.multiple_of(u * share + piece * width, width), width)
        sources = [
            pl.ds(pl.multiple_of((first_t + x) * (LBLK + GAP), 8), LBLK) for x in range(2)
        ]
        rows = slice(g * q_group, (g + 1) * q_group)
        p_rows = jnp.concatenate([scales_ref[first_t + x, rows, :] for x in range(2)], axis=1)
        leg = jnp.concatenate(
            [
                jnp.concatenate(
                    [leg_ref[g * (KDIM // 128) + h, src, :] for h in range(KDIM // 128)], axis=1
                )
                for src in sources
            ],
            axis=0,
        ).astype(jnp.bfloat16)
        out = lax.dot_general(
            weight_ref[g], leg, (((1,), (1,)), ((), ())), preferred_element_type=jnp.float32
        )
        crossed = (out.reshape(parts, q_group, width) * p_rows[None]).astype(jnp.bfloat16)
        harm_ref[:, rows, cols] = crossed
        near_ref[:, rows, piece * width : (piece + 1) * width] = crossed

    return [
        functools.partial(tile, piece, g) for piece in range(share // width) for g in range(groups)
    ]


def product_steps(maps, share, near_ref, sums_ref):
    local_cols = near_ref.shape[1]
    pairs = [(i, k) for i in range(maps) for k in range(i, maps)]
    bounds = [len(pairs) * i // PAIR_GROUPS for i in range(PAIR_GROUPS + 1)]

    def some(half, first, last):
        cols = slice(half * 128, half * 128 + 128)
        total = [None] * (last - first)
        for h in range(2):
            for t in range(local_cols // PACK):
                x = {}
                for n in sorted({v for pair in pairs[first:last] for v in pair}):
                    x[n] = near_ref[h * maps + n, t * PACK : (t + 1) * PACK, cols]
                for p in range(first, last):
                    i, k = pairs[p]
                    term = x[i] * x[k]
                    had = total[p - first]
                    total[p - first] = term if had is None else had + term
        for p in range(first, last):
            sums_ref[p * PACK : (p + 1) * PACK, cols] = total[p - first]

    return [
        functools.partial(some, half, bounds[i], bounds[i + 1])
        for half in range(share // 128)
        for i in range(PAIR_GROUPS)
    ]


def interleave(one, other):
    for i in range(max(len(one), len(other))):
        for steps in (one, other):
            if i < len(steps):
                steps[i]()


def whole_kernel(
    dims, number_hbm, sky_hbm, starts_hbm, first_hbm, wave_hbm, phase_hbm,
    harm_ref, out_ref,
    number_ref, sky_ref, starts_ref, first_ref, wave_ref, phase_ref,
    lhs_ref, rows_ref, turned_ref, held_ref, pieces_ref, scales_ref, z_ref, p_ref,
    turn_ref, init_ref, leg_ref, weight_ref, near_a, near_b, sums_ref, part_ref, other_ref,
    load_sem, send_sem, recv_sem, part_send, part_recv,
):
    blk_total, map_total, maps, factor, scale = dims
    count = blk_total * map_total
    cycles = number_hbm.shape[0]
    share = out_ref.shape[1]
    me_blk, me_map = lax.axis_index("blk"), lax.axis_index("map")
    me = me_blk * map_total + me_map
    k_share = RES // blk_total
    fetched = [
        pltpu.make_async_copy(source, target, load_sem.at[i])
        for i, (source, target) in enumerate(
            [
                (sky_hbm, sky_ref), (wave_hbm, wave_ref), (first_hbm, first_ref),
                (phase_hbm, phase_ref), (number_hbm, number_ref), (starts_hbm, starts_ref),
            ]
        )
    ]
    for copy in fetched:
        copy.start()
    barrier = pltpu.get_barrier_semaphore()
    for i in range(1, count):
        peer = lax.rem(me + i, count)
        pl.semaphore_signal(
            barrier, inc=1,
            device_id={"blk": peer // map_total, "map": lax.rem(peer, map_total)},
            device_id_type=pl.DeviceIdType.MESH,
        )
    for copy in fetched[:-1]:
        copy.wait()
    sky_modes(
        (maps, factor), number_ref, sky_ref, first_ref, wave_ref, phase_ref, lhs_ref, rows_ref, me
    )
    turned_ref[...] = rows_ref[...].T.astype(jnp.bfloat16)
    pl.semaphore_wait(barrier, count - 1)

    def modes_to(peer, source):
        target_blk = peer // map_total
        return pltpu.make_async_remote_copy(
            src_ref=turned_ref.at[pl.ds(pl.multiple_of(target_blk * k_share, k_share), k_share)],
            dst_ref=held_ref.at[source],
            send_sem=send_sem.at[peer],
            recv_sem=recv_sem.at[source],
            device_id={"blk": target_blk, "map": lax.rem(peer, map_total)},
            device_id_type=pl.DeviceIdType.MESH,
        )

    for i in range(1, count):
        modes_to(lax.rem(me + i, count), me).start()
    held_ref[me] = turned_ref[pl.ds(pl.multiple_of(me_blk * k_share, k_share), k_share), :]

    prepare(blk_total, scale, number_ref, pieces_ref, scales_ref, z_ref, p_ref)
    fetched[-1].wait()
    start_values(starts_ref, turn_ref, init_ref)
    for part in range(init_ref.shape[2] // STEP_LANES):
        recurrence(part, cycles, z_ref, pieces_ref, init_ref, leg_ref)

    for i in range(1, count):
        peer = lax.rem(me + i, count)
        modes_to(peer, peer).wait_recv()
    block_weights(maps, held_ref, weight_ref)

    pairs = maps * (maps + 1) // 2
    pair_rows = part_ref.shape[1]
    row = lax.broadcasted_iota(jnp.int32, (pair_rows, pair_rows * PACK), 0)
    lane = lax.broadcasted_iota(jnp.int32, (pair_rows, pair_rows * PACK), 1)
    gather = jnp.where(lane // PACK == row, 1.0, 0.0).astype(jnp.bfloat16)
    for p in range(pairs, pair_rows):
        sums_ref[p * PACK : (p + 1) * PACK, :] = jnp.zeros((PACK, share), jnp.bfloat16)

    def part_to(peer, source):
        return pltpu.make_async_remote_copy(
            src_ref=part_ref.at[peer],
            dst_ref=other_ref.at[source],
            send_sem=part_send.at[peer],
            recv_sem=part_recv.at[source],
            device_id={"blk": peer},
            device_id_type=pl.DeviceIdType.MESH,
        )

    def project(s, near_ref):
        u = lax.rem(me_blk + s, blk_total)
        return project_tiles(u, maps, share, leg_ref, scales_ref, weight_ref, harm_ref, near_ref)

    def finish(s):
        u = lax.rem(me_blk + s, blk_total)
        part_ref[u] = jnp.dot(
            gather, sums_ref[...], preferred_element_type=jnp.float32
        ).astype(jnp.bfloat16)
        return u

    def two_shares(i, _):
        for now, near_ref, next_ref in ((2 * i + 1, near_a, near_b), (2 * i + 2, near_b, near_a)):
            interleave(
                product_steps(maps, share, near_ref, sums_ref), project(now + 1, next_ref)
            )
            part_to(finish(now), me_blk).start()
        return 0

    interleave(project(1, near_a), [])
    lax.fori_loop(0, blk_total // 2 - 1, two_shares, 0)
    interleave(
        product_steps(maps, share, near_a, sums_ref), project(blk_total, near_b)
    )
    part_to(finish(blk_total - 1), me_blk).start()
    interleave(product_steps(maps, share, near_b, sums_ref), [])
    finish(blk_total)
    out_rows = maps * maps
    row = lax.broadcasted_iota(jnp.int32, (out_rows, pair_rows), 0)
    lane = lax.broadcasted_iota(jnp.int32, (out_rows, pair_rows), 1)
    low = jnp.minimum(row // maps, row % maps)
    high = jnp.maximum(row // maps, row % maps)
    pair_at = low * maps - low * (low - 1) // 2 + high - low
    unfold = jnp.where(lane == pair_at, 1.0, 0.0).astype(jnp.bfloat16)
    unfolded = lambda x: jnp.dot(unfold, x, preferred_element_type=jnp.float32)
    total = unfolded(part_ref[me_blk])
    for i in range(1, blk_total):
        peer = lax.rem(me_blk + blk_total - i, blk_total)
        part_to(peer, peer).wait_recv()
        total = total + unfolded(other_ref[peer])
    out_ref[...] = total * (1.0 / (MGRP * RES))
    for i in range(1, count):
        modes_to(lax.rem(me + i, count), me).wait_send()
    for i in range(1, blk_total):
        part_to(lax.rem(me_blk + i, blk_total), me_blk).wait_send()


def constant_tables(cycle_len):
    low_len = cycle_len // RES
    residue = np.arange(RES)
    angle = np.float32(2.0 * math.pi / RES) * (
        residue[:, None] * residue[None, :] % RES
    ).astype(np.float32)
    first = np.concatenate([np.cos(angle), -np.sin(angle)], axis=1)
    first = first.astype(jnp.bfloat16).astype(np.float32)
    m_value = MSTART + RES * np.arange(MGRP)[:, None, None] + residue[None, None, :]
    turn = m_value * np.arange(low_len)[None, :, None] % cycle_len
    angle = np.float32(2.0 * math.pi / cycle_len) * turn.astype(np.float32)
    wave = np.concatenate([np.cos(angle), -np.sin(angle)], axis=2).astype(jnp.bfloat16)
    m_value = MSTART + np.arange(MGRP)[:, None] * RES + np.arange(RES)[None, :]
    angle = np.float32(math.pi / cycle_len) * (m_value % (2 * cycle_len)).astype(np.float32)
    phase = np.concatenate([np.cos(angle), np.sin(angle)], axis=0)
    return jnp.asarray(first), jnp.asarray(wave), jnp.asarray(phase)


def kernel_fits(own_cycles, blk_total, cycles, maps_count, block_count):
    local_cols = MGRP * RES // blk_total
    return (
        own_cycles == 1
        and blk_total % 2 == 0
        and local_cols == 64
        and KDIM % cycles == 0
        and KDIM // cycles == 8
        and 2 * maps_count * MGRP <= 128
        and block_count % 8 == 0
        and block_count % blk_total == 0
        and (block_count * LBLK // blk_total) % (2 * LBLK) == 0
    )


def fast_body(sky_maps, cycle_number, legendre_starts):
    _, maps, cycle_len = sky_maps.shape
    map_total = lax.axis_size("map")
    blk_total = lax.axis_size("blk")
    local_cols, blocks, cycles = legendre_starts.shape[1:]
    count = blk_total * map_total
    local_len = blocks * LBLK
    share = local_len // blk_total
    parts = 2 * maps
    q_group = KDIM // cycles
    lanes = local_cols * cycles
    pair_rows = -(-(maps * (maps + 1) // 2) // 8) * 8
    tables = constant_tables(cycle_len)
    starts = jnp.transpose(legendre_starts, (0, 2, 3, 1))
    dims = (blk_total, map_total, maps, 1.0 / math.sqrt(cycle_len), 1.0 / math.sqrt(cycles))
    vmem = pl.BlockSpec(memory_space=pltpu.VMEM)
    pitch = LBLK + GAP
    harmonics, spectra = pl.pallas_call(
        functools.partial(whole_kernel, dims),
        out_shape=(
            pltpu.VMEM((parts, local_cols, local_len), jnp.bfloat16),
            pltpu.VMEM((maps * maps, share), jnp.float32),
        ),
        in_specs=[pl.BlockSpec(memory_space=pl.ANY)] * 6,
        out_specs=(vmem, vmem),
        scratch_shapes=[pltpu.SMEM(cycle_number.shape, jnp.int32)]
        + [pltpu.VMEM(x.shape, x.dtype) for x in (sky_maps, starts, *tables)]
        + [
            pltpu.VMEM((RES * PACK, cycle_len // RES), jnp.bfloat16),
            pltpu.VMEM((128, RES), jnp.float32),
            pltpu.VMEM((RES, 128), jnp.bfloat16),
            pltpu.VMEM((count, RES // blk_total, 128), jnp.bfloat16),
            pltpu.VMEM((local_len, 256), jnp.bfloat16),
            pltpu.VMEM((blocks, local_cols, LBLK), jnp.float32),
            pltpu.VMEM((1, STEP_LANES), jnp.float32),
            pltpu.VMEM((blocks * pitch, 128), jnp.float32),
            pltpu.VMEM((2, blocks * (local_cols + START_GAP), 128), jnp.float32),
            pltpu.VMEM((2, blocks, lanes), jnp.float32),
            pltpu.VMEM((lanes // 128, blocks * pitch, 128), jnp.float32),
            pltpu.VMEM((local_cols // q_group, parts * q_group, KDIM), jnp.bfloat16),
            pltpu.VMEM((parts, local_cols, share), jnp.bfloat16),
            pltpu.VMEM((parts, local_cols, share), jnp.bfloat16),
            pltpu.VMEM((pair_rows * PACK, share), jnp.bfloat16),
            pltpu.VMEM((blk_total, pair_rows, share), jnp.bfloat16),
            pltpu.VMEM((blk_total, pair_rows, share), jnp.bfloat16),
            pltpu.SemaphoreType.DMA((6,)),
            pltpu.SemaphoreType.DMA((count,)),
            pltpu.SemaphoreType.DMA((count,)),
            pltpu.SemaphoreType.DMA((blk_total,)),
            pltpu.SemaphoreType.DMA((blk_total,)),
        ],
        compiler_params=pltpu.CompilerParams(
            collective_id=0, has_side_effects=True, vmem_limit_bytes=48 * 1024 * 1024
        ),
    )(
        *(
            pltpu.with_memory_space_constraint(x, pltpu.HBM)
            for x in (cycle_number, sky_maps, starts, *tables)
        )
    )
    harmonics, spectra = write_out(harmonics, spectra, maps)
    return (jnp.transpose(harmonics, (1, 0, 2)), jnp.transpose(spectra, (2, 0, 1, 3)))


def write_kernel(maps, harm_ref, sums_ref, harm_out, spectra_ref, sem):
    pieces = sem.shape[0]
    rows = harm_ref.shape[0] // pieces
    copies = [
        pltpu.make_async_copy(
            harm_ref.at[pl.ds(i * rows, rows)], harm_out.at[pl.ds(i * rows, rows)], sem.at[i]
        )
        for i in range(pieces)
    ]
    for copy in copies:
        copy.start()
    for i in range(maps):
        for k in range(maps):
            spectra_ref[i, k] = sums_ref[i * maps + k : i * maps + k + 1]
    for copy in copies:
        copy.wait()


def write_out(harmonics, spectra, maps):
    vmem = pl.BlockSpec(memory_space=pltpu.VMEM)
    return pl.pallas_call(
        functools.partial(write_kernel, maps),
        out_shape=(
            jax.ShapeDtypeStruct(harmonics.shape, harmonics.dtype),
            jax.ShapeDtypeStruct((maps, maps, 1, spectra.shape[1]), jnp.float32),
        ),
        in_specs=[vmem, vmem],
        out_specs=(pl.BlockSpec(memory_space=pl.ANY), vmem),
        scratch_shapes=[pltpu.SemaphoreType.DMA((4,))],
        compiler_params=pltpu.CompilerParams(vmem_limit_bytes=8 * 1024 * 1024),
    )(harmonics, spectra)


def body(sky_maps, cycle_number, legendre_starts):
    own_cycles, maps_count, cycle_len = sky_maps.shape
    map_total = lax.axis_size("map")
    blk_total = lax.axis_size("blk")
    cycles, block_count = cycle_number.shape[0], legendre_starts.shape[2]
    if kernel_fits(own_cycles, blk_total, cycles, maps_count, block_count):
        return fast_body(sky_maps, cycle_number, legendre_starts)
    tables = dft_tables(cycle_len)
    first_row = (lax.axis_index("blk") * map_total + lax.axis_index("map")) * own_cycles
    own_numbers = lax.dynamic_slice_in_dim(cycle_number, first_row, own_cycles)
    parity = (own_numbers - NSIDE + 1) % 2
    local_modes = cycle_transform(sky_maps, parity, tables)
    grouped = lax.all_gather(local_modes, "map", axis=0, tiled=True)
    regrouped = lax.all_to_all(grouped, "blk", split_axis=4, concat_axis=0, tiled=True)
    ordered = jnp.transpose(regrouped, (4, 3, 1, 2, 0))
    local_cols = ordered.shape[0] * ordered.shape[1]
    cycle_modes = ordered.reshape(local_cols, 2 * maps_count, -1)
    heights = cycle_height(cycle_number)
    column = lax.axis_index("blk") * local_cols + jnp.arange(local_cols, dtype=jnp.int32)
    m_float = (MSTART + RES * (column % MGRP) + column // MGRP).astype(jnp.float32)
    block_count = legendre_starts.shape[2]
    local_len = block_count * LBLK
    first_l = LSTART + lax.axis_index("map") * local_len
    cycle_scale = 1.0 / math.sqrt(cycle_modes.shape[-1])

    def one_block(block_index):
        start_pair = lax.dynamic_index_in_dim(legendre_starts, block_index, 2, keepdims=False)
        legendre_tile = legendre_rows(
            start_pair, heights, m_float, first_l + block_index * LBLK
        ).astype(jnp.bfloat16)
        projected = (
            jnp.einsum(
                "qlr,qnr->qnl", legendre_tile, cycle_modes, preferred_element_type=jnp.float32
            )
            * cycle_scale
        )
        return projected.astype(jnp.bfloat16)

    blocks_out = lax.map(one_block, jnp.arange(block_count, dtype=jnp.int32))
    harmonics = jnp.transpose(blocks_out, (1, 2, 0, 3)).reshape(
        local_cols, 2 * maps_count, local_len
    )
    total_cols = MGRP * RES
    spread = harmonics.reshape(local_cols, 2 * maps_count, blk_total, local_len // blk_total)
    spread = jnp.transpose(spread, (2, 3, 1, 0))
    received = lax.all_to_all(
        shortened(spread), "blk", split_axis=0, concat_axis=3, tiled=True
    ).astype(spread.dtype)
    item_count = received.shape[1]
    split_piece = received.reshape(item_count, 2, maps_count, received.shape[3])
    cross_sum = jnp.einsum(
        "gciq,gcjq->ijg", split_piece, split_piece, preferred_element_type=jnp.float32
    )
    owned = (cross_sum / total_cols)[None]
    return (harmonics, owned)


def solution(mesh):
    return jax.shard_map(
        body,
        mesh=mesh,
        in_specs=(P(("blk", "map"), None, None), P(), P(None, "blk", "map", None)),
        out_specs=(P("blk", None, "map"), P("map", None, None, "blk")),
        check_vma=False,
    )
```

```python
import functools
import math

import jax
import jax.numpy as jnp
import numpy as np
from jax import lax
from jax.experimental import pallas as pl
from jax.experimental.pallas import tpu as pltpu
from jax.sharding import PartitionSpec as P

NSIDE = 8192
RES = 128
MGRP = 4
MSTART = 4096
LSTART = 8192
LBLK = 128


def shortened(array):

    def short(part):
        return part.astype(jnp.bfloat16) if part.dtype == jnp.float32 else part

    return jax.tree.map(short, array)


def cycle_height(cycle_ids):
    return (4.0 * NSIDE - 2.0 * cycle_ids.astype(jnp.float32)) / (3.0 * NSIDE)


def dft_tables(cycle_len):
    low_len = cycle_len // RES
    residue = jnp.arange(RES, dtype=jnp.int32)
    turn_one = residue[:, None] * residue[None, :] % RES
    angle_one = 2.0 * math.pi / RES * turn_one.astype(jnp.float32)
    first_table = jnp.concatenate([jnp.cos(angle_one), -jnp.sin(angle_one)], axis=1).astype(
        jnp.bfloat16
    )
    column_group = jnp.arange(MGRP, dtype=jnp.int32)
    sample = jnp.arange(low_len, dtype=jnp.int32)
    m_value = MSTART + RES * column_group[:, None, None] + residue[None, None, :]
    turn_two = m_value * sample[None, :, None] % cycle_len
    angle_two = 2.0 * math.pi / cycle_len * turn_two.astype(jnp.float32)
    twiddle_re = jnp.cos(angle_two).astype(jnp.bfloat16)
    twiddle_im = (-jnp.sin(angle_two)).astype(jnp.bfloat16)
    return (first_table, twiddle_re, twiddle_im)


def cycle_transform(cycle_rows, parity, tables):
    first_table, twiddle_re, twiddle_im = tables
    cycle_count, maps_count, cycle_len = cycle_rows.shape
    low_len = cycle_len // RES
    folded = cycle_rows.reshape(cycle_count, maps_count, RES, low_len)
    section_one = jnp.einsum(
        "rnaj,ak->rnjk", folded, first_table, preferred_element_type=jnp.float32
    )
    section_one = section_one.astype(jnp.bfloat16)
    part_re = section_one[..., :RES]
    part_im = section_one[..., RES:]
    real_sum = jnp.einsum(
        "rnjk,cjk->rnck", part_re, twiddle_re, preferred_element_type=jnp.float32
    ) - jnp.einsum("rnjk,cjk->rnck", part_im, twiddle_im, preferred_element_type=jnp.float32)
    imag_sum = jnp.einsum(
        "rnjk,cjk->rnck", part_im, twiddle_re, preferred_element_type=jnp.float32
    ) + jnp.einsum("rnjk,cjk->rnck", part_re, twiddle_im, preferred_element_type=jnp.float32)
    column_group = jnp.arange(MGRP, dtype=jnp.int32)
    residue = jnp.arange(RES, dtype=jnp.int32)
    m_value = MSTART + RES * column_group[:, None] + residue[None, :]
    shifted = m_value[None, :, :] * parity[:, None, None] % (2 * cycle_len)
    phase_angle = math.pi / cycle_len * shifted.astype(jnp.float32)
    cos_part = jnp.cos(phase_angle)[:, None]
    sin_part = jnp.sin(phase_angle)[:, None]
    factor = 1.0 / math.sqrt(cycle_len)
    out_re = factor * (cos_part * real_sum + sin_part * imag_sum)
    out_im = factor * (cos_part * imag_sum - sin_part * real_sum)
    return jnp.stack([out_re, out_im], axis=1).astype(jnp.bfloat16)


def legendre_rows(start_pair, height, m_float, first_l):
    m_column = m_float[:, None]

    def recur_coef(degree):
        return jnp.sqrt((4.0 * degree * degree - 1.0) / ((degree - m_column) * (degree + m_column)))

    base_l = first_l.astype(jnp.float32)
    value_older = start_pair[0]
    value_newer = start_pair[1]
    prior_coef = recur_coef(base_l - 1.0)
    height_row = height[None, :]
    stacked_rows = []
    for offset in range(LBLK):
        present_coef = recur_coef(base_l + offset)
        value_now = present_coef * (height_row * value_newer - value_older / prior_coef)
        stacked_rows.append(value_now)
        value_older = value_newer
        value_newer = value_now
        prior_coef = present_coef
    return jnp.stack(stacked_rows, axis=1)


STEP_LANES = 1024
KDIM = 256
GAP = 8
RUN = 64
PACK = 16
START_GAP = 8
PAIR_GROUPS = 2


def sky_modes(totals, number_ref, sky_ref, first_ref, twice_ref, wave_ref, phase_ref, lhs_ref,
              rest_ref, rows_ref, me):
    maps, factor = totals
    low_len = wave_ref.shape[1]
    more = maps - 8
    for a in range(RES):
        values = sky_ref[0, :, a * low_len : (a + 1) * low_len].astype(jnp.float32)
        lhs_ref[a * 8 : a * 8 + 8, :] = values[:8]
        rest_ref[a * more : (a + 1) * more, :] = values[8:]
    rows_ref[...] = jnp.zeros_like(rows_ref)
    parity = (number_ref[me] - NSIDE + 1) % 2
    odd = jnp.full((MGRP, RES), parity, jnp.int32) == 1
    cosines = jnp.where(odd, phase_ref[:MGRP], 1.0)
    sines = jnp.where(odd, phase_ref[MGRP:], 0.0)
    none = jnp.zeros((8, RES), jnp.float32)
    for c in range(MGRP):
        real, imag, real_more, imag_more = none, none, none, none
        out = jnp.dot(
            lhs_ref[...].astype(jnp.bfloat16), wave_ref[c], preferred_element_type=jnp.float32
        )
        for a in range(RES):
            e_re, e_im = first_ref[a : a + 1, :RES], first_ref[a : a + 1, RES:]
            w_re, w_im = out[a * 8 : a * 8 + 8, :RES], out[a * 8 : a * 8 + 8, RES:]
            real = real + (e_re * w_re - e_im * w_im)
            imag = imag + (e_re * w_im + e_im * w_re)
        out = jnp.dot(
            rest_ref[...].astype(jnp.bfloat16), wave_ref[c], preferred_element_type=jnp.float32
        )
        for a in range(RES * more // 8):
            rows = slice(a * 8, a * 8 + 8)
            e_re, e_im = twice_ref[rows, :RES], twice_ref[rows, RES:]
            w_re, w_im = out[rows, :RES], out[rows, RES:]
            real_more = real_more + (e_re * w_re - e_im * w_im)
            imag_more = imag_more + (e_re * w_im + e_im * w_re)
        cos, sin = cosines[c : c + 1], sines[c : c + 1]
        row = c * 2 * maps
        for re, im, at, size in ((real, imag, 0, 8), (real_more, imag_more, 8, more)):
            if size != 8:
                re = sum(re[i : i + size] for i in range(0, 8, size))
                im = sum(im[i : i + size] for i in range(0, 8, size))
            first = row + at
            rows_ref[first : first + size, :] = factor * (cos * re + sin * im)
            rows_ref[first + maps : first + maps + size, :] = factor * (cos * im - sin * re)


def heights(number_ref, z_ref):
    lane = lax.broadcasted_iota(jnp.int32, z_ref.shape, 1) % number_ref.shape[0]
    numbers = jnp.zeros(z_ref.shape, jnp.int32)
    for r in range(number_ref.shape[0]):
        numbers = jnp.where(lane == r, number_ref[r], numbers)
    z_ref[...] = cycle_height(numbers)


def prepare(blk_total, scale, pieces_ref, scales_ref, p_ref):
    blocks = scales_ref.shape[0]
    local_cols = MGRP * RES // blk_total
    lane = lax.broadcasted_iota(jnp.int32, (blocks, 128), 1)
    column = lax.axis_index("blk") * local_cols + lane % local_cols
    m_row = (MSTART + RES * (column % MGRP) + column // MGRP).astype(jnp.float32)
    block = lax.broadcasted_iota(jnp.int32, (blocks, 128), 0)
    base = LSTART + (lax.axis_index("map") * blocks + block) * LBLK

    def setup(j, carry):
        p_prev, q_prev = carry
        degree = (base + j).astype(jnp.float32)
        num = 4.0 * degree * degree - 1.0
        den = (degree - m_row) * (degree + m_row)
        root = lax.rsqrt(num * den)
        kappa = p_prev * p_prev
        high = kappa.astype(jnp.bfloat16).astype(jnp.float32)
        rest = kappa - high
        mid = rest.astype(jnp.bfloat16).astype(jnp.float32)
        low = rest - mid
        rows = pl.ds(pl.multiple_of(j * blocks, blocks), blocks)
        pieces_ref[rows, :128] = jnp.where(lane < local_cols, high, mid).astype(jnp.bfloat16)
        pieces_ref[rows, 128:] = low.astype(jnp.bfloat16)
        p_now = num * root * q_prev
        q_now = den * root * p_prev
        for half in range(blocks // 8):
            p_ref[pl.ds(half * 8 * (LBLK + GAP) + j, 8, stride=LBLK + GAP), :] = p_now[
                half * 8 : half * 8 + 8
            ]
        return p_now, q_now

    one = jnp.ones((blocks, 128), jnp.float32)
    lax.fori_loop(0, LBLK, setup, (one, one), unroll=4)

    def turn(t, _):
        turned = p_ref[pl.ds(pl.multiple_of(t * (LBLK + GAP), 8), LBLK), :].T
        scales_ref[t] = turned[:local_cols] * scale
        return 0

    lax.fori_loop(0, blocks, turn, 0)


def start_values(starts_ref, turn_ref, init_ref):
    _, blocks, cycles, local_cols = starts_ref.shape
    lane = lax.broadcasted_iota(jnp.int32, (blocks, local_cols), 1)
    column = lax.axis_index("blk") * local_cols + lane
    m_row = (MSTART + RES * (column % MGRP) + column // MGRP).astype(jnp.float32)
    block = lax.broadcasted_iota(jnp.int32, (blocks, local_cols), 0)
    degree = (LSTART + (lax.axis_index("map") * blocks + block) * LBLK - 1).astype(jnp.float32)
    inverse = jnp.sqrt(((degree - m_row) * (degree + m_row)) / (4.0 * degree * degree - 1.0))
    pitch = local_cols + START_GAP
    for kind in range(2):
        for t in range(blocks):
            values = starts_ref[kind, t]
            if kind == 0:
                values = values * inverse[t : t + 1]
            turn_ref[kind, t * pitch : t * pitch + local_cols, :cycles] = values.T
    per_tile = 128 // cycles
    slot = lax.broadcasted_iota(jnp.int32, (8, 128), 1) // cycles
    for kind in range(2):
        for half in range(blocks // 8):
            for tile in range(local_cols // per_tile):
                row = None
                for i in range(per_tile):
                    first = half * 8 * pitch + tile * per_tile + i
                    part = turn_ref[kind, pl.ds(first, 8, stride=pitch), :]
                    if i == 0:
                        row = part
                    else:
                        row = jnp.where(slot == i, pltpu.roll(part, i * cycles, 1), row)
                init_ref[kind, half * 8 : half * 8 + 8, tile * 128 : tile * 128 + 128] = row


def recurrence(part, cycles, z_ref, pieces_ref, init_ref, leg_ref):
    blocks = init_ref.shape[1]
    halves = STEP_LANES // 128
    q_row = lax.broadcasted_iota(jnp.int32, (256, STEP_LANES), 0)
    q_lane = lax.broadcasted_iota(jnp.int32, (256, STEP_LANES), 1) // cycles + part * (
        STEP_LANES // cycles
    )
    spread = jnp.where((q_row % 64 == q_lane) & (q_row < 192), 1.0, 0.0).astype(jnp.bfloat16)

    def recur(i, carry):
        older, newer = carry
        rows = pl.ds(pl.multiple_of(i * RUN * blocks, RUN * blocks), RUN * blocks)
        kap = jnp.dot(pieces_ref[rows, :], spread, preferred_element_type=jnp.float32)
        for j in range(RUN):
            now = (kap[j * blocks : (j + 1) * blocks] * z_ref[...]) * newer - older
            for half in range(blocks // 8):
                at = pl.ds(half * 8 * (LBLK + GAP) + i * RUN + j, 8, stride=LBLK + GAP)
                for g in range(halves):
                    leg_ref[part * halves + g, at, :] = now[
                        half * 8 : half * 8 + 8, g * 128 : g * 128 + 128
                    ]
            older, newer = newer, now
        return older, newer

    lanes = slice(part * STEP_LANES, (part + 1) * STEP_LANES)
    lax.fori_loop(0, LBLK // RUN, recur, (init_ref[0, :, lanes], init_ref[1, :, lanes]))


def block_weights(maps, held_ref, weight_ref):
    groups, rows_all, _ = weight_ref.shape
    cycles, _, _ = held_ref.shape
    parts = 2 * maps
    q_group = rows_all // parts
    per_group = q_group // MGRP
    row = lax.broadcasted_iota(jnp.int32, (rows_all, per_group * 128), 0)
    lane = lax.broadcasted_iota(jnp.int32, (rows_all, per_group * 128), 1)
    q = row % q_group
    wanted = q // MGRP * 128 + (q % MGRP) * parts + row // q_group
    pick = jnp.where(lane == wanted, 1.0, 0.0).astype(jnp.bfloat16)
    row = lax.broadcasted_iota(jnp.int32, (rows_all, KDIM), 0)
    lane = lax.broadcasted_iota(jnp.int32, (rows_all, KDIM), 1)
    same_q = row % q_group == lane // cycles
    modes = jnp.swapaxes(held_ref[...].astype(jnp.float32), 0, 1).astype(jnp.bfloat16)
    for g in range(groups):
        own = jnp.concatenate([modes[g * per_group + k] for k in range(per_group)], axis=1)
        wide = lax.dot_general(
            pick, jnp.concatenate([own] * q_group, axis=0), (((1,), (1,)), ((), ())),
            preferred_element_type=jnp.float32,
        )
        weight_ref[g] = jnp.where(same_q, wide, 0.0).astype(jnp.bfloat16)


def project_tiles(u, maps, share, leg_ref, scales_ref, weight_ref, harm_ref, near_ref):
    groups, rows_all, _ = weight_ref.shape
    parts = 2 * maps
    q_group = rows_all // parts
    width = 2 * LBLK

    def tile(piece, g):
        first_t = u * (share // LBLK) + 2 * piece
        cols = pl.ds(pl.multiple_of(u * share + piece * width, width), width)
        sources = [
            pl.ds(pl.multiple_of((first_t + x) * (LBLK + GAP), 8), LBLK) for x in range(2)
        ]
        rows = slice(g * q_group, (g + 1) * q_group)
        p_rows = jnp.concatenate([scales_ref[first_t + x, rows, :] for x in range(2)], axis=1)
        leg = jnp.concatenate(
            [
                jnp.concatenate(
                    [leg_ref[g * (KDIM // 128) + h, src, :] for h in range(KDIM // 128)], axis=1
                )
                for src in sources
            ],
            axis=0,
        ).astype(jnp.bfloat16)
        out = lax.dot_general(
            weight_ref[g], leg, (((1,), (1,)), ((), ())), preferred_element_type=jnp.float32
        )
        crossed = (out.reshape(parts, q_group, width) * p_rows[None]).astype(jnp.bfloat16)
        harm_ref[:, rows, cols] = crossed
        for x in range(2):
            near_ref[2 * piece + x, :, rows, :] = crossed[:, :, x * LBLK : (x + 1) * LBLK]

    return [
        functools.partial(tile, piece, g) for piece in range(share // width) for g in range(groups)
    ]


def product_steps(maps, share, near_ref, sums_ref):
    local_cols = near_ref.shape[2]
    pairs = [(i, k) for i in range(maps) for k in range(i, maps)]
    bounds = [len(pairs) * i // PAIR_GROUPS for i in range(PAIR_GROUPS + 1)]

    def some(half, first, last):
        total = [None] * (last - first)
        for h in range(2):
            for t in range(local_cols // PACK):
                x = {}
                for n in sorted({v for pair in pairs[first:last] for v in pair}):
                    x[n] = near_ref[half, h * maps + n, t * PACK : (t + 1) * PACK, :]
                for p in range(first, last):
                    i, k = pairs[p]
                    term = x[i] * x[k]
                    had = total[p - first]
                    total[p - first] = term if had is None else had + term
        for p in range(first, last):
            sums_ref[half, p * PACK : (p + 1) * PACK, :] = total[p - first]

    return [
        functools.partial(some, half, bounds[i], bounds[i + 1])
        for half in range(share // 128)
        for i in range(PAIR_GROUPS)
    ]


def interleave(one, other):
    for i in range(max(len(one), len(other))):
        for steps in (one, other):
            if i < len(steps):
                steps[i]()


def whole_kernel(
    dims, number_hbm, sky_hbm, starts_hbm, first_hbm, twice_hbm, wave_hbm, phase_hbm,
    harm_ref, out_ref,
    number_ref, sky_ref, starts_ref, first_ref, twice_ref, wave_ref, phase_ref,
    lhs_ref, rest_ref, rows_ref, turned_ref, held_ref, pieces_ref, scales_ref, z_ref, p_ref,
    turn_ref, init_ref, leg_ref, weight_ref, near_a, near_b, sums_ref, part_ref, other_ref,
    load_sem, send_sem, recv_sem, part_send, part_recv,
):
    blk_total, map_total, maps, factor, scale = dims
    count = blk_total * map_total
    cycles = number_hbm.shape[0]
    share = out_ref.shape[1]
    me_blk, me_map = lax.axis_index("blk"), lax.axis_index("map")
    me = me_blk * map_total + me_map
    k_share = RES // blk_total
    fetched = [
        pltpu.make_async_copy(source, target, load_sem.at[i])
        for i, (source, target) in enumerate(
            [
                (sky_hbm, sky_ref), (wave_hbm, wave_ref), (first_hbm, first_ref),
                (twice_hbm, twice_ref),
                (phase_hbm, phase_ref), (number_hbm, number_ref), (starts_hbm, starts_ref),
            ]
        )
    ]
    for copy in fetched:
        copy.start()
    barrier = pltpu.get_barrier_semaphore()
    for i in range(1, count):
        peer = lax.rem(me + i, count)
        pl.semaphore_signal(
            barrier, inc=1,
            device_id={"blk": peer // map_total, "map": lax.rem(peer, map_total)},
            device_id_type=pl.DeviceIdType.MESH,
        )
    prepare(blk_total, scale, pieces_ref, scales_ref, p_ref)
    for copy in fetched[:-1]:
        copy.wait()
    sky_modes(
        (maps, factor), number_ref, sky_ref, first_ref, twice_ref, wave_ref, phase_ref, lhs_ref,
        rest_ref, rows_ref, me,
    )
    turned_ref[...] = rows_ref[...].T.astype(jnp.bfloat16)
    pl.semaphore_wait(barrier, count - 1)

    def modes_to(peer, source):
        target_blk = peer // map_total
        return pltpu.make_async_remote_copy(
            src_ref=turned_ref.at[pl.ds(pl.multiple_of(target_blk * k_share, k_share), k_share)],
            dst_ref=held_ref.at[source],
            send_sem=send_sem.at[peer],
            recv_sem=recv_sem.at[source],
            device_id={"blk": target_blk, "map": lax.rem(peer, map_total)},
            device_id_type=pl.DeviceIdType.MESH,
        )

    for i in range(1, count):
        modes_to(lax.rem(me + i, count), me).start()
    held_ref[me] = turned_ref[pl.ds(pl.multiple_of(me_blk * k_share, k_share), k_share), :]

    heights(number_ref, z_ref)
    fetched[-1].wait()
    start_values(starts_ref, turn_ref, init_ref)
    for part in range(init_ref.shape[2] // STEP_LANES):
        recurrence(part, cycles, z_ref, pieces_ref, init_ref, leg_ref)

    for i in range(1, count):
        peer = lax.rem(me + i, count)
        modes_to(peer, peer).wait_recv()
    block_weights(maps, held_ref, weight_ref)

    pairs = maps * (maps + 1) // 2
    pair_rows = part_ref.shape[1]
    row = lax.broadcasted_iota(jnp.int32, (pair_rows, pair_rows * PACK), 0)
    lane = lax.broadcasted_iota(jnp.int32, (pair_rows, pair_rows * PACK), 1)
    gather = jnp.where(lane // PACK == row, 1.0, 0.0).astype(jnp.bfloat16)
    for p in range(pairs, pair_rows):
        for half in range(share // 128):
            sums_ref[half, p * PACK : (p + 1) * PACK, :] = jnp.zeros((PACK, 128), jnp.bfloat16)

    def part_to(peer, source):
        return pltpu.make_async_remote_copy(
            src_ref=part_ref.at[peer],
            dst_ref=other_ref.at[source],
            send_sem=part_send.at[peer],
            recv_sem=part_recv.at[source],
            device_id={"blk": peer},
            device_id_type=pl.DeviceIdType.MESH,
        )

    def project(s, near_ref):
        u = lax.rem(me_blk + s, blk_total)
        return project_tiles(u, maps, share, leg_ref, scales_ref, weight_ref, harm_ref, near_ref)

    def finish(s):
        u = lax.rem(me_blk + s, blk_total)
        sums = jnp.concatenate([sums_ref[half] for half in range(share // 128)], axis=1)
        part_ref[u] = jnp.dot(gather, sums, preferred_element_type=jnp.float32).astype(
            jnp.bfloat16
        )
        return u

    def two_shares(i, _):
        for now, near_ref, next_ref in ((2 * i + 1, near_a, near_b), (2 * i + 2, near_b, near_a)):
            interleave(
                product_steps(maps, share, near_ref, sums_ref), project(now + 1, next_ref)
            )
            part_to(finish(now), me_blk).start()
        return 0

    interleave(project(1, near_a), [])
    lax.fori_loop(0, blk_total // 2 - 1, two_shares, 0)
    interleave(product_steps(maps, share, near_a, sums_ref), [])
    part_to(finish(blk_total - 1), me_blk).start()
    interleave(project(blk_total, near_b), [])
    interleave(product_steps(maps, share, near_b, sums_ref), [])
    finish(blk_total)
    out_rows = maps * maps
    row = lax.broadcasted_iota(jnp.int32, (out_rows, pair_rows), 0)
    lane = lax.broadcasted_iota(jnp.int32, (out_rows, pair_rows), 1)
    low = jnp.minimum(row // maps, row % maps)
    high = jnp.maximum(row // maps, row % maps)
    pair_at = low * maps - low * (low - 1) // 2 + high - low
    unfold = jnp.where(lane == pair_at, 1.0, 0.0).astype(jnp.bfloat16)
    unfolded = lambda x: jnp.dot(unfold, x, preferred_element_type=jnp.float32)
    total = unfolded(part_ref[me_blk])
    for i in range(1, blk_total):
        peer = lax.rem(me_blk + blk_total - i, blk_total)
        part_to(peer, peer).wait_recv()
        total = total + unfolded(other_ref[peer])
    out_ref[...] = total * (1.0 / (MGRP * RES))
    for i in range(1, count):
        modes_to(lax.rem(me + i, count), me).wait_send()
    for i in range(1, blk_total):
        part_to(lax.rem(me_blk + i, blk_total), me_blk).wait_send()


def constant_tables(cycle_len, maps):
    low_len = cycle_len // RES
    residue = np.arange(RES)
    angle = np.float32(2.0 * math.pi / RES) * (
        residue[:, None] * residue[None, :] % RES
    ).astype(np.float32)
    first = np.concatenate([np.cos(angle), -np.sin(angle)], axis=1)
    first = first.astype(jnp.bfloat16).astype(np.float32)
    m_value = MSTART + RES * np.arange(MGRP)[:, None, None] + residue[None, None, :]
    turn = m_value * np.arange(low_len)[None, :, None] % cycle_len
    angle = np.float32(2.0 * math.pi / cycle_len) * turn.astype(np.float32)
    wave = np.concatenate([np.cos(angle), -np.sin(angle)], axis=2).astype(jnp.bfloat16)
    m_value = MSTART + np.arange(MGRP)[:, None] * RES + np.arange(RES)[None, :]
    angle = np.float32(math.pi / cycle_len) * (m_value % (2 * cycle_len)).astype(np.float32)
    phase = np.concatenate([np.cos(angle), np.sin(angle)], axis=0)
    twice = np.repeat(first, maps - 8, axis=0)
    return jnp.asarray(first), jnp.asarray(twice), jnp.asarray(wave), jnp.asarray(phase)


def kernel_fits(own_cycles, blk_total, cycles, maps_count, block_count):
    local_cols = MGRP * RES // blk_total
    return (
        own_cycles == 1
        and blk_total % 2 == 0
        and maps_count in (9, 10, 12)
        and local_cols == 64
        and KDIM % cycles == 0
        and KDIM // cycles == 8
        and 2 * maps_count * MGRP <= 128
        and block_count % 8 == 0
        and block_count % blk_total == 0
        and (block_count * LBLK // blk_total) % (2 * LBLK) == 0
    )


def fast_body(sky_maps, cycle_number, legendre_starts):
    _, maps, cycle_len = sky_maps.shape
    map_total = lax.axis_size("map")
    blk_total = lax.axis_size("blk")
    local_cols, blocks, cycles = legendre_starts.shape[1:]
    count = blk_total * map_total
    local_len = blocks * LBLK
    share = local_len // blk_total
    parts = 2 * maps
    q_group = KDIM // cycles
    lanes = local_cols * cycles
    pair_rows = -(-(maps * (maps + 1) // 2) // 8) * 8
    tables = constant_tables(cycle_len, maps)
    starts = jnp.transpose(legendre_starts, (0, 2, 3, 1))
    dims = (blk_total, map_total, maps, 1.0 / math.sqrt(cycle_len), 1.0 / math.sqrt(cycles))
    vmem = pl.BlockSpec(memory_space=pltpu.VMEM)
    pitch = LBLK + GAP
    harmonics, spectra = pl.pallas_call(
        functools.partial(whole_kernel, dims),
        out_shape=(
            pltpu.VMEM((parts, local_cols, local_len), jnp.bfloat16),
            pltpu.VMEM((maps * maps, share), jnp.float32),
        ),
        in_specs=[pl.BlockSpec(memory_space=pl.ANY)] * 7,
        out_specs=(vmem, vmem),
        scratch_shapes=[pltpu.SMEM(cycle_number.shape, jnp.int32)]
        + [pltpu.VMEM(x.shape, x.dtype) for x in (sky_maps, starts, *tables)]
        + [
            pltpu.VMEM((RES * 8, cycle_len // RES), jnp.float32),
            pltpu.VMEM((RES * (maps - 8), cycle_len // RES), jnp.float32),
            pltpu.VMEM((128, RES), jnp.float32),
            pltpu.VMEM((RES, 128), jnp.bfloat16),
            pltpu.VMEM((count, RES // blk_total, 128), jnp.bfloat16),
            pltpu.VMEM((local_len, 256), jnp.bfloat16),
            pltpu.VMEM((blocks, local_cols, LBLK), jnp.float32),
            pltpu.VMEM((1, STEP_LANES), jnp.float32),
            pltpu.VMEM((blocks * pitch, 128), jnp.float32),
            pltpu.VMEM((2, blocks * (local_cols + START_GAP), 128), jnp.float32),
            pltpu.VMEM((2, blocks, lanes), jnp.float32),
            pltpu.VMEM((lanes // 128, blocks * pitch, 128), jnp.float32),
            pltpu.VMEM((local_cols // q_group, parts * q_group, KDIM), jnp.bfloat16),
            pltpu.VMEM((share // 128, parts, local_cols, 128), jnp.bfloat16),
            pltpu.VMEM((share // 128, parts, local_cols, 128), jnp.bfloat16),
            pltpu.VMEM((share // 128, pair_rows * PACK, 128), jnp.bfloat16),
            pltpu.VMEM((blk_total, pair_rows, share), jnp.bfloat16),
            pltpu.VMEM((blk_total, pair_rows, share), jnp.bfloat16),
            pltpu.SemaphoreType.DMA((7,)),
            pltpu.SemaphoreType.DMA((count,)),
            pltpu.SemaphoreType.DMA((count,)),
            pltpu.SemaphoreType.DMA((blk_total,)),
            pltpu.SemaphoreType.DMA((blk_total,)),
        ],
        compiler_params=pltpu.CompilerParams(
            collective_id=0, has_side_effects=True, vmem_limit_bytes=48 * 1024 * 1024
        ),
    )(
        *(
            pltpu.with_memory_space_constraint(x, pltpu.HBM)
            for x in (cycle_number, sky_maps, starts, *tables)
        )
    )
    harmonics, spectra = write_out(harmonics, spectra, maps)
    return (jnp.transpose(harmonics, (1, 0, 2)), jnp.transpose(spectra, (2, 0, 1, 3)))


def write_kernel(maps, harm_ref, sums_ref, harm_out, spectra_out, spectra_ref, sem, spectra_sem):
    pieces = sem.shape[0]
    rows = harm_ref.shape[0] // pieces
    copies = [
        pltpu.make_async_copy(
            harm_ref.at[pl.ds(i * rows, rows)], harm_out.at[pl.ds(i * rows, rows)], sem.at[i]
        )
        for i in range(pieces)
    ]
    for copy in copies:
        copy.start()
    for i in range(maps):
        for k in range(maps):
            spectra_ref[i, k] = sums_ref[i * maps + k : i * maps + k + 1]
    last = pltpu.make_async_copy(spectra_ref, spectra_out, spectra_sem)
    last.start()
    for copy in copies:
        copy.wait()
    last.wait()


def write_out(harmonics, spectra, maps):
    vmem = pl.BlockSpec(memory_space=pltpu.VMEM)
    shape = (maps, maps, 1, spectra.shape[1])
    return pl.pallas_call(
        functools.partial(write_kernel, maps),
        out_shape=(
            jax.ShapeDtypeStruct(harmonics.shape, harmonics.dtype),
            jax.ShapeDtypeStruct(shape, jnp.float32),
        ),
        in_specs=[vmem, vmem],
        out_specs=(pl.BlockSpec(memory_space=pl.ANY),) * 2,
        scratch_shapes=[
            pltpu.VMEM(shape, jnp.float32),
            pltpu.SemaphoreType.DMA((2,)),
            pltpu.SemaphoreType.DMA,
        ],
        compiler_params=pltpu.CompilerParams(vmem_limit_bytes=8 * 1024 * 1024),
    )(harmonics, spectra)


def body(sky_maps, cycle_number, legendre_starts):
    own_cycles, maps_count, cycle_len = sky_maps.shape
    map_total = lax.axis_size("map")
    blk_total = lax.axis_size("blk")
    cycles, block_count = cycle_number.shape[0], legendre_starts.shape[2]
    if kernel_fits(own_cycles, blk_total, cycles, maps_count, block_count):
        return fast_body(sky_maps, cycle_number, legendre_starts)
    tables = dft_tables(cycle_len)
    first_row = (lax.axis_index("blk") * map_total + lax.axis_index("map")) * own_cycles
    own_numbers = lax.dynamic_slice_in_dim(cycle_number, first_row, own_cycles)
    parity = (own_numbers - NSIDE + 1) % 2
    local_modes = cycle_transform(sky_maps, parity, tables)
    grouped = lax.all_gather(local_modes, "map", axis=0, tiled=True)
    regrouped = lax.all_to_all(grouped, "blk", split_axis=4, concat_axis=0, tiled=True)
    ordered = jnp.transpose(regrouped, (4, 3, 1, 2, 0))
    local_cols = ordered.shape[0] * ordered.shape[1]
    cycle_modes = ordered.reshape(local_cols, 2 * maps_count, -1)
    heights = cycle_height(cycle_number)
    column = lax.axis_index("blk") * local_cols + jnp.arange(local_cols, dtype=jnp.int32)
    m_float = (MSTART + RES * (column % MGRP) + column // MGRP).astype(jnp.float32)
    block_count = legendre_starts.shape[2]
    local_len = block_count * LBLK
    first_l = LSTART + lax.axis_index("map") * local_len
    cycle_scale = 1.0 / math.sqrt(cycle_modes.shape[-1])

    def one_block(block_index):
        start_pair = lax.dynamic_index_in_dim(legendre_starts, block_index, 2, keepdims=False)
        legendre_tile = legendre_rows(
            start_pair, heights, m_float, first_l + block_index * LBLK
        ).astype(jnp.bfloat16)
        projected = (
            jnp.einsum(
                "qlr,qnr->qnl", legendre_tile, cycle_modes, preferred_element_type=jnp.float32
            )
            * cycle_scale
        )
        return projected.astype(jnp.bfloat16)

    blocks_out = lax.map(one_block, jnp.arange(block_count, dtype=jnp.int32))
    harmonics = jnp.transpose(blocks_out, (1, 2, 0, 3)).reshape(
        local_cols, 2 * maps_count, local_len
    )
    total_cols = MGRP * RES
    spread = harmonics.reshape(local_cols, 2 * maps_count, blk_total, local_len // blk_total)
    spread = jnp.transpose(spread, (2, 3, 1, 0))
    received = lax.all_to_all(
        shortened(spread), "blk", split_axis=0, concat_axis=3, tiled=True
    ).astype(spread.dtype)
    item_count = received.shape[1]
    split_piece = received.reshape(item_count, 2, maps_count, received.shape[3])
    cross_sum = jnp.einsum(
        "gciq,gcjq->ijg", split_piece, split_piece, preferred_element_type=jnp.float32
    )
    owned = (cross_sum / total_cols)[None]
    return (harmonics, owned)


def solution(mesh):
    return jax.shard_map(
        body,
        mesh=mesh,
        in_specs=(P(("blk", "map"), None, None), P(), P(None, "blk", "map", None)),
        out_specs=(P("blk", None, "map"), P("map", None, None, "blk")),
        check_vma=False,
    )
```

```python
import functools
import math

import jax
import jax.numpy as jnp
import numpy as np
from jax import lax
from jax.experimental import pallas as pl
from jax.experimental.pallas import tpu as pltpu
from jax.sharding import PartitionSpec as P

NSIDE = 8192
RES = 128
MGRP = 4
MSTART = 4096
LSTART = 8192
LBLK = 128


def shortened(array):

    def short(part):
        return part.astype(jnp.bfloat16) if part.dtype == jnp.float32 else part

    return jax.tree.map(short, array)


def cycle_height(cycle_ids):
    return (4.0 * NSIDE - 2.0 * cycle_ids.astype(jnp.float32)) / (3.0 * NSIDE)


def dft_tables(cycle_len):
    low_len = cycle_len // RES
    residue = jnp.arange(RES, dtype=jnp.int32)
    turn_one = residue[:, None] * residue[None, :] % RES
    angle_one = 2.0 * math.pi / RES * turn_one.astype(jnp.float32)
    first_table = jnp.concatenate([jnp.cos(angle_one), -jnp.sin(angle_one)], axis=1).astype(
        jnp.bfloat16
    )
    column_group = jnp.arange(MGRP, dtype=jnp.int32)
    sample = jnp.arange(low_len, dtype=jnp.int32)
    m_value = MSTART + RES * column_group[:, None, None] + residue[None, None, :]
    turn_two = m_value * sample[None, :, None] % cycle_len
    angle_two = 2.0 * math.pi / cycle_len * turn_two.astype(jnp.float32)
    twiddle_re = jnp.cos(angle_two).astype(jnp.bfloat16)
    twiddle_im = (-jnp.sin(angle_two)).astype(jnp.bfloat16)
    return (first_table, twiddle_re, twiddle_im)


def cycle_transform(cycle_rows, parity, tables):
    first_table, twiddle_re, twiddle_im = tables
    cycle_count, maps_count, cycle_len = cycle_rows.shape
    low_len = cycle_len // RES
    folded = cycle_rows.reshape(cycle_count, maps_count, RES, low_len)
    section_one = jnp.einsum(
        "rnaj,ak->rnjk", folded, first_table, preferred_element_type=jnp.float32
    )
    section_one = section_one.astype(jnp.bfloat16)
    part_re = section_one[..., :RES]
    part_im = section_one[..., RES:]
    real_sum = jnp.einsum(
        "rnjk,cjk->rnck", part_re, twiddle_re, preferred_element_type=jnp.float32
    ) - jnp.einsum("rnjk,cjk->rnck", part_im, twiddle_im, preferred_element_type=jnp.float32)
    imag_sum = jnp.einsum(
        "rnjk,cjk->rnck", part_im, twiddle_re, preferred_element_type=jnp.float32
    ) + jnp.einsum("rnjk,cjk->rnck", part_re, twiddle_im, preferred_element_type=jnp.float32)
    column_group = jnp.arange(MGRP, dtype=jnp.int32)
    residue = jnp.arange(RES, dtype=jnp.int32)
    m_value = MSTART + RES * column_group[:, None] + residue[None, :]
    shifted = m_value[None, :, :] * parity[:, None, None] % (2 * cycle_len)
    phase_angle = math.pi / cycle_len * shifted.astype(jnp.float32)
    cos_part = jnp.cos(phase_angle)[:, None]
    sin_part = jnp.sin(phase_angle)[:, None]
    factor = 1.0 / math.sqrt(cycle_len)
    out_re = factor * (cos_part * real_sum + sin_part * imag_sum)
    out_im = factor * (cos_part * imag_sum - sin_part * real_sum)
    return jnp.stack([out_re, out_im], axis=1).astype(jnp.bfloat16)


def legendre_rows(start_pair, height, m_float, first_l):
    m_column = m_float[:, None]

    def recur_coef(degree):
        return jnp.sqrt((4.0 * degree * degree - 1.0) / ((degree - m_column) * (degree + m_column)))

    base_l = first_l.astype(jnp.float32)
    value_older = start_pair[0]
    value_newer = start_pair[1]
    prior_coef = recur_coef(base_l - 1.0)
    height_row = height[None, :]
    stacked_rows = []
    for offset in range(LBLK):
        present_coef = recur_coef(base_l + offset)
        value_now = present_coef * (height_row * value_newer - value_older / prior_coef)
        stacked_rows.append(value_now)
        value_older = value_newer
        value_newer = value_now
        prior_coef = present_coef
    return jnp.stack(stacked_rows, axis=1)


STEP_LANES = 1024
KDIM = 256
GAP = 8
RUN = 64
PACK = 8
WIDE = 256
START_GAP = 8


def sky_modes(totals, number_ref, sky_ref, first_ref, twice_ref, wave_ref, phase_ref, lhs_ref,
              rest_ref, rows_ref, me):
    maps, factor = totals
    low_len = wave_ref.shape[1]
    more = maps - 8
    for a in range(RES):
        values = sky_ref[0, :, a * low_len : (a + 1) * low_len].astype(jnp.float32)
        lhs_ref[a * 8 : a * 8 + 8, :] = values[:8]
        rest_ref[a * more : (a + 1) * more, :] = values[8:]
    rows_ref[...] = jnp.zeros_like(rows_ref)
    parity = (number_ref[me] - NSIDE + 1) % 2
    odd = jnp.full((MGRP, RES), parity, jnp.int32) == 1
    cosines = jnp.where(odd, phase_ref[:MGRP], 1.0)
    sines = jnp.where(odd, phase_ref[MGRP:], 0.0)
    none = jnp.zeros((8, RES), jnp.float32)
    for c in range(MGRP):
        real, imag, real_more, imag_more = none, none, none, none
        out = jnp.dot(
            lhs_ref[...].astype(jnp.bfloat16), wave_ref[c], preferred_element_type=jnp.float32
        )
        for a in range(RES):
            e_re, e_im = first_ref[a : a + 1, :RES], first_ref[a : a + 1, RES:]
            w_re, w_im = out[a * 8 : a * 8 + 8, :RES], out[a * 8 : a * 8 + 8, RES:]
            real = real + (e_re * w_re - e_im * w_im)
            imag = imag + (e_re * w_im + e_im * w_re)
        out = jnp.dot(
            rest_ref[...].astype(jnp.bfloat16), wave_ref[c], preferred_element_type=jnp.float32
        )
        for a in range(RES * more // 8):
            rows = slice(a * 8, a * 8 + 8)
            e_re, e_im = twice_ref[rows, :RES], twice_ref[rows, RES:]
            w_re, w_im = out[rows, :RES], out[rows, RES:]
            real_more = real_more + (e_re * w_re - e_im * w_im)
            imag_more = imag_more + (e_re * w_im + e_im * w_re)
        cos, sin = cosines[c : c + 1], sines[c : c + 1]
        row = c * 2 * maps
        for re, im, at, size in ((real, imag, 0, 8), (real_more, imag_more, 8, more)):
            if size != 8:
                re = sum(re[i : i + size] for i in range(0, 8, size))
                im = sum(im[i : i + size] for i in range(0, 8, size))
            first = row + at
            rows_ref[first : first + size, :] = factor * (cos * re + sin * im)
            rows_ref[first + maps : first + maps + size, :] = factor * (cos * im - sin * re)


def heights(number_ref, z_ref):
    lane = lax.broadcasted_iota(jnp.int32, z_ref.shape, 1) % number_ref.shape[0]
    numbers = jnp.zeros(z_ref.shape, jnp.int32)
    for r in range(number_ref.shape[0]):
        numbers = jnp.where(lane == r, number_ref[r], numbers)
    z_ref[...] = cycle_height(numbers)


def prepare(blk_total, scale, pieces_ref, scales_ref, p_ref):
    blocks = scales_ref.shape[0]
    local_cols = MGRP * RES // blk_total
    lane = lax.broadcasted_iota(jnp.int32, (blocks, 128), 1)
    column = lax.axis_index("blk") * local_cols + lane % local_cols
    m_row = (MSTART + RES * (column % MGRP) + column // MGRP).astype(jnp.float32)
    block = lax.broadcasted_iota(jnp.int32, (blocks, 128), 0)
    base = LSTART + (lax.axis_index("map") * blocks + block) * LBLK

    def setup(j, carry):
        p_prev, q_prev = carry
        degree = (base + j).astype(jnp.float32)
        num = 4.0 * degree * degree - 1.0
        den = (degree - m_row) * (degree + m_row)
        root = lax.rsqrt(num * den)
        kappa = p_prev * p_prev
        high = kappa.astype(jnp.bfloat16).astype(jnp.float32)
        rest = kappa - high
        mid = rest.astype(jnp.bfloat16).astype(jnp.float32)
        low = rest - mid
        rows = pl.ds(pl.multiple_of(j * blocks, blocks), blocks)
        pieces_ref[rows, :128] = jnp.where(lane < local_cols, high, mid).astype(jnp.bfloat16)
        pieces_ref[rows, 128:] = low.astype(jnp.bfloat16)
        p_now = num * root * q_prev
        q_now = den * root * p_prev
        for half in range(blocks // 8):
            p_ref[pl.ds(half * 8 * (LBLK + GAP) + j, 8, stride=LBLK + GAP), :] = p_now[
                half * 8 : half * 8 + 8
            ]
        return p_now, q_now

    one = jnp.ones((blocks, 128), jnp.float32)
    lax.fori_loop(0, LBLK, setup, (one, one), unroll=4)

    def turn(t, _):
        turned = p_ref[pl.ds(pl.multiple_of(t * (LBLK + GAP), 8), LBLK), :].T
        scales_ref[t] = turned[:local_cols] * scale
        return 0

    lax.fori_loop(0, blocks, turn, 0)


def start_values(starts_ref, turn_ref, init_ref):
    _, blocks, cycles, local_cols = starts_ref.shape
    lane = lax.broadcasted_iota(jnp.int32, (blocks, local_cols), 1)
    column = lax.axis_index("blk") * local_cols + lane
    m_row = (MSTART + RES * (column % MGRP) + column // MGRP).astype(jnp.float32)
    block = lax.broadcasted_iota(jnp.int32, (blocks, local_cols), 0)
    degree = (LSTART + (lax.axis_index("map") * blocks + block) * LBLK - 1).astype(jnp.float32)
    inverse = jnp.sqrt(((degree - m_row) * (degree + m_row)) / (4.0 * degree * degree - 1.0))
    pitch = local_cols + START_GAP
    for kind in range(2):
        for t in range(blocks):
            values = starts_ref[kind, t]
            if kind == 0:
                values = values * inverse[t : t + 1]
            turn_ref[kind, t * pitch : t * pitch + local_cols, :cycles] = values.T
    per_tile = 128 // cycles
    slot = lax.broadcasted_iota(jnp.int32, (8, 128), 1) // cycles
    for kind in range(2):
        for half in range(blocks // 8):
            for tile in range(local_cols // per_tile):
                row = None
                for i in range(per_tile):
                    first = half * 8 * pitch + tile * per_tile + i
                    part = turn_ref[kind, pl.ds(first, 8, stride=pitch), :]
                    if i == 0:
                        row = part
                    else:
                        row = jnp.where(slot == i, pltpu.roll(part, i * cycles, 1), row)
                init_ref[kind, half * 8 : half * 8 + 8, tile * 128 : tile * 128 + 128] = row


def recurrence(part, cycles, z_ref, pieces_ref, init_ref, leg_ref):
    blocks = init_ref.shape[1]
    halves = STEP_LANES // 128
    q_row = lax.broadcasted_iota(jnp.int32, (256, STEP_LANES), 0)
    q_lane = lax.broadcasted_iota(jnp.int32, (256, STEP_LANES), 1) // cycles + part * (
        STEP_LANES // cycles
    )
    spread = jnp.where((q_row % 64 == q_lane) & (q_row < 192), 1.0, 0.0).astype(jnp.bfloat16)

    def recur(i, carry):
        older, newer = carry
        rows = pl.ds(pl.multiple_of(i * RUN * blocks, RUN * blocks), RUN * blocks)
        kap = jnp.dot(pieces_ref[rows, :], spread, preferred_element_type=jnp.float32)
        for j in range(RUN):
            now = (kap[j * blocks : (j + 1) * blocks] * z_ref[...]) * newer - older
            for half in range(blocks // 8):
                at = pl.ds(half * 8 * (LBLK + GAP) + i * RUN + j, 8, stride=LBLK + GAP)
                for g in range(halves):
                    leg_ref[part * halves + g, at, :] = now[
                        half * 8 : half * 8 + 8, g * 128 : g * 128 + 128
                    ]
            older, newer = newer, now
        return older, newer

    lanes = slice(part * STEP_LANES, (part + 1) * STEP_LANES)
    lax.fori_loop(0, LBLK // RUN, recur, (init_ref[0, :, lanes], init_ref[1, :, lanes]))


def block_weights(maps, held_ref, weight_ref):
    groups, rows_all, _ = weight_ref.shape
    cycles, _, _ = held_ref.shape
    parts = 2 * maps
    q_group = rows_all // parts
    per_group = q_group // MGRP
    row = lax.broadcasted_iota(jnp.int32, (rows_all, per_group * 128), 0)
    lane = lax.broadcasted_iota(jnp.int32, (rows_all, per_group * 128), 1)
    q = row % q_group
    wanted = q // MGRP * 128 + (q % MGRP) * parts + row // q_group
    pick = jnp.where(lane == wanted, 1.0, 0.0).astype(jnp.bfloat16)
    row = lax.broadcasted_iota(jnp.int32, (rows_all, KDIM), 0)
    lane = lax.broadcasted_iota(jnp.int32, (rows_all, KDIM), 1)
    same_q = row % q_group == lane // cycles
    modes = jnp.swapaxes(held_ref[...].astype(jnp.float32), 0, 1).astype(jnp.bfloat16)
    for g in range(groups):
        own = jnp.concatenate([modes[g * per_group + k] for k in range(per_group)], axis=1)
        wide = lax.dot_general(
            pick, jnp.concatenate([own] * q_group, axis=0), (((1,), (1,)), ((), ())),
            preferred_element_type=jnp.float32,
        )
        weight_ref[g] = jnp.where(same_q, wide, 0.0).astype(jnp.bfloat16)


def project_tiles(u, maps, share, leg_ref, scales_ref, weight_ref, harm_ref, near_ref):
    groups, rows_all, _ = weight_ref.shape
    parts = 2 * maps
    q_group = rows_all // parts
    width = 2 * LBLK

    def tile(piece, g):
        first_t = u * (share // LBLK) + 2 * piece
        cols = pl.ds(pl.multiple_of(u * share + piece * width, width), width)
        sources = [
            pl.ds(pl.multiple_of((first_t + x) * (LBLK + GAP), 8), LBLK) for x in range(2)
        ]
        rows = slice(g * q_group, (g + 1) * q_group)
        p_rows = jnp.concatenate([scales_ref[first_t + x, rows, :] for x in range(2)], axis=1)
        leg = jnp.concatenate(
            [
                jnp.concatenate(
                    [leg_ref[g * (KDIM // 128) + h, src, :] for h in range(KDIM // 128)], axis=1
                )
                for src in sources
            ],
            axis=0,
        ).astype(jnp.bfloat16)
        out = lax.dot_general(
            weight_ref[g], leg, (((1,), (1,)), ((), ())), preferred_element_type=jnp.float32
        )
        crossed = (out.reshape(parts, q_group, width) * p_rows[None]).astype(jnp.bfloat16)
        harm_ref[:, rows, cols] = crossed
        near_ref[:, rows, piece * width : (piece + 1) * width] = crossed

    return [
        functools.partial(tile, piece, g) for piece in range(share // width) for g in range(groups)
    ]


def product_steps(maps, share, near_ref, sums_ref):
    local_cols = near_ref.shape[1]
    pairs = [(i, k) for i in range(maps) for k in range(i, maps)]
    middle = maps // 2
    sets = [
        [p for p, (i, k) in enumerate(pairs) if k < middle],
        [p for p, (i, k) in enumerate(pairs) if i >= middle],
        [p for p, (i, k) in enumerate(pairs) if i < middle <= k],
    ]

    def some(piece, chosen):
        cols = slice(piece * WIDE, (piece + 1) * WIDE)
        total = {}
        for h in range(2):
            for t in range(local_cols // PACK):
                x = {}
                for n in sorted({v for p in chosen for v in pairs[p]}):
                    x[n] = near_ref[h * maps + n, t * PACK : (t + 1) * PACK, cols]
                for p in chosen:
                    i, k = pairs[p]
                    term = x[i] * x[k]
                    total[p] = term if p not in total else total[p] + term
        for p in chosen:
            sums_ref[p * PACK : (p + 1) * PACK, cols] = total[p]

    return [
        functools.partial(some, piece, chosen)
        for piece in range(share // WIDE)
        for chosen in sets
    ]


def interleave(one, other):
    for i in range(max(len(one), len(other))):
        for steps in (one, other):
            if i < len(steps):
                steps[i]()


def whole_kernel(
    dims, number_hbm, sky_hbm, starts_hbm, first_hbm, twice_hbm, wave_hbm, phase_hbm,
    harm_ref, out_ref,
    number_ref, sky_ref, starts_ref, first_ref, twice_ref, wave_ref, phase_ref,
    lhs_ref, rest_ref, rows_ref, turned_ref, held_ref, pieces_ref, scales_ref, z_ref, p_ref,
    turn_ref, init_ref, leg_ref, weight_ref, near_a, near_b, sums_ref, part_ref, other_ref,
    load_sem, send_sem, recv_sem, part_send, part_recv,
):
    blk_total, map_total, maps, factor, scale = dims
    count = blk_total * map_total
    cycles = number_hbm.shape[0]
    share = out_ref.shape[1]
    me_blk, me_map = lax.axis_index("blk"), lax.axis_index("map")
    me = me_blk * map_total + me_map
    k_share = RES // blk_total
    fetched = [
        pltpu.make_async_copy(source, target, load_sem.at[i])
        for i, (source, target) in enumerate(
            [
                (sky_hbm, sky_ref), (wave_hbm, wave_ref), (first_hbm, first_ref),
                (twice_hbm, twice_ref),
                (phase_hbm, phase_ref), (number_hbm, number_ref), (starts_hbm, starts_ref),
            ]
        )
    ]
    for copy in fetched:
        copy.start()
    barrier = pltpu.get_barrier_semaphore()
    for i in range(1, count):
        peer = lax.rem(me + i, count)
        pl.semaphore_signal(
            barrier, inc=1,
            device_id={"blk": peer // map_total, "map": lax.rem(peer, map_total)},
            device_id_type=pl.DeviceIdType.MESH,
        )
    prepare(blk_total, scale, pieces_ref, scales_ref, p_ref)
    for copy in fetched[:-1]:
        copy.wait()
    sky_modes(
        (maps, factor), number_ref, sky_ref, first_ref, twice_ref, wave_ref, phase_ref, lhs_ref,
        rest_ref, rows_ref, me,
    )
    turned_ref[...] = rows_ref[...].T.astype(jnp.bfloat16)
    pl.semaphore_wait(barrier, count - 1)

    def modes_to(peer, source):
        target_blk = peer // map_total
        return pltpu.make_async_remote_copy(
            src_ref=turned_ref.at[pl.ds(pl.multiple_of(target_blk * k_share, k_share), k_share)],
            dst_ref=held_ref.at[source],
            send_sem=send_sem.at[peer],
            recv_sem=recv_sem.at[source],
            device_id={"blk": target_blk, "map": lax.rem(peer, map_total)},
            device_id_type=pl.DeviceIdType.MESH,
        )

    for i in range(1, count):
        modes_to(lax.rem(me + i, count), me).start()
    held_ref[me] = turned_ref[pl.ds(pl.multiple_of(me_blk * k_share, k_share), k_share), :]

    heights(number_ref, z_ref)
    fetched[-1].wait()
    start_values(starts_ref, turn_ref, init_ref)
    for part in range(init_ref.shape[2] // STEP_LANES):
        recurrence(part, cycles, z_ref, pieces_ref, init_ref, leg_ref)

    for i in range(1, count):
        peer = lax.rem(me + i, count)
        modes_to(peer, peer).wait_recv()
    block_weights(maps, held_ref, weight_ref)

    pairs = maps * (maps + 1) // 2
    pair_rows = part_ref.shape[1]
    row = lax.broadcasted_iota(jnp.int32, (pair_rows, pair_rows * PACK), 0)
    lane = lax.broadcasted_iota(jnp.int32, (pair_rows, pair_rows * PACK), 1)
    gather = jnp.where(lane // PACK == row, 1.0, 0.0).astype(jnp.bfloat16)
    for p in range(pairs, pair_rows):
        sums_ref[p * PACK : (p + 1) * PACK, :] = jnp.zeros((PACK, share), jnp.bfloat16)

    def part_to(peer, source):
        return pltpu.make_async_remote_copy(
            src_ref=part_ref.at[peer],
            dst_ref=other_ref.at[source],
            send_sem=part_send.at[peer],
            recv_sem=part_recv.at[source],
            device_id={"blk": peer},
            device_id_type=pl.DeviceIdType.MESH,
        )

    def project(s, near_ref):
        u = lax.rem(me_blk + s, blk_total)
        return project_tiles(u, maps, share, leg_ref, scales_ref, weight_ref, harm_ref, near_ref)

    def finish(s):
        u = lax.rem(me_blk + s, blk_total)
        part_ref[u] = jnp.dot(
            gather, sums_ref[...], preferred_element_type=jnp.float32
        ).astype(jnp.bfloat16)
        return u

    def two_shares(i, _):
        for now, near_ref, next_ref in ((2 * i + 1, near_a, near_b), (2 * i + 2, near_b, near_a)):
            interleave(
                product_steps(maps, share, near_ref, sums_ref), project(now + 1, next_ref)
            )
            part_to(finish(now), me_blk).start()
        return 0

    interleave(project(1, near_a), [])
    lax.fori_loop(0, blk_total // 2 - 1, two_shares, 0)
    interleave(product_steps(maps, share, near_a, sums_ref), [])
    part_to(finish(blk_total - 1), me_blk).start()
    interleave(project(blk_total, near_b), [])
    interleave(product_steps(maps, share, near_b, sums_ref), [])
    finish(blk_total)
    out_rows = maps * maps
    row = lax.broadcasted_iota(jnp.int32, (out_rows, pair_rows), 0)
    lane = lax.broadcasted_iota(jnp.int32, (out_rows, pair_rows), 1)
    low = jnp.minimum(row // maps, row % maps)
    high = jnp.maximum(row // maps, row % maps)
    pair_at = low * maps - low * (low - 1) // 2 + high - low
    unfold = jnp.where(lane == pair_at, 1.0, 0.0).astype(jnp.bfloat16)
    unfolded = lambda x: jnp.dot(unfold, x, preferred_element_type=jnp.float32)
    total = unfolded(part_ref[me_blk])
    for i in range(1, blk_total):
        peer = lax.rem(me_blk + blk_total - i, blk_total)
        part_to(peer, peer).wait_recv()
        total = total + unfolded(other_ref[peer])
    out_ref[...] = total * (1.0 / (MGRP * RES))
    for i in range(1, count):
        modes_to(lax.rem(me + i, count), me).wait_send()
    for i in range(1, blk_total):
        part_to(lax.rem(me_blk + i, blk_total), me_blk).wait_send()


def constant_tables(cycle_len, maps):
    low_len = cycle_len // RES
    residue = np.arange(RES)
    angle = np.float32(2.0 * math.pi / RES) * (
        residue[:, None] * residue[None, :] % RES
    ).astype(np.float32)
    first = np.concatenate([np.cos(angle), -np.sin(angle)], axis=1)
    first = first.astype(jnp.bfloat16).astype(np.float32)
    m_value = MSTART + RES * np.arange(MGRP)[:, None, None] + residue[None, None, :]
    turn = m_value * np.arange(low_len)[None, :, None] % cycle_len
    angle = np.float32(2.0 * math.pi / cycle_len) * turn.astype(np.float32)
    wave = np.concatenate([np.cos(angle), -np.sin(angle)], axis=2).astype(jnp.bfloat16)
    m_value = MSTART + np.arange(MGRP)[:, None] * RES + np.arange(RES)[None, :]
    angle = np.float32(math.pi / cycle_len) * (m_value % (2 * cycle_len)).astype(np.float32)
    phase = np.concatenate([np.cos(angle), np.sin(angle)], axis=0)
    twice = np.repeat(first, maps - 8, axis=0)
    return jnp.asarray(first), jnp.asarray(twice), jnp.asarray(wave), jnp.asarray(phase)


def kernel_fits(own_cycles, blk_total, cycles, maps_count, block_count):
    local_cols = MGRP * RES // blk_total
    return (
        own_cycles == 1
        and blk_total % 2 == 0
        and maps_count in (9, 10, 12)
        and local_cols == 64
        and KDIM % cycles == 0
        and KDIM // cycles == 8
        and 2 * maps_count * MGRP <= 128
        and block_count % 8 == 0
        and block_count % blk_total == 0
        and (block_count * LBLK // blk_total) % (2 * LBLK) == 0
    )


def fast_body(sky_maps, cycle_number, legendre_starts):
    _, maps, cycle_len = sky_maps.shape
    map_total = lax.axis_size("map")
    blk_total = lax.axis_size("blk")
    local_cols, blocks, cycles = legendre_starts.shape[1:]
    count = blk_total * map_total
    local_len = blocks * LBLK
    share = local_len // blk_total
    parts = 2 * maps
    q_group = KDIM // cycles
    lanes = local_cols * cycles
    pair_rows = -(-(maps * (maps + 1) // 2) // 8) * 8
    tables = constant_tables(cycle_len, maps)
    starts = jnp.transpose(legendre_starts, (0, 2, 3, 1))
    dims = (blk_total, map_total, maps, 1.0 / math.sqrt(cycle_len), 1.0 / math.sqrt(cycles))
    vmem = pl.BlockSpec(memory_space=pltpu.VMEM)
    pitch = LBLK + GAP
    harmonics, spectra = pl.pallas_call(
        functools.partial(whole_kernel, dims),
        out_shape=(
            pltpu.VMEM((parts, local_cols, local_len), jnp.bfloat16),
            pltpu.VMEM((maps * maps, share), jnp.float32),
        ),
        in_specs=[pl.BlockSpec(memory_space=pl.ANY)] * 7,
        out_specs=(vmem, vmem),
        scratch_shapes=[pltpu.SMEM(cycle_number.shape, jnp.int32)]
        + [pltpu.VMEM(x.shape, x.dtype) for x in (sky_maps, starts, *tables)]
        + [
            pltpu.VMEM((RES * 8, cycle_len // RES), jnp.float32),
            pltpu.VMEM((RES * (maps - 8), cycle_len // RES), jnp.float32),
            pltpu.VMEM((128, RES), jnp.float32),
            pltpu.VMEM((RES, 128), jnp.bfloat16),
            pltpu.VMEM((count, RES // blk_total, 128), jnp.bfloat16),
            pltpu.VMEM((local_len, 256), jnp.bfloat16),
            pltpu.VMEM((blocks, local_cols, LBLK), jnp.float32),
            pltpu.VMEM((1, STEP_LANES), jnp.float32),
            pltpu.VMEM((blocks * pitch, 128), jnp.float32),
            pltpu.VMEM((2, blocks * (local_cols + START_GAP), 128), jnp.float32),
            pltpu.VMEM((2, blocks, lanes), jnp.float32),
            pltpu.VMEM((lanes // 128, blocks * pitch, 128), jnp.float32),
            pltpu.VMEM((local_cols // q_group, parts * q_group, KDIM), jnp.bfloat16),
            pltpu.VMEM((parts, local_cols, share), jnp.bfloat16),
            pltpu.VMEM((parts, local_cols, share), jnp.bfloat16),
            pltpu.VMEM((pair_rows * PACK, share), jnp.bfloat16),
            pltpu.VMEM((blk_total, pair_rows, share), jnp.bfloat16),
            pltpu.VMEM((blk_total, pair_rows, share), jnp.bfloat16),
            pltpu.SemaphoreType.DMA((7,)),
            pltpu.SemaphoreType.DMA((count,)),
            pltpu.SemaphoreType.DMA((count,)),
            pltpu.SemaphoreType.DMA((blk_total,)),
            pltpu.SemaphoreType.DMA((blk_total,)),
        ],
        compiler_params=pltpu.CompilerParams(
            collective_id=0, has_side_effects=True, vmem_limit_bytes=48 * 1024 * 1024
        ),
    )(
        *(
            pltpu.with_memory_space_constraint(x, pltpu.HBM)
            for x in (cycle_number, sky_maps, starts, *tables)
        )
    )
    harmonics, spectra = write_out(harmonics, spectra, maps)
    return (jnp.transpose(harmonics, (1, 0, 2)), jnp.transpose(spectra, (2, 0, 1, 3)))


def write_kernel(maps, harm_ref, sums_ref, harm_out, spectra_out, spectra_ref, sem, spectra_sem):
    pieces = sem.shape[0]
    rows = harm_ref.shape[0] // pieces
    copies = [
        pltpu.make_async_copy(
            harm_ref.at[pl.ds(i * rows, rows)], harm_out.at[pl.ds(i * rows, rows)], sem.at[i]
        )
        for i in range(pieces)
    ]
    for copy in copies:
        copy.start()
    for i in range(maps):
        for k in range(maps):
            spectra_ref[i, k] = sums_ref[i * maps + k : i * maps + k + 1]
    last = pltpu.make_async_copy(spectra_ref, spectra_out, spectra_sem)
    last.start()
    for copy in copies:
        copy.wait()
    last.wait()


def write_out(harmonics, spectra, maps):
    vmem = pl.BlockSpec(memory_space=pltpu.VMEM)
    shape = (maps, maps, 1, spectra.shape[1])
    return pl.pallas_call(
        functools.partial(write_kernel, maps),
        out_shape=(
            jax.ShapeDtypeStruct(harmonics.shape, harmonics.dtype),
            jax.ShapeDtypeStruct(shape, jnp.float32),
        ),
        in_specs=[vmem, vmem],
        out_specs=(pl.BlockSpec(memory_space=pl.ANY),) * 2,
        scratch_shapes=[
            pltpu.VMEM(shape, jnp.float32),
            pltpu.SemaphoreType.DMA((2,)),
            pltpu.SemaphoreType.DMA,
        ],
        compiler_params=pltpu.CompilerParams(vmem_limit_bytes=8 * 1024 * 1024),
    )(harmonics, spectra)


def body(sky_maps, cycle_number, legendre_starts):
    own_cycles, maps_count, cycle_len = sky_maps.shape
    map_total = lax.axis_size("map")
    blk_total = lax.axis_size("blk")
    cycles, block_count = cycle_number.shape[0], legendre_starts.shape[2]
    if kernel_fits(own_cycles, blk_total, cycles, maps_count, block_count):
        return fast_body(sky_maps, cycle_number, legendre_starts)
    tables = dft_tables(cycle_len)
    first_row = (lax.axis_index("blk") * map_total + lax.axis_index("map")) * own_cycles
    own_numbers = lax.dynamic_slice_in_dim(cycle_number, first_row, own_cycles)
    parity = (own_numbers - NSIDE + 1) % 2
    local_modes = cycle_transform(sky_maps, parity, tables)
    grouped = lax.all_gather(local_modes, "map", axis=0, tiled=True)
    regrouped = lax.all_to_all(grouped, "blk", split_axis=4, concat_axis=0, tiled=True)
    ordered = jnp.transpose(regrouped, (4, 3, 1, 2, 0))
    local_cols = ordered.shape[0] * ordered.shape[1]
    cycle_modes = ordered.reshape(local_cols, 2 * maps_count, -1)
    heights = cycle_height(cycle_number)
    column = lax.axis_index("blk") * local_cols + jnp.arange(local_cols, dtype=jnp.int32)
    m_float = (MSTART + RES * (column % MGRP) + column // MGRP).astype(jnp.float32)
    block_count = legendre_starts.shape[2]
    local_len = block_count * LBLK
    first_l = LSTART + lax.axis_index("map") * local_len
    cycle_scale = 1.0 / math.sqrt(cycle_modes.shape[-1])

    def one_block(block_index):
        start_pair = lax.dynamic_index_in_dim(legendre_starts, block_index, 2, keepdims=False)
        legendre_tile = legendre_rows(
            start_pair, heights, m_float, first_l + block_index * LBLK
        ).astype(jnp.bfloat16)
        projected = (
            jnp.einsum(
                "qlr,qnr->qnl", legendre_tile, cycle_modes, preferred_element_type=jnp.float32
            )
            * cycle_scale
        )
        return projected.astype(jnp.bfloat16)

    blocks_out = lax.map(one_block, jnp.arange(block_count, dtype=jnp.int32))
    harmonics = jnp.transpose(blocks_out, (1, 2, 0, 3)).reshape(
        local_cols, 2 * maps_count, local_len
    )
    total_cols = MGRP * RES
    spread = harmonics.reshape(local_cols, 2 * maps_count, blk_total, local_len // blk_total)
    spread = jnp.transpose(spread, (2, 3, 1, 0))
    received = lax.all_to_all(
        shortened(spread), "blk", split_axis=0, concat_axis=3, tiled=True
    ).astype(spread.dtype)
    item_count = received.shape[1]
    split_piece = received.reshape(item_count, 2, maps_count, received.shape[3])
    cross_sum = jnp.einsum(
        "gciq,gcjq->ijg", split_piece, split_piece, preferred_element_type=jnp.float32
    )
    owned = (cross_sum / total_cols)[None]
    return (harmonics, owned)


def solution(mesh):
    return jax.shard_map(
        body,
        mesh=mesh,
        in_specs=(P(("blk", "map"), None, None), P(), P(None, "blk", "map", None)),
        out_specs=(P("blk", None, "map"), P("map", None, None, "blk")),
        check_vma=False,
    )
```

```python
import functools
import math

import jax
import jax.numpy as jnp
import numpy as np
from jax import lax
from jax.experimental import pallas as pl
from jax.experimental.pallas import tpu as pltpu
from jax.sharding import PartitionSpec as P

NSIDE = 8192
RES = 128
MGRP = 4
MSTART = 4096
LSTART = 8192
LBLK = 128


def shortened(array):

    def short(part):
        return part.astype(jnp.bfloat16) if part.dtype == jnp.float32 else part

    return jax.tree.map(short, array)


def cycle_height(cycle_ids):
    return (4.0 * NSIDE - 2.0 * cycle_ids.astype(jnp.float32)) / (3.0 * NSIDE)


def dft_tables(cycle_len):
    low_len = cycle_len // RES
    residue = jnp.arange(RES, dtype=jnp.int32)
    turn_one = residue[:, None] * residue[None, :] % RES
    angle_one = 2.0 * math.pi / RES * turn_one.astype(jnp.float32)
    first_table = jnp.concatenate([jnp.cos(angle_one), -jnp.sin(angle_one)], axis=1).astype(
        jnp.bfloat16
    )
    column_group = jnp.arange(MGRP, dtype=jnp.int32)
    sample = jnp.arange(low_len, dtype=jnp.int32)
    m_value = MSTART + RES * column_group[:, None, None] + residue[None, None, :]
    turn_two = m_value * sample[None, :, None] % cycle_len
    angle_two = 2.0 * math.pi / cycle_len * turn_two.astype(jnp.float32)
    twiddle_re = jnp.cos(angle_two).astype(jnp.bfloat16)
    twiddle_im = (-jnp.sin(angle_two)).astype(jnp.bfloat16)
    return (first_table, twiddle_re, twiddle_im)


def cycle_transform(cycle_rows, parity, tables):
    first_table, twiddle_re, twiddle_im = tables
    cycle_count, maps_count, cycle_len = cycle_rows.shape
    low_len = cycle_len // RES
    folded = cycle_rows.reshape(cycle_count, maps_count, RES, low_len)
    section_one = jnp.einsum(
        "rnaj,ak->rnjk", folded, first_table, preferred_element_type=jnp.float32
    )
    section_one = section_one.astype(jnp.bfloat16)
    part_re = section_one[..., :RES]
    part_im = section_one[..., RES:]
    real_sum = jnp.einsum(
        "rnjk,cjk->rnck", part_re, twiddle_re, preferred_element_type=jnp.float32
    ) - jnp.einsum("rnjk,cjk->rnck", part_im, twiddle_im, preferred_element_type=jnp.float32)
    imag_sum = jnp.einsum(
        "rnjk,cjk->rnck", part_im, twiddle_re, preferred_element_type=jnp.float32
    ) + jnp.einsum("rnjk,cjk->rnck", part_re, twiddle_im, preferred_element_type=jnp.float32)
    column_group = jnp.arange(MGRP, dtype=jnp.int32)
    residue = jnp.arange(RES, dtype=jnp.int32)
    m_value = MSTART + RES * column_group[:, None] + residue[None, :]
    shifted = m_value[None, :, :] * parity[:, None, None] % (2 * cycle_len)
    phase_angle = math.pi / cycle_len * shifted.astype(jnp.float32)
    cos_part = jnp.cos(phase_angle)[:, None]
    sin_part = jnp.sin(phase_angle)[:, None]
    factor = 1.0 / math.sqrt(cycle_len)
    out_re = factor * (cos_part * real_sum + sin_part * imag_sum)
    out_im = factor * (cos_part * imag_sum - sin_part * real_sum)
    return jnp.stack([out_re, out_im], axis=1).astype(jnp.bfloat16)


def legendre_rows(start_pair, height, m_float, first_l):
    m_column = m_float[:, None]

    def recur_coef(degree):
        return jnp.sqrt((4.0 * degree * degree - 1.0) / ((degree - m_column) * (degree + m_column)))

    base_l = first_l.astype(jnp.float32)
    value_older = start_pair[0]
    value_newer = start_pair[1]
    prior_coef = recur_coef(base_l - 1.0)
    height_row = height[None, :]
    stacked_rows = []
    for offset in range(LBLK):
        present_coef = recur_coef(base_l + offset)
        value_now = present_coef * (height_row * value_newer - value_older / prior_coef)
        stacked_rows.append(value_now)
        value_older = value_newer
        value_newer = value_now
        prior_coef = present_coef
    return jnp.stack(stacked_rows, axis=1)


STEP_LANES = 1024
KDIM = 256
GAP = 8
RUN = 64
PACK = 8
WIDE = 256
START_GAP = 8


def sky_modes(totals, number_ref, sky_ref, first_ref, twice_ref, wave_ref, phase_ref, lhs_ref,
              rest_ref, rows_ref, me):
    maps, factor = totals
    low_len = wave_ref.shape[1]
    more = maps - 8
    for a in range(RES):
        values = sky_ref[0, :, a * low_len : (a + 1) * low_len].astype(jnp.float32)
        lhs_ref[a * 8 : a * 8 + 8, :] = values[:8]
        rest_ref[a * more : (a + 1) * more, :] = values[8:]
    rows_ref[...] = jnp.zeros_like(rows_ref)
    parity = (number_ref[me] - NSIDE + 1) % 2
    odd = jnp.full((MGRP, RES), parity, jnp.int32) == 1
    cosines = jnp.where(odd, phase_ref[:MGRP], 1.0)
    sines = jnp.where(odd, phase_ref[MGRP:], 0.0)
    none = jnp.zeros((8, RES), jnp.float32)
    for c in range(MGRP):
        real, imag, real_more, imag_more = none, none, none, none
        out = jnp.dot(
            lhs_ref[...].astype(jnp.bfloat16), wave_ref[c], preferred_element_type=jnp.float32
        )
        for a in range(RES):
            e_re, e_im = first_ref[a : a + 1, :RES], first_ref[a : a + 1, RES:]
            w_re, w_im = out[a * 8 : a * 8 + 8, :RES], out[a * 8 : a * 8 + 8, RES:]
            real = real + (e_re * w_re - e_im * w_im)
            imag = imag + (e_re * w_im + e_im * w_re)
        out = jnp.dot(
            rest_ref[...].astype(jnp.bfloat16), wave_ref[c], preferred_element_type=jnp.float32
        )
        for a in range(RES * more // 8):
            rows = slice(a * 8, a * 8 + 8)
            e_re, e_im = twice_ref[rows, :RES], twice_ref[rows, RES:]
            w_re, w_im = out[rows, :RES], out[rows, RES:]
            real_more = real_more + (e_re * w_re - e_im * w_im)
            imag_more = imag_more + (e_re * w_im + e_im * w_re)
        cos, sin = cosines[c : c + 1], sines[c : c + 1]
        row = c * 2 * maps
        for re, im, at, size in ((real, imag, 0, 8), (real_more, imag_more, 8, more)):
            if size != 8:
                re = sum(re[i : i + size] for i in range(0, 8, size))
                im = sum(im[i : i + size] for i in range(0, 8, size))
            first = row + at
            rows_ref[first : first + size, :] = factor * (cos * re + sin * im)
            rows_ref[first + maps : first + maps + size, :] = factor * (cos * im - sin * re)


def heights(number_ref, z_ref):
    lane = lax.broadcasted_iota(jnp.int32, z_ref.shape, 1) % number_ref.shape[0]
    numbers = jnp.zeros(z_ref.shape, jnp.int32)
    for r in range(number_ref.shape[0]):
        numbers = jnp.where(lane == r, number_ref[r], numbers)
    z_ref[...] = cycle_height(numbers)


def prepare(blk_total, blocks, pieces_ref, p_ref):
    local_cols = MGRP * RES // blk_total
    lane = lax.broadcasted_iota(jnp.int32, (blocks, 128), 1)
    column = lax.axis_index("blk") * local_cols + lane % local_cols
    m_row = (MSTART + RES * (column % MGRP) + column // MGRP).astype(jnp.float32)
    block = lax.broadcasted_iota(jnp.int32, (blocks, 128), 0)
    base = LSTART + (lax.axis_index("map") * blocks + block) * LBLK

    def setup(j, carry):
        p_prev, q_prev = carry
        degree = (base + j).astype(jnp.float32)
        num = 4.0 * degree * degree - 1.0
        den = (degree - m_row) * (degree + m_row)
        root = lax.rsqrt(num * den)
        kappa = p_prev * p_prev
        high = kappa.astype(jnp.bfloat16).astype(jnp.float32)
        rest = kappa - high
        mid = rest.astype(jnp.bfloat16).astype(jnp.float32)
        low = rest - mid
        rows = pl.ds(pl.multiple_of(j * blocks, blocks), blocks)
        pieces_ref[rows, :128] = jnp.where(lane < local_cols, high, mid).astype(jnp.bfloat16)
        pieces_ref[rows, 128:] = low.astype(jnp.bfloat16)
        p_now = num * root * q_prev
        q_now = den * root * p_prev
        for half in range(blocks // 8):
            p_ref[pl.ds(half * 8 * (LBLK + GAP) + j, 8, stride=LBLK + GAP), :] = p_now[
                half * 8 : half * 8 + 8
            ]
        return p_now, q_now

    one = jnp.ones((blocks, 128), jnp.float32)
    lax.fori_loop(0, LBLK, setup, (one, one), unroll=4)


def turn_factors(scale, scales_ref, p_ref):
    blocks, local_cols, _ = scales_ref.shape

    def turn(t, _):
        turned = p_ref[pl.ds(pl.multiple_of(t * (LBLK + GAP), 8), LBLK), :].T
        scales_ref[t] = turned[:local_cols] * scale
        return 0

    lax.fori_loop(0, blocks, turn, 0)


def start_values(starts_ref, turn_ref, init_ref):
    _, blocks, cycles, local_cols = starts_ref.shape
    lane = lax.broadcasted_iota(jnp.int32, (blocks, local_cols), 1)
    column = lax.axis_index("blk") * local_cols + lane
    m_row = (MSTART + RES * (column % MGRP) + column // MGRP).astype(jnp.float32)
    block = lax.broadcasted_iota(jnp.int32, (blocks, local_cols), 0)
    degree = (LSTART + (lax.axis_index("map") * blocks + block) * LBLK - 1).astype(jnp.float32)
    inverse = jnp.sqrt(((degree - m_row) * (degree + m_row)) / (4.0 * degree * degree - 1.0))
    pitch = local_cols + START_GAP
    for kind in range(2):
        for t in range(blocks):
            values = starts_ref[kind, t]
            if kind == 0:
                values = values * inverse[t : t + 1]
            turn_ref[kind, t * pitch : t * pitch + local_cols, :cycles] = values.T
    per_tile = 128 // cycles
    slot = lax.broadcasted_iota(jnp.int32, (8, 128), 1) // cycles
    for kind in range(2):
        for half in range(blocks // 8):
            for tile in range(local_cols // per_tile):
                row = None
                for i in range(per_tile):
                    first = half * 8 * pitch + tile * per_tile + i
                    part = turn_ref[kind, pl.ds(first, 8, stride=pitch), :]
                    if i == 0:
                        row = part
                    else:
                        row = jnp.where(slot == i, pltpu.roll(part, i * cycles, 1), row)
                init_ref[kind, half * 8 : half * 8 + 8, tile * 128 : tile * 128 + 128] = row


def recurrence(part, cycles, z_ref, pieces_ref, init_ref, leg_ref):
    blocks = init_ref.shape[1]
    halves = STEP_LANES // 128
    q_row = lax.broadcasted_iota(jnp.int32, (256, STEP_LANES), 0)
    q_lane = lax.broadcasted_iota(jnp.int32, (256, STEP_LANES), 1) // cycles + part * (
        STEP_LANES // cycles
    )
    spread = jnp.where((q_row % 64 == q_lane) & (q_row < 192), 1.0, 0.0).astype(jnp.bfloat16)

    def recur(i, carry):
        older, newer = carry
        rows = pl.ds(pl.multiple_of(i * RUN * blocks, RUN * blocks), RUN * blocks)
        kap = jnp.dot(pieces_ref[rows, :], spread, preferred_element_type=jnp.float32)
        for j in range(RUN):
            now = (kap[j * blocks : (j + 1) * blocks] * z_ref[...]) * newer - older
            for half in range(blocks // 8):
                at = pl.ds(half * 8 * (LBLK + GAP) + i * RUN + j, 8, stride=LBLK + GAP)
                for g in range(halves):
                    leg_ref[part * halves + g, at, :] = now[
                        half * 8 : half * 8 + 8, g * 128 : g * 128 + 128
                    ]
            older, newer = newer, now
        return older, newer

    lanes = slice(part * STEP_LANES, (part + 1) * STEP_LANES)
    lax.fori_loop(0, LBLK // RUN, recur, (init_ref[0, :, lanes], init_ref[1, :, lanes]))


def block_weights(maps, held_ref, weight_ref):
    groups, rows_all, _ = weight_ref.shape
    cycles, _, _ = held_ref.shape
    parts = 2 * maps
    q_group = rows_all // parts
    per_group = q_group // MGRP
    row = lax.broadcasted_iota(jnp.int32, (rows_all, per_group * 128), 0)
    lane = lax.broadcasted_iota(jnp.int32, (rows_all, per_group * 128), 1)
    q = row % q_group
    wanted = q // MGRP * 128 + (q % MGRP) * parts + row // q_group
    pick = jnp.where(lane == wanted, 1.0, 0.0).astype(jnp.bfloat16)
    row = lax.broadcasted_iota(jnp.int32, (rows_all, KDIM), 0)
    lane = lax.broadcasted_iota(jnp.int32, (rows_all, KDIM), 1)
    same_q = row % q_group == lane // cycles
    modes = jnp.swapaxes(held_ref[...].astype(jnp.float32), 0, 1).astype(jnp.bfloat16)
    for g in range(groups):
        own = jnp.concatenate([modes[g * per_group + k] for k in range(per_group)], axis=1)
        wide = lax.dot_general(
            pick, jnp.concatenate([own] * q_group, axis=0), (((1,), (1,)), ((), ())),
            preferred_element_type=jnp.float32,
        )
        weight_ref[g] = jnp.where(same_q, wide, 0.0).astype(jnp.bfloat16)


def project_tiles(u, maps, share, leg_ref, scales_ref, weight_ref, harm_ref, near_ref):
    groups, rows_all, _ = weight_ref.shape
    parts = 2 * maps
    q_group = rows_all // parts
    width = 2 * LBLK

    def tile(piece, g):
        first_t = u * (share // LBLK) + 2 * piece
        cols = pl.ds(pl.multiple_of(u * share + piece * width, width), width)
        sources = [
            pl.ds(pl.multiple_of((first_t + x) * (LBLK + GAP), 8), LBLK) for x in range(2)
        ]
        rows = slice(g * q_group, (g + 1) * q_group)
        p_rows = jnp.concatenate([scales_ref[first_t + x, rows, :] for x in range(2)], axis=1)
        leg = jnp.concatenate(
            [
                jnp.concatenate(
                    [leg_ref[g * (KDIM // 128) + h, src, :] for h in range(KDIM // 128)], axis=1
                )
                for src in sources
            ],
            axis=0,
        ).astype(jnp.bfloat16)
        out = lax.dot_general(
            weight_ref[g], leg, (((1,), (1,)), ((), ())), preferred_element_type=jnp.float32
        )
        crossed = (out.reshape(parts, q_group, width) * p_rows[None]).astype(jnp.bfloat16)
        harm_ref[:, rows, cols] = crossed
        near_ref[:, rows, piece * width : (piece + 1) * width] = crossed

    return [
        functools.partial(tile, piece, g) for piece in range(share // width) for g in range(groups)
    ]


def product_steps(maps, share, near_ref, sums_ref):
    local_cols = near_ref.shape[1]
    pairs = [(i, k) for i in range(maps) for k in range(i, maps)]
    middle = maps // 2
    sets = [
        [p for p, (i, k) in enumerate(pairs) if k < middle],
        [p for p, (i, k) in enumerate(pairs) if i >= middle],
        [p for p, (i, k) in enumerate(pairs) if i < middle <= k],
    ]

    def some(piece, chosen):
        cols = slice(piece * WIDE, (piece + 1) * WIDE)
        total = {}
        for h in range(2):
            for t in range(local_cols // PACK):
                x = {}
                for n in sorted({v for p in chosen for v in pairs[p]}):
                    x[n] = near_ref[h * maps + n, t * PACK : (t + 1) * PACK, cols]
                for p in chosen:
                    i, k = pairs[p]
                    term = x[i] * x[k]
                    total[p] = term if p not in total else total[p] + term
        for p in chosen:
            sums_ref[p * PACK : (p + 1) * PACK, cols] = total[p]

    return [
        functools.partial(some, piece, chosen)
        for piece in range(share // WIDE)
        for chosen in sets
    ]


def interleave(one, other):
    for i in range(max(len(one), len(other))):
        for steps in (one, other):
            if i < len(steps):
                steps[i]()


def wrapped(index, total):
    return jnp.where(index >= total, index - total, index)


def visit(me_blk, i, inner, blk_total):
    half = blk_total // 2
    outer, side = me_blk // 2, lax.rem(me_blk, 2)
    if isinstance(i, int):
        sign = i % 2 * 2 - 1
    else:
        sign = lax.rem(i, 2) * 2 - 1
    other = lax.rem(outer * sign + (half - 1) - i + 2 * half, half)
    return other * 2 + (side if inner else 1 - side)


def whole_kernel(
    dims, number_hbm, sky_hbm, starts_hbm, first_hbm, twice_hbm, wave_hbm, phase_hbm,
    harm_ref, out_ref,
    number_ref, sky_ref, starts_ref, first_ref, twice_ref, wave_ref, phase_ref,
    lhs_ref, rest_ref, rows_ref, turned_ref, held_ref, pieces_ref, scales_ref, z_ref, p_ref,
    turn_ref, init_ref, leg_ref, weight_ref, near_a, near_b, sums_ref, part_ref, other_ref, relay_ref,
    load_sem, send_sem, recv_sem, part_send, part_recv, relay_sem,
):
    blk_total, map_total, maps, factor, scale = dims
    count = blk_total * map_total
    cycles = number_hbm.shape[0]
    share = out_ref.shape[1]
    me_blk, me_map = lax.axis_index("blk"), lax.axis_index("map")
    me = me_blk * map_total + me_map
    k_share = RES // blk_total
    fetched = [
        pltpu.make_async_copy(source, target, load_sem.at[i])
        for i, (source, target) in enumerate(
            [
                (sky_hbm, sky_ref), (wave_hbm, wave_ref), (first_hbm, first_ref),
                (twice_hbm, twice_ref),
                (phase_hbm, phase_ref), (number_hbm, number_ref), (starts_hbm, starts_ref),
            ]
        )
    ]
    for copy in fetched:
        copy.start()
    barrier = pltpu.get_barrier_semaphore()
    blk_at = [me_blk] + [wrapped(me_blk + i, blk_total) for i in range(1, blk_total)]
    map_at = [me_map] + [wrapped(me_map + i, map_total) for i in range(1, map_total)]
    away = [(b, m) for b in range(blk_total) for m in range(map_total) if b or m]
    for b, m in away:
        pl.semaphore_signal(
            barrier, inc=1, device_id={"blk": blk_at[b], "map": map_at[m]},
            device_id_type=pl.DeviceIdType.MESH,
        )
    prepare(blk_total, scales_ref.shape[0], pieces_ref, p_ref)
    turn_factors(scale, scales_ref, p_ref)
    for copy in fetched[:-1]:
        copy.wait()
    sky_modes(
        (maps, factor), number_ref, sky_ref, first_ref, twice_ref, wave_ref, phase_ref, lhs_ref,
        rest_ref, rows_ref, me,
    )
    turned_ref[...] = rows_ref[...].T.astype(jnp.bfloat16)
    pl.semaphore_wait(barrier, count - 1)

    def modes_to(target_blk, target_map, source):
        peer = target_blk * map_total + target_map
        return pltpu.make_async_remote_copy(
            src_ref=turned_ref.at[pl.ds(pl.multiple_of(target_blk * k_share, k_share), k_share)],
            dst_ref=held_ref.at[source],
            send_sem=send_sem.at[peer],
            recv_sem=recv_sem.at[source],
            device_id={"blk": target_blk, "map": target_map},
            device_id_type=pl.DeviceIdType.MESH,
        )

    half = blk_total // 2
    for b, m in away:
        modes_to(blk_at[b], map_at[m], me).start()
    held_ref[me] = turned_ref[pl.ds(pl.multiple_of(me_blk * k_share, k_share), k_share), :]

    heights(number_ref, z_ref)
    fetched[-1].wait()
    start_values(starts_ref, turn_ref, init_ref)
    for part in range(init_ref.shape[2] // STEP_LANES):
        recurrence(part, cycles, z_ref, pieces_ref, init_ref, leg_ref)

    for b, m in away:
        modes_to(blk_at[b], map_at[m], blk_at[b] * map_total + map_at[m]).wait_recv()
    block_weights(maps, held_ref, weight_ref)

    pairs = maps * (maps + 1) // 2
    pair_rows = part_ref.shape[1]
    row = lax.broadcasted_iota(jnp.int32, (pair_rows, pair_rows * PACK), 0)
    lane = lax.broadcasted_iota(jnp.int32, (pair_rows, pair_rows * PACK), 1)
    gather = jnp.where(lane // PACK == row, 1.0, 0.0).astype(jnp.bfloat16)
    for p in range(pairs, pair_rows):
        sums_ref[p * PACK : (p + 1) * PACK, :] = jnp.zeros((PACK, share), jnp.bfloat16)

    def part_to(peer, source):
        return pltpu.make_async_remote_copy(
            src_ref=part_ref.at[peer],
            dst_ref=other_ref.at[source],
            send_sem=part_send.at[peer],
            recv_sem=part_recv.at[source],
            device_id={"blk": peer},
            device_id_type=pl.DeviceIdType.MESH,
        )

    def place(i, inner):
        return visit(me_blk, i, inner, blk_total)

    def project(u, near_ref):
        return project_tiles(u, maps, share, leg_ref, scales_ref, weight_ref, harm_ref, near_ref)

    def finish(u):
        part_ref[u] = jnp.dot(
            gather, sums_ref[...], preferred_element_type=jnp.float32
        ).astype(jnp.bfloat16)
        return u

    beside = place(half - 1, 0)
    firsts = (place(1, 0), place(0, 1), place(2, 0), beside)
    seconds = (place(0, 0), place(1, 1), place(2, 1))
    relay = pltpu.make_async_remote_copy(
        src_ref=part_ref.at[firsts[0]],
        dst_ref=relay_ref,
        send_sem=relay_sem.at[0],
        recv_sem=relay_sem.at[1],
        device_id={"blk": beside},
        device_id_type=pl.DeviceIdType.MESH,
    )

    def chosen(i, options):
        value = options[-1]
        for at in range(len(options) - 1):
            value = jnp.where(i == at, options[at], value)
        return value

    def two_shares(i, _):
        first, second = chosen(i, firsts[:3]), chosen(i, seconds)
        third = chosen(i, firsts[1:])
        interleave(product_steps(maps, share, near_a, sums_ref), project(second, near_b))
        finish(first)

        @pl.when(i == 0)
        def _():
            relay.start()

        @pl.when(i > 0)
        def _():
            part_to(first, me_blk).start()

        interleave(product_steps(maps, share, near_b, sums_ref), project(third, near_a))
        finish(second)

        @pl.when(i != 1)
        def _():
            part_to(second, me_blk).start()

        return 0

    interleave(project(firsts[0], near_a), [])
    lax.fori_loop(0, 3, two_shares, 0)
    relay.wait_recv()
    both = part_ref[seconds[1]].astype(jnp.float32) + relay_ref[...].astype(jnp.float32)
    part_ref[seconds[1]] = both.astype(jnp.bfloat16)
    part_to(seconds[1], me_blk).start()
    interleave(product_steps(maps, share, near_a, sums_ref), [])
    finish(beside)
    part_to(beside, me_blk).start()
    interleave(project(me_blk, near_b), [])
    interleave(product_steps(maps, share, near_b, sums_ref), [])
    finish(me_blk)
    direct = (seconds[0], firsts[1], firsts[2], seconds[2], beside, seconds[1])
    out_rows = maps * maps
    row = lax.broadcasted_iota(jnp.int32, (out_rows, pair_rows), 0)
    lane = lax.broadcasted_iota(jnp.int32, (out_rows, pair_rows), 1)
    low = jnp.minimum(row // maps, row % maps)
    high = jnp.maximum(row // maps, row % maps)
    pair_at = low * maps - low * (low - 1) // 2 + high - low
    unfold = jnp.where(lane == pair_at, 1.0, 0.0).astype(jnp.bfloat16)
    unfolded = lambda x: jnp.dot(unfold, x, preferred_element_type=jnp.float32)
    total = unfolded(part_ref[me_blk])
    for peer in direct:
        part_to(peer, peer).wait_recv()
        total = total + unfolded(other_ref[peer])
    out_ref[...] = total * (1.0 / (MGRP * RES))
    for b, m in away:
        modes_to(blk_at[b], map_at[m], me).wait_send()
    for peer in direct:
        part_to(peer, me_blk).wait_send()
    relay.wait_send()


def constant_tables(cycle_len, maps):
    low_len = cycle_len // RES
    residue = np.arange(RES)
    angle = np.float32(2.0 * math.pi / RES) * (
        residue[:, None] * residue[None, :] % RES
    ).astype(np.float32)
    first = np.concatenate([np.cos(angle), -np.sin(angle)], axis=1)
    first = first.astype(jnp.bfloat16).astype(np.float32)
    m_value = MSTART + RES * np.arange(MGRP)[:, None, None] + residue[None, None, :]
    turn = m_value * np.arange(low_len)[None, :, None] % cycle_len
    angle = np.float32(2.0 * math.pi / cycle_len) * turn.astype(np.float32)
    wave = np.concatenate([np.cos(angle), -np.sin(angle)], axis=2).astype(jnp.bfloat16)
    m_value = MSTART + np.arange(MGRP)[:, None] * RES + np.arange(RES)[None, :]
    angle = np.float32(math.pi / cycle_len) * (m_value % (2 * cycle_len)).astype(np.float32)
    phase = np.concatenate([np.cos(angle), np.sin(angle)], axis=0)
    twice = np.repeat(first, maps - 8, axis=0)
    return jnp.asarray(first), jnp.asarray(twice), jnp.asarray(wave), jnp.asarray(phase)


def kernel_fits(own_cycles, blk_total, cycles, maps_count, block_count):
    local_cols = MGRP * RES // blk_total
    return (
        own_cycles == 1
        and blk_total == 8
        and maps_count in (9, 10, 12)
        and local_cols == 64
        and KDIM % cycles == 0
        and KDIM // cycles == 8
        and 2 * maps_count * MGRP <= 128
        and block_count % 8 == 0
        and block_count % blk_total == 0
        and (block_count * LBLK // blk_total) % (2 * LBLK) == 0
    )


def fast_body(sky_maps, cycle_number, legendre_starts):
    _, maps, cycle_len = sky_maps.shape
    map_total = lax.axis_size("map")
    blk_total = lax.axis_size("blk")
    local_cols, blocks, cycles = legendre_starts.shape[1:]
    count = blk_total * map_total
    local_len = blocks * LBLK
    share = local_len // blk_total
    parts = 2 * maps
    q_group = KDIM // cycles
    lanes = local_cols * cycles
    pair_rows = -(-(maps * (maps + 1) // 2) // 8) * 8
    tables = constant_tables(cycle_len, maps)
    starts = jnp.transpose(legendre_starts, (0, 2, 3, 1))
    dims = (blk_total, map_total, maps, 1.0 / math.sqrt(cycle_len), 1.0 / math.sqrt(cycles))
    vmem = pl.BlockSpec(memory_space=pltpu.VMEM)
    pitch = LBLK + GAP
    harmonics, spectra = pl.pallas_call(
        functools.partial(whole_kernel, dims),
        out_shape=(
            pltpu.VMEM((parts, local_cols, local_len), jnp.bfloat16),
            pltpu.VMEM((maps * maps, share), jnp.float32),
        ),
        in_specs=[pl.BlockSpec(memory_space=pl.ANY)] * 7,
        out_specs=(vmem, vmem),
        scratch_shapes=[pltpu.SMEM(cycle_number.shape, jnp.int32)]
        + [pltpu.VMEM(x.shape, x.dtype) for x in (sky_maps, starts, *tables)]
        + [
            pltpu.VMEM((RES * 8, cycle_len // RES), jnp.float32),
            pltpu.VMEM((RES * (maps - 8), cycle_len // RES), jnp.float32),
            pltpu.VMEM((128, RES), jnp.float32),
            pltpu.VMEM((RES, 128), jnp.bfloat16),
            pltpu.VMEM((count, RES // blk_total, 128), jnp.bfloat16),
            pltpu.VMEM((local_len, 256), jnp.bfloat16),
            pltpu.VMEM((blocks, local_cols, LBLK), jnp.float32),
            pltpu.VMEM((1, STEP_LANES), jnp.float32),
            pltpu.VMEM((blocks * pitch, 128), jnp.float32),
            pltpu.VMEM((2, blocks * (local_cols + START_GAP), 128), jnp.float32),
            pltpu.VMEM((2, blocks, lanes), jnp.float32),
            pltpu.VMEM((lanes // 128, blocks * pitch, 128), jnp.float32),
            pltpu.VMEM((local_cols // q_group, parts * q_group, KDIM), jnp.bfloat16),
            pltpu.VMEM((parts, local_cols, share), jnp.bfloat16),
            pltpu.VMEM((parts, local_cols, share), jnp.bfloat16),
            pltpu.VMEM((pair_rows * PACK, share), jnp.bfloat16),
            pltpu.VMEM((blk_total, pair_rows, share), jnp.bfloat16),
            pltpu.VMEM((blk_total, pair_rows, share), jnp.bfloat16),
            pltpu.VMEM((pair_rows, share), jnp.bfloat16),
            pltpu.SemaphoreType.DMA((7,)),
            pltpu.SemaphoreType.DMA((count,)),
            pltpu.SemaphoreType.DMA((count,)),
            pltpu.SemaphoreType.DMA((blk_total,)),
            pltpu.SemaphoreType.DMA((blk_total,)),
            pltpu.SemaphoreType.DMA((2,)),
        ],
        compiler_params=pltpu.CompilerParams(
            collective_id=0, has_side_effects=True, vmem_limit_bytes=48 * 1024 * 1024
        ),
    )(
        *(
            pltpu.with_memory_space_constraint(x, pltpu.HBM)
            for x in (cycle_number, sky_maps, starts, *tables)
        )
    )
    harmonics, spectra = write_out(harmonics, spectra, maps)
    return (jnp.transpose(harmonics, (1, 0, 2)), jnp.transpose(spectra, (2, 0, 1, 3)))


def write_kernel(maps, harm_ref, sums_ref, harm_out, spectra_out, spectra_ref, sem, spectra_sem):
    pieces = sem.shape[0]
    rows = harm_ref.shape[0] // pieces
    copies = [
        pltpu.make_async_copy(
            harm_ref.at[pl.ds(i * rows, rows)], harm_out.at[pl.ds(i * rows, rows)], sem.at[i]
        )
        for i in range(pieces)
    ]
    for copy in copies:
        copy.start()
    for i in range(maps):
        for k in range(maps):
            spectra_ref[i, k] = sums_ref[i * maps + k : i * maps + k + 1]
    last = pltpu.make_async_copy(spectra_ref, spectra_out, spectra_sem)
    last.start()
    for copy in copies:
        copy.wait()
    last.wait()


def write_out(harmonics, spectra, maps):
    vmem = pl.BlockSpec(memory_space=pltpu.VMEM)
    shape = (maps, maps, 1, spectra.shape[1])
    return pl.pallas_call(
        functools.partial(write_kernel, maps),
        out_shape=(
            jax.ShapeDtypeStruct(harmonics.shape, harmonics.dtype),
            jax.ShapeDtypeStruct(shape, jnp.float32),
        ),
        in_specs=[vmem, vmem],
        out_specs=(pl.BlockSpec(memory_space=pl.ANY),) * 2,
        scratch_shapes=[
            pltpu.VMEM(shape, jnp.float32),
            pltpu.SemaphoreType.DMA((2,)),
            pltpu.SemaphoreType.DMA,
        ],
        compiler_params=pltpu.CompilerParams(vmem_limit_bytes=8 * 1024 * 1024),
    )(harmonics, spectra)


def body(sky_maps, cycle_number, legendre_starts):
    own_cycles, maps_count, cycle_len = sky_maps.shape
    map_total = lax.axis_size("map")
    blk_total = lax.axis_size("blk")
    cycles, block_count = cycle_number.shape[0], legendre_starts.shape[2]
    if kernel_fits(own_cycles, blk_total, cycles, maps_count, block_count):
        return fast_body(sky_maps, cycle_number, legendre_starts)
    tables = dft_tables(cycle_len)
    first_row = (lax.axis_index("blk") * map_total + lax.axis_index("map")) * own_cycles
    own_numbers = lax.dynamic_slice_in_dim(cycle_number, first_row, own_cycles)
    parity = (own_numbers - NSIDE + 1) % 2
    local_modes = cycle_transform(sky_maps, parity, tables)
    grouped = lax.all_gather(local_modes, "map", axis=0, tiled=True)
    regrouped = lax.all_to_all(grouped, "blk", split_axis=4, concat_axis=0, tiled=True)
    ordered = jnp.transpose(regrouped, (4, 3, 1, 2, 0))
    local_cols = ordered.shape[0] * ordered.shape[1]
    cycle_modes = ordered.reshape(local_cols, 2 * maps_count, -1)
    heights = cycle_height(cycle_number)
    column = lax.axis_index("blk") * local_cols + jnp.arange(local_cols, dtype=jnp.int32)
    m_float = (MSTART + RES * (column % MGRP) + column // MGRP).astype(jnp.float32)
    block_count = legendre_starts.shape[2]
    local_len = block_count * LBLK
    first_l = LSTART + lax.axis_index("map") * local_len
    cycle_scale = 1.0 / math.sqrt(cycle_modes.shape[-1])

    def one_block(block_index):
        start_pair = lax.dynamic_index_in_dim(legendre_starts, block_index, 2, keepdims=False)
        legendre_tile = legendre_rows(
            start_pair, heights, m_float, first_l + block_index * LBLK
        ).astype(jnp.bfloat16)
        projected = (
            jnp.einsum(
                "qlr,qnr->qnl", legendre_tile, cycle_modes, preferred_element_type=jnp.float32
            )
            * cycle_scale
        )
        return projected.astype(jnp.bfloat16)

    blocks_out = lax.map(one_block, jnp.arange(block_count, dtype=jnp.int32))
    harmonics = jnp.transpose(blocks_out, (1, 2, 0, 3)).reshape(
        local_cols, 2 * maps_count, local_len
    )
    total_cols = MGRP * RES
    spread = harmonics.reshape(local_cols, 2 * maps_count, blk_total, local_len // blk_total)
    spread = jnp.transpose(spread, (2, 3, 1, 0))
    received = lax.all_to_all(
        shortened(spread), "blk", split_axis=0, concat_axis=3, tiled=True
    ).astype(spread.dtype)
    item_count = received.shape[1]
    split_piece = received.reshape(item_count, 2, maps_count, received.shape[3])
    cross_sum = jnp.einsum(
        "gciq,gcjq->ijg", split_piece, split_piece, preferred_element_type=jnp.float32
    )
    owned = (cross_sum / total_cols)[None]
    return (harmonics, owned)


def solution(mesh):
    return jax.shard_map(
        body,
        mesh=mesh,
        in_specs=(P(("blk", "map"), None, None), P(), P(None, "blk", "map", None)),
        out_specs=(P("blk", None, "map"), P("map", None, None, "blk")),
        check_vma=False,
    )
```

```python
import functools
import math

import jax
import jax.numpy as jnp
import numpy as np
from jax import lax
from jax.experimental import pallas as pl
from jax.experimental.pallas import tpu as pltpu
from jax.sharding import PartitionSpec as P

NSIDE = 8192
RES = 128
MGRP = 4
MSTART = 4096
LSTART = 8192
LBLK = 128


def shortened(array):

    def short(part):
        return part.astype(jnp.bfloat16) if part.dtype == jnp.float32 else part

    return jax.tree.map(short, array)


def cycle_height(cycle_ids):
    return (4.0 * NSIDE - 2.0 * cycle_ids.astype(jnp.float32)) / (3.0 * NSIDE)


def dft_tables(cycle_len):
    low_len = cycle_len // RES
    residue = jnp.arange(RES, dtype=jnp.int32)
    turn_one = residue[:, None] * residue[None, :] % RES
    angle_one = 2.0 * math.pi / RES * turn_one.astype(jnp.float32)
    first_table = jnp.concatenate([jnp.cos(angle_one), -jnp.sin(angle_one)], axis=1).astype(
        jnp.bfloat16
    )
    column_group = jnp.arange(MGRP, dtype=jnp.int32)
    sample = jnp.arange(low_len, dtype=jnp.int32)
    m_value = MSTART + RES * column_group[:, None, None] + residue[None, None, :]
    turn_two = m_value * sample[None, :, None] % cycle_len
    angle_two = 2.0 * math.pi / cycle_len * turn_two.astype(jnp.float32)
    twiddle_re = jnp.cos(angle_two).astype(jnp.bfloat16)
    twiddle_im = (-jnp.sin(angle_two)).astype(jnp.bfloat16)
    return (first_table, twiddle_re, twiddle_im)


def cycle_transform(cycle_rows, parity, tables):
    first_table, twiddle_re, twiddle_im = tables
    cycle_count, maps_count, cycle_len = cycle_rows.shape
    low_len = cycle_len // RES
    folded = cycle_rows.reshape(cycle_count, maps_count, RES, low_len)
    section_one = jnp.einsum(
        "rnaj,ak->rnjk", folded, first_table, preferred_element_type=jnp.float32
    )
    section_one = section_one.astype(jnp.bfloat16)
    part_re = section_one[..., :RES]
    part_im = section_one[..., RES:]
    real_sum = jnp.einsum(
        "rnjk,cjk->rnck", part_re, twiddle_re, preferred_element_type=jnp.float32
    ) - jnp.einsum("rnjk,cjk->rnck", part_im, twiddle_im, preferred_element_type=jnp.float32)
    imag_sum = jnp.einsum(
        "rnjk,cjk->rnck", part_im, twiddle_re, preferred_element_type=jnp.float32
    ) + jnp.einsum("rnjk,cjk->rnck", part_re, twiddle_im, preferred_element_type=jnp.float32)
    column_group = jnp.arange(MGRP, dtype=jnp.int32)
    residue = jnp.arange(RES, dtype=jnp.int32)
    m_value = MSTART + RES * column_group[:, None] + residue[None, :]
    shifted = m_value[None, :, :] * parity[:, None, None] % (2 * cycle_len)
    phase_angle = math.pi / cycle_len * shifted.astype(jnp.float32)
    cos_part = jnp.cos(phase_angle)[:, None]
    sin_part = jnp.sin(phase_angle)[:, None]
    factor = 1.0 / math.sqrt(cycle_len)
    out_re = factor * (cos_part * real_sum + sin_part * imag_sum)
    out_im = factor * (cos_part * imag_sum - sin_part * real_sum)
    return jnp.stack([out_re, out_im], axis=1).astype(jnp.bfloat16)


def legendre_rows(start_pair, height, m_float, first_l):
    m_column = m_float[:, None]

    def recur_coef(degree):
        return jnp.sqrt((4.0 * degree * degree - 1.0) / ((degree - m_column) * (degree + m_column)))

    base_l = first_l.astype(jnp.float32)
    value_older = start_pair[0]
    value_newer = start_pair[1]
    prior_coef = recur_coef(base_l - 1.0)
    height_row = height[None, :]
    stacked_rows = []
    for offset in range(LBLK):
        present_coef = recur_coef(base_l + offset)
        value_now = present_coef * (height_row * value_newer - value_older / prior_coef)
        stacked_rows.append(value_now)
        value_older = value_newer
        value_newer = value_now
        prior_coef = present_coef
    return jnp.stack(stacked_rows, axis=1)


STEP_LANES = 1024
KDIM = 256
GAP = 8
RUN = 64
PACK = 8
WIDE = 256
START_GAP = 8


def sky_modes(totals, number_ref, sky_ref, first_ref, twice_ref, wave_ref, phase_ref, lhs_ref,
              rest_ref, rows_ref, me):
    maps, factor = totals
    low_len = wave_ref.shape[1]
    more = maps - 8
    for a in range(RES):
        values = sky_ref[0, :, a * low_len : (a + 1) * low_len].astype(jnp.float32)
        lhs_ref[a * 8 : a * 8 + 8, :] = values[:8]
        rest_ref[a * more : (a + 1) * more, :] = values[8:]
    rows_ref[...] = jnp.zeros_like(rows_ref)
    parity = (number_ref[me] - NSIDE + 1) % 2
    odd = jnp.full((MGRP, RES), parity, jnp.int32) == 1
    cosines = jnp.where(odd, phase_ref[:MGRP], 1.0)
    sines = jnp.where(odd, phase_ref[MGRP:], 0.0)
    none = jnp.zeros((8, RES), jnp.float32)
    for c in range(MGRP):
        real, imag, real_more, imag_more = none, none, none, none
        out = jnp.dot(
            lhs_ref[...].astype(jnp.bfloat16), wave_ref[c], preferred_element_type=jnp.float32
        )
        for a in range(RES):
            e_re, e_im = first_ref[a : a + 1, :RES], first_ref[a : a + 1, RES:]
            w_re, w_im = out[a * 8 : a * 8 + 8, :RES], out[a * 8 : a * 8 + 8, RES:]
            real = real + (e_re * w_re - e_im * w_im)
            imag = imag + (e_re * w_im + e_im * w_re)
        out = jnp.dot(
            rest_ref[...].astype(jnp.bfloat16), wave_ref[c], preferred_element_type=jnp.float32
        )
        for a in range(RES * more // 8):
            rows = slice(a * 8, a * 8 + 8)
            e_re, e_im = twice_ref[rows, :RES], twice_ref[rows, RES:]
            w_re, w_im = out[rows, :RES], out[rows, RES:]
            real_more = real_more + (e_re * w_re - e_im * w_im)
            imag_more = imag_more + (e_re * w_im + e_im * w_re)
        cos, sin = cosines[c : c + 1], sines[c : c + 1]
        row = c * 2 * maps
        for re, im, at, size in ((real, imag, 0, 8), (real_more, imag_more, 8, more)):
            if size != 8:
                re = sum(re[i : i + size] for i in range(0, 8, size))
                im = sum(im[i : i + size] for i in range(0, 8, size))
            first = row + at
            rows_ref[first : first + size, :] = factor * (cos * re + sin * im)
            rows_ref[first + maps : first + maps + size, :] = factor * (cos * im - sin * re)


def heights(number_ref, z_ref):
    lane = lax.broadcasted_iota(jnp.int32, z_ref.shape, 1) % number_ref.shape[0]
    numbers = jnp.zeros(z_ref.shape, jnp.int32)
    for r in range(number_ref.shape[0]):
        numbers = jnp.where(lane == r, number_ref[r], numbers)
    z_ref[...] = cycle_height(numbers)


def prepare(blk_total, blocks, pieces_ref, p_ref):
    local_cols = MGRP * RES // blk_total
    lane = lax.broadcasted_iota(jnp.int32, (blocks, 128), 1)
    column = lax.axis_index("blk") * local_cols + lane % local_cols
    m_row = (MSTART + RES * (column % MGRP) + column // MGRP).astype(jnp.float32)
    block = lax.broadcasted_iota(jnp.int32, (blocks, 128), 0)
    base = LSTART + (lax.axis_index("map") * blocks + block) * LBLK

    def setup(j, carry):
        p_prev, q_prev = carry
        degree = (base + j).astype(jnp.float32)
        num = 4.0 * degree * degree - 1.0
        den = (degree - m_row) * (degree + m_row)
        root = lax.rsqrt(num * den)
        kappa = p_prev * p_prev
        high = kappa.astype(jnp.bfloat16).astype(jnp.float32)
        rest = kappa - high
        mid = rest.astype(jnp.bfloat16).astype(jnp.float32)
        low = rest - mid
        rows = pl.ds(pl.multiple_of(j * blocks, blocks), blocks)
        pieces_ref[rows, :128] = jnp.where(lane < local_cols, high, mid).astype(jnp.bfloat16)
        pieces_ref[rows, 128:] = low.astype(jnp.bfloat16)
        p_now = num * root * q_prev
        q_now = den * root * p_prev
        for half in range(blocks // 8):
            p_ref[pl.ds(half * 8 * (LBLK + GAP) + j, 8, stride=LBLK + GAP), :] = p_now[
                half * 8 : half * 8 + 8
            ]
        return p_now, q_now

    one = jnp.ones((blocks, 128), jnp.float32)
    lax.fori_loop(0, LBLK, setup, (one, one), unroll=4)


def turn_factors(scale, scales_ref, p_ref):
    blocks, local_cols, _ = scales_ref.shape

    def turn(t, _):
        turned = p_ref[pl.ds(pl.multiple_of(t * (LBLK + GAP), 8), LBLK), :].T
        scales_ref[t] = turned[:local_cols] * scale
        return 0

    lax.fori_loop(0, blocks, turn, 0)


def start_values(starts_ref, turn_ref, init_ref):
    _, blocks, cycles, local_cols = starts_ref.shape
    lane = lax.broadcasted_iota(jnp.int32, (blocks, local_cols), 1)
    column = lax.axis_index("blk") * local_cols + lane
    m_row = (MSTART + RES * (column % MGRP) + column // MGRP).astype(jnp.float32)
    block = lax.broadcasted_iota(jnp.int32, (blocks, local_cols), 0)
    degree = (LSTART + (lax.axis_index("map") * blocks + block) * LBLK - 1).astype(jnp.float32)
    inverse = jnp.sqrt(((degree - m_row) * (degree + m_row)) / (4.0 * degree * degree - 1.0))
    pitch = local_cols + START_GAP
    for kind in range(2):
        for t in range(blocks):
            values = starts_ref[kind, t]
            if kind == 0:
                values = values * inverse[t : t + 1]
            turn_ref[kind, t * pitch : t * pitch + local_cols, :cycles] = values.T
    per_tile = 128 // cycles
    slot = lax.broadcasted_iota(jnp.int32, (8, 128), 1) // cycles
    for kind in range(2):
        for half in range(blocks // 8):
            for tile in range(local_cols // per_tile):
                row = None
                for i in range(per_tile):
                    first = half * 8 * pitch + tile * per_tile + i
                    part = turn_ref[kind, pl.ds(first, 8, stride=pitch), :]
                    if i == 0:
                        row = part
                    else:
                        row = jnp.where(slot == i, pltpu.roll(part, i * cycles, 1), row)
                init_ref[kind, half * 8 : half * 8 + 8, tile * 128 : tile * 128 + 128] = row


def recurrence(part, cycles, z_ref, pieces_ref, init_ref, leg_ref):
    blocks = init_ref.shape[1]
    halves = STEP_LANES // 128
    q_row = lax.broadcasted_iota(jnp.int32, (256, STEP_LANES), 0)
    q_lane = lax.broadcasted_iota(jnp.int32, (256, STEP_LANES), 1) // cycles + part * (
        STEP_LANES // cycles
    )
    spread = jnp.where((q_row % 64 == q_lane) & (q_row < 192), 1.0, 0.0).astype(jnp.bfloat16)

    def recur(i, carry):
        older, newer = carry
        rows = pl.ds(pl.multiple_of(i * RUN * blocks, RUN * blocks), RUN * blocks)
        kap = jnp.dot(pieces_ref[rows, :], spread, preferred_element_type=jnp.float32)
        for j in range(RUN):
            now = (kap[j * blocks : (j + 1) * blocks] * z_ref[...]) * newer - older
            for half in range(blocks // 8):
                at = pl.ds(half * 8 * (LBLK + GAP) + i * RUN + j, 8, stride=LBLK + GAP)
                for g in range(halves):
                    leg_ref[part * halves + g, at, :] = now[
                        half * 8 : half * 8 + 8, g * 128 : g * 128 + 128
                    ]
            older, newer = newer, now
        return older, newer

    lanes = slice(part * STEP_LANES, (part + 1) * STEP_LANES)
    lax.fori_loop(0, LBLK // RUN, recur, (init_ref[0, :, lanes], init_ref[1, :, lanes]))


def block_weights(maps, held_ref, weight_ref):
    groups, rows_all, _ = weight_ref.shape
    cycles, _, _ = held_ref.shape
    parts = 2 * maps
    q_group = rows_all // parts
    per_group = q_group // MGRP
    row = lax.broadcasted_iota(jnp.int32, (rows_all, per_group * 128), 0)
    lane = lax.broadcasted_iota(jnp.int32, (rows_all, per_group * 128), 1)
    q = row % q_group
    wanted = q // MGRP * 128 + (q % MGRP) * parts + row // q_group
    pick = jnp.where(lane == wanted, 1.0, 0.0).astype(jnp.bfloat16)
    row = lax.broadcasted_iota(jnp.int32, (rows_all, KDIM), 0)
    lane = lax.broadcasted_iota(jnp.int32, (rows_all, KDIM), 1)
    same_q = row % q_group == lane // cycles
    modes = jnp.swapaxes(held_ref[...].astype(jnp.float32), 0, 1).astype(jnp.bfloat16)
    for g in range(groups):
        own = jnp.concatenate([modes[g * per_group + k] for k in range(per_group)], axis=1)
        wide = lax.dot_general(
            pick, jnp.concatenate([own] * q_group, axis=0), (((1,), (1,)), ((), ())),
            preferred_element_type=jnp.float32,
        )
        weight_ref[g] = jnp.where(same_q, wide, 0.0).astype(jnp.bfloat16)


def project_tiles(u, maps, share, leg_ref, scales_ref, weight_ref, harm_ref, near_ref):
    groups, rows_all, _ = weight_ref.shape
    parts = 2 * maps
    q_group = rows_all // parts
    width = 2 * LBLK

    def tile(piece, g):
        first_t = u * (share // LBLK) + 2 * piece
        cols = pl.ds(pl.multiple_of(u * share + piece * width, width), width)
        sources = [
            pl.ds(pl.multiple_of((first_t + x) * (LBLK + GAP), 8), LBLK) for x in range(2)
        ]
        rows = slice(g * q_group, (g + 1) * q_group)
        p_rows = jnp.concatenate([scales_ref[first_t + x, rows, :] for x in range(2)], axis=1)
        leg = jnp.concatenate(
            [
                jnp.concatenate(
                    [leg_ref[g * (KDIM // 128) + h, src, :] for h in range(KDIM // 128)], axis=1
                )
                for src in sources
            ],
            axis=0,
        ).astype(jnp.bfloat16)
        out = lax.dot_general(
            weight_ref[g], leg, (((1,), (1,)), ((), ())), preferred_element_type=jnp.float32
        )
        crossed = (out.reshape(parts, q_group, width) * p_rows[None]).astype(jnp.bfloat16)
        harm_ref[:, rows, cols] = crossed
        near_ref[:, rows, piece * width : (piece + 1) * width] = crossed

    return [
        functools.partial(tile, piece, g) for piece in range(share // width) for g in range(groups)
    ]


def product_steps(maps, share, near_ref, sums_ref):
    local_cols = near_ref.shape[1]
    pairs = [(i, k) for i in range(maps) for k in range(i, maps)]
    middle = maps // 2
    sets = [
        [p for p, (i, k) in enumerate(pairs) if k < middle],
        [p for p, (i, k) in enumerate(pairs) if i >= middle],
        [p for p, (i, k) in enumerate(pairs) if i < middle <= k and i % 2 == 0],
        [p for p, (i, k) in enumerate(pairs) if i < middle <= k and i % 2 == 1],
    ]

    def some(piece, chosen):
        cols = slice(piece * WIDE, (piece + 1) * WIDE)
        total = {}
        for h in range(2):
            for t in range(local_cols // PACK):
                x = {}
                for n in sorted({v for p in chosen for v in pairs[p]}):
                    x[n] = near_ref[h * maps + n, t * PACK : (t + 1) * PACK, cols]
                for p in chosen:
                    i, k = pairs[p]
                    term = x[i] * x[k]
                    total[p] = term if p not in total else total[p] + term
        for p in chosen:
            sums_ref[p * PACK : (p + 1) * PACK, cols] = total[p]

    return [
        functools.partial(some, piece, chosen)
        for piece in range(share // WIDE)
        for chosen in sets
    ]


def interleave(one, other):
    for i in range(max(len(one), len(other))):
        for steps in (one, other):
            if i < len(steps):
                steps[i]()


def wrapped(index, total):
    return jnp.where(index >= total, index - total, index)


def visit(me_blk, i, inner, blk_total):
    half = blk_total // 2
    outer, side = me_blk // 2, lax.rem(me_blk, 2)
    if isinstance(i, int):
        sign = i % 2 * 2 - 1
    else:
        sign = lax.rem(i, 2) * 2 - 1
    other = lax.rem(outer * sign + (half - 1) - i + 2 * half, half)
    return other * 2 + (side if inner else 1 - side)


def whole_kernel(
    dims, number_hbm, sky_hbm, starts_hbm, first_hbm, twice_hbm, wave_hbm, phase_hbm,
    harm_ref, out_ref,
    number_ref, sky_ref, starts_ref, first_ref, twice_ref, wave_ref, phase_ref,
    lhs_ref, rest_ref, rows_ref, turned_ref, held_ref, pieces_ref, scales_ref, z_ref, p_ref,
    turn_ref, init_ref, leg_ref, weight_ref, near_a, near_b, sums_ref, part_ref, other_ref, relay_ref,
    load_sem, send_sem, recv_sem, part_send, part_recv, relay_sem,
):
    blk_total, map_total, maps, factor, scale = dims
    count = blk_total * map_total
    cycles = number_hbm.shape[0]
    share = out_ref.shape[1]
    me_blk, me_map = lax.axis_index("blk"), lax.axis_index("map")
    me = me_blk * map_total + me_map
    k_share = RES // blk_total
    fetched = [
        pltpu.make_async_copy(source, target, load_sem.at[i])
        for i, (source, target) in enumerate(
            [
                (sky_hbm, sky_ref), (wave_hbm, wave_ref), (first_hbm, first_ref),
                (twice_hbm, twice_ref),
                (phase_hbm, phase_ref), (number_hbm, number_ref), (starts_hbm, starts_ref),
            ]
        )
    ]
    for copy in fetched:
        copy.start()
    barrier = pltpu.get_barrier_semaphore()
    blk_at = [me_blk] + [wrapped(me_blk + i, blk_total) for i in range(1, blk_total)]
    map_at = [me_map] + [wrapped(me_map + i, map_total) for i in range(1, map_total)]
    away = [(b, m) for b in range(blk_total) for m in range(map_total) if b or m]
    for b, m in away:
        pl.semaphore_signal(
            barrier, inc=1, device_id={"blk": blk_at[b], "map": map_at[m]},
            device_id_type=pl.DeviceIdType.MESH,
        )
    prepare(blk_total, scales_ref.shape[0], pieces_ref, p_ref)
    turn_factors(scale, scales_ref, p_ref)
    for copy in fetched[:-1]:
        copy.wait()
    sky_modes(
        (maps, factor), number_ref, sky_ref, first_ref, twice_ref, wave_ref, phase_ref, lhs_ref,
        rest_ref, rows_ref, me,
    )
    turned_ref[...] = rows_ref[...].T.astype(jnp.bfloat16)
    pl.semaphore_wait(barrier, count - 1)

    def modes_to(target_blk, target_map, source):
        peer = target_blk * map_total + target_map
        return pltpu.make_async_remote_copy(
            src_ref=turned_ref.at[pl.ds(pl.multiple_of(target_blk * k_share, k_share), k_share)],
            dst_ref=held_ref.at[source],
            send_sem=send_sem.at[peer],
            recv_sem=recv_sem.at[source],
            device_id={"blk": target_blk, "map": target_map},
            device_id_type=pl.DeviceIdType.MESH,
        )

    half = blk_total // 2
    for b, m in away:
        modes_to(blk_at[b], map_at[m], me).start()
    held_ref[me] = turned_ref[pl.ds(pl.multiple_of(me_blk * k_share, k_share), k_share), :]

    heights(number_ref, z_ref)
    fetched[-1].wait()
    start_values(starts_ref, turn_ref, init_ref)
    for part in range(init_ref.shape[2] // STEP_LANES):
        recurrence(part, cycles, z_ref, pieces_ref, init_ref, leg_ref)

    for b, m in away:
        modes_to(blk_at[b], map_at[m], blk_at[b] * map_total + map_at[m]).wait_recv()
    block_weights(maps, held_ref, weight_ref)

    pairs = maps * (maps + 1) // 2
    pair_rows = part_ref.shape[1]
    row = lax.broadcasted_iota(jnp.int32, (pair_rows, pair_rows * PACK), 0)
    lane = lax.broadcasted_iota(jnp.int32, (pair_rows, pair_rows * PACK), 1)
    gather = jnp.where(lane // PACK == row, 1.0, 0.0).astype(jnp.bfloat16)
    for p in range(pairs, pair_rows):
        sums_ref[p * PACK : (p + 1) * PACK, :] = jnp.zeros((PACK, share), jnp.bfloat16)

    def part_to(peer, source):
        return pltpu.make_async_remote_copy(
            src_ref=part_ref.at[peer],
            dst_ref=other_ref.at[source],
            send_sem=part_send.at[peer],
            recv_sem=part_recv.at[source],
            device_id={"blk": peer},
            device_id_type=pl.DeviceIdType.MESH,
        )

    def place(i, inner):
        return visit(me_blk, i, inner, blk_total)

    def project(u, near_ref):
        return project_tiles(u, maps, share, leg_ref, scales_ref, weight_ref, harm_ref, near_ref)

    def finish(u):
        part_ref[u] = jnp.dot(
            gather, sums_ref[...], preferred_element_type=jnp.float32
        ).astype(jnp.bfloat16)
        return u

    beside = place(half - 1, 0)
    firsts = (place(1, 0), place(0, 1), place(2, 0), beside)
    seconds = (place(0, 0), place(1, 1), place(2, 1))
    relay = pltpu.make_async_remote_copy(
        src_ref=part_ref.at[firsts[0]],
        dst_ref=relay_ref,
        send_sem=relay_sem.at[0],
        recv_sem=relay_sem.at[1],
        device_id={"blk": beside},
        device_id_type=pl.DeviceIdType.MESH,
    )

    def chosen(i, options):
        value = options[-1]
        for at in range(len(options) - 1):
            value = jnp.where(i == at, options[at], value)
        return value

    def two_shares(i, _):
        first, second = chosen(i, firsts[:3]), chosen(i, seconds)
        third = chosen(i, firsts[1:])
        interleave(product_steps(maps, share, near_a, sums_ref), project(second, near_b))
        finish(first)

        @pl.when(i == 0)
        def _():
            relay.start()

        @pl.when(i > 0)
        def _():
            part_to(first, me_blk).start()

        interleave(product_steps(maps, share, near_b, sums_ref), project(third, near_a))
        finish(second)

        @pl.when(i != 1)
        def _():
            part_to(second, me_blk).start()

        return 0

    interleave(project(firsts[0], near_a), [])
    lax.fori_loop(0, 3, two_shares, 0)
    relay.wait_recv()
    both = part_ref[seconds[1]].astype(jnp.float32) + relay_ref[...].astype(jnp.float32)
    part_ref[seconds[1]] = both.astype(jnp.bfloat16)
    part_to(seconds[1], me_blk).start()
    interleave(product_steps(maps, share, near_a, sums_ref), [])
    finish(beside)
    part_to(beside, me_blk).start()
    interleave(project(me_blk, near_b), [])
    interleave(product_steps(maps, share, near_b, sums_ref), [])
    finish(me_blk)
    direct = (seconds[0], firsts[1], firsts[2], seconds[2], beside, seconds[1])
    out_rows = maps * maps
    row = lax.broadcasted_iota(jnp.int32, (out_rows, pair_rows), 0)
    lane = lax.broadcasted_iota(jnp.int32, (out_rows, pair_rows), 1)
    low = jnp.minimum(row // maps, row % maps)
    high = jnp.maximum(row // maps, row % maps)
    pair_at = low * maps - low * (low - 1) // 2 + high - low
    unfold = jnp.where(lane == pair_at, 1.0, 0.0).astype(jnp.bfloat16)
    unfolded = lambda x: jnp.dot(unfold, x, preferred_element_type=jnp.float32)
    total = unfolded(part_ref[me_blk])
    for peer in direct:
        part_to(peer, peer).wait_recv()
        total = total + unfolded(other_ref[peer])
    out_ref[...] = total * (1.0 / (MGRP * RES))
    for b, m in away:
        modes_to(blk_at[b], map_at[m], me).wait_send()
    for peer in direct:
        part_to(peer, me_blk).wait_send()
    relay.wait_send()


def constant_tables(cycle_len, maps):
    low_len = cycle_len // RES
    residue = np.arange(RES)
    angle = np.float32(2.0 * math.pi / RES) * (
        residue[:, None] * residue[None, :] % RES
    ).astype(np.float32)
    first = np.concatenate([np.cos(angle), -np.sin(angle)], axis=1)
    first = first.astype(jnp.bfloat16).astype(np.float32)
    m_value = MSTART + RES * np.arange(MGRP)[:, None, None] + residue[None, None, :]
    turn = m_value * np.arange(low_len)[None, :, None] % cycle_len
    angle = np.float32(2.0 * math.pi / cycle_len) * turn.astype(np.float32)
    wave = np.concatenate([np.cos(angle), -np.sin(angle)], axis=2).astype(jnp.bfloat16)
    m_value = MSTART + np.arange(MGRP)[:, None] * RES + np.arange(RES)[None, :]
    angle = np.float32(math.pi / cycle_len) * (m_value % (2 * cycle_len)).astype(np.float32)
    phase = np.concatenate([np.cos(angle), np.sin(angle)], axis=0)
    twice = np.repeat(first, maps - 8, axis=0)
    return jnp.asarray(first), jnp.asarray(twice), jnp.asarray(wave), jnp.asarray(phase)


def kernel_fits(own_cycles, blk_total, cycles, maps_count, block_count):
    local_cols = MGRP * RES // blk_total
    return (
        own_cycles == 1
        and blk_total == 8
        and maps_count in (9, 10, 12)
        and local_cols == 64
        and KDIM % cycles == 0
        and KDIM // cycles == 8
        and 2 * maps_count * MGRP <= 128
        and block_count % 8 == 0
        and block_count % blk_total == 0
        and (block_count * LBLK // blk_total) % (2 * LBLK) == 0
    )


def fast_body(sky_maps, cycle_number, legendre_starts):
    _, maps, cycle_len = sky_maps.shape
    map_total = lax.axis_size("map")
    blk_total = lax.axis_size("blk")
    local_cols, blocks, cycles = legendre_starts.shape[1:]
    count = blk_total * map_total
    local_len = blocks * LBLK
    share = local_len // blk_total
    parts = 2 * maps
    q_group = KDIM // cycles
    lanes = local_cols * cycles
    pair_rows = -(-(maps * (maps + 1) // 2) // 8) * 8
    tables = constant_tables(cycle_len, maps)
    starts = jnp.transpose(legendre_starts, (0, 2, 3, 1))
    dims = (blk_total, map_total, maps, 1.0 / math.sqrt(cycle_len), 1.0 / math.sqrt(cycles))
    vmem = pl.BlockSpec(memory_space=pltpu.VMEM)
    pitch = LBLK + GAP
    harmonics, spectra = pl.pallas_call(
        functools.partial(whole_kernel, dims),
        out_shape=(
            pltpu.VMEM((parts, local_cols, local_len), jnp.bfloat16),
            pltpu.VMEM((maps * maps, share), jnp.float32),
        ),
        in_specs=[pl.BlockSpec(memory_space=pl.ANY)] * 7,
        out_specs=(vmem, vmem),
        scratch_shapes=[pltpu.SMEM(cycle_number.shape, jnp.int32)]
        + [pltpu.VMEM(x.shape, x.dtype) for x in (sky_maps, starts, *tables)]
        + [
            pltpu.VMEM((RES * 8, cycle_len // RES), jnp.float32),
            pltpu.VMEM((RES * (maps - 8), cycle_len // RES), jnp.float32),
            pltpu.VMEM((128, RES), jnp.float32),
            pltpu.VMEM((RES, 128), jnp.bfloat16),
            pltpu.VMEM((count, RES // blk_total, 128), jnp.bfloat16),
            pltpu.VMEM((local_len, 256), jnp.bfloat16),
            pltpu.VMEM((blocks, local_cols, LBLK), jnp.float32),
            pltpu.VMEM((1, STEP_LANES), jnp.float32),
            pltpu.VMEM((blocks * pitch, 128), jnp.float32),
            pltpu.VMEM((2, blocks * (local_cols + START_GAP), 128), jnp.float32),
            pltpu.VMEM((2, blocks, lanes), jnp.float32),
            pltpu.VMEM((lanes // 128, blocks * pitch, 128), jnp.float32),
            pltpu.VMEM((local_cols // q_group, parts * q_group, KDIM), jnp.bfloat16),
            pltpu.VMEM((parts, local_cols, share), jnp.bfloat16),
            pltpu.VMEM((parts, local_cols, share), jnp.bfloat16),
            pltpu.VMEM((pair_rows * PACK, share), jnp.bfloat16),
            pltpu.VMEM((blk_total, pair_rows, share), jnp.bfloat16),
            pltpu.VMEM((blk_total, pair_rows, share), jnp.bfloat16),
            pltpu.VMEM((pair_rows, share), jnp.bfloat16),
            pltpu.SemaphoreType.DMA((7,)),
            pltpu.SemaphoreType.DMA((count,)),
            pltpu.SemaphoreType.DMA((count,)),
            pltpu.SemaphoreType.DMA((blk_total,)),
            pltpu.SemaphoreType.DMA((blk_total,)),
            pltpu.SemaphoreType.DMA((2,)),
        ],
        compiler_params=pltpu.CompilerParams(
            collective_id=0, has_side_effects=True, vmem_limit_bytes=48 * 1024 * 1024
        ),
    )(
        *(
            pltpu.with_memory_space_constraint(x, pltpu.HBM)
            for x in (cycle_number, sky_maps, starts, *tables)
        )
    )
    harmonics, spectra = write_out(harmonics, spectra, maps)
    return (jnp.transpose(harmonics, (1, 0, 2)), jnp.transpose(spectra, (2, 0, 1, 3)))


def write_kernel(maps, harm_ref, sums_ref, harm_out, spectra_out, spectra_ref, sem, spectra_sem):
    pieces = sem.shape[0]
    rows = harm_ref.shape[0] // pieces
    copies = [
        pltpu.make_async_copy(
            harm_ref.at[pl.ds(i * rows, rows)], harm_out.at[pl.ds(i * rows, rows)], sem.at[i]
        )
        for i in range(pieces)
    ]
    for copy in copies:
        copy.start()
    for i in range(maps):
        for k in range(maps):
            spectra_ref[i, k] = sums_ref[i * maps + k : i * maps + k + 1]
    last = pltpu.make_async_copy(spectra_ref, spectra_out, spectra_sem)
    last.start()
    for copy in copies:
        copy.wait()
    last.wait()


def write_out(harmonics, spectra, maps):
    vmem = pl.BlockSpec(memory_space=pltpu.VMEM)
    shape = (maps, maps, 1, spectra.shape[1])
    return pl.pallas_call(
        functools.partial(write_kernel, maps),
        out_shape=(
            jax.ShapeDtypeStruct(harmonics.shape, harmonics.dtype),
            jax.ShapeDtypeStruct(shape, jnp.float32),
        ),
        in_specs=[vmem, vmem],
        out_specs=(pl.BlockSpec(memory_space=pl.ANY),) * 2,
        scratch_shapes=[
            pltpu.VMEM(shape, jnp.float32),
            pltpu.SemaphoreType.DMA((2,)),
            pltpu.SemaphoreType.DMA,
        ],
        compiler_params=pltpu.CompilerParams(vmem_limit_bytes=8 * 1024 * 1024),
    )(harmonics, spectra)


def body(sky_maps, cycle_number, legendre_starts):
    own_cycles, maps_count, cycle_len = sky_maps.shape
    map_total = lax.axis_size("map")
    blk_total = lax.axis_size("blk")
    cycles, block_count = cycle_number.shape[0], legendre_starts.shape[2]
    if kernel_fits(own_cycles, blk_total, cycles, maps_count, block_count):
        return fast_body(sky_maps, cycle_number, legendre_starts)
    tables = dft_tables(cycle_len)
    first_row = (lax.axis_index("blk") * map_total + lax.axis_index("map")) * own_cycles
    own_numbers = lax.dynamic_slice_in_dim(cycle_number, first_row, own_cycles)
    parity = (own_numbers - NSIDE + 1) % 2
    local_modes = cycle_transform(sky_maps, parity, tables)
    grouped = lax.all_gather(local_modes, "map", axis=0, tiled=True)
    regrouped = lax.all_to_all(grouped, "blk", split_axis=4, concat_axis=0, tiled=True)
    ordered = jnp.transpose(regrouped, (4, 3, 1, 2, 0))
    local_cols = ordered.shape[0] * ordered.shape[1]
    cycle_modes = ordered.reshape(local_cols, 2 * maps_count, -1)
    heights = cycle_height(cycle_number)
    column = lax.axis_index("blk") * local_cols + jnp.arange(local_cols, dtype=jnp.int32)
    m_float = (MSTART + RES * (column % MGRP) + column // MGRP).astype(jnp.float32)
    block_count = legendre_starts.shape[2]
    local_len = block_count * LBLK
    first_l = LSTART + lax.axis_index("map") * local_len
    cycle_scale = 1.0 / math.sqrt(cycle_modes.shape[-1])

    def one_block(block_index):
        start_pair = lax.dynamic_index_in_dim(legendre_starts, block_index, 2, keepdims=False)
        legendre_tile = legendre_rows(
            start_pair, heights, m_float, first_l + block_index * LBLK
        ).astype(jnp.bfloat16)
        projected = (
            jnp.einsum(
                "qlr,qnr->qnl", legendre_tile, cycle_modes, preferred_element_type=jnp.float32
            )
            * cycle_scale
        )
        return projected.astype(jnp.bfloat16)

    blocks_out = lax.map(one_block, jnp.arange(block_count, dtype=jnp.int32))
    harmonics = jnp.transpose(blocks_out, (1, 2, 0, 3)).reshape(
        local_cols, 2 * maps_count, local_len
    )
    total_cols = MGRP * RES
    spread = harmonics.reshape(local_cols, 2 * maps_count, blk_total, local_len // blk_total)
    spread = jnp.transpose(spread, (2, 3, 1, 0))
    received = lax.all_to_all(
        shortened(spread), "blk", split_axis=0, concat_axis=3, tiled=True
    ).astype(spread.dtype)
    item_count = received.shape[1]
    split_piece = received.reshape(item_count, 2, maps_count, received.shape[3])
    cross_sum = jnp.einsum(
        "gciq,gcjq->ijg", split_piece, split_piece, preferred_element_type=jnp.float32
    )
    owned = (cross_sum / total_cols)[None]
    return (harmonics, owned)


def solution(mesh):
    return jax.shard_map(
        body,
        mesh=mesh,
        in_specs=(P(("blk", "map"), None, None), P(), P(None, "blk", "map", None)),
        out_specs=(P("blk", None, "map"), P("map", None, None, "blk")),
        check_vma=False,
    )
```

```python
import functools
import math

import jax
import jax.numpy as jnp
import numpy as np
from jax import lax
from jax.experimental import pallas as pl
from jax.experimental.pallas import tpu as pltpu
from jax.sharding import PartitionSpec as P

NSIDE = 8192
RES = 128
MGRP = 4
MSTART = 4096
LSTART = 8192
LBLK = 128


def shortened(array):

    def short(part):
        return part.astype(jnp.bfloat16) if part.dtype == jnp.float32 else part

    return jax.tree.map(short, array)


def cycle_height(cycle_ids):
    return (4.0 * NSIDE - 2.0 * cycle_ids.astype(jnp.float32)) / (3.0 * NSIDE)


def dft_tables(cycle_len):
    low_len = cycle_len // RES
    residue = jnp.arange(RES, dtype=jnp.int32)
    turn_one = residue[:, None] * residue[None, :] % RES
    angle_one = 2.0 * math.pi / RES * turn_one.astype(jnp.float32)
    first_table = jnp.concatenate([jnp.cos(angle_one), -jnp.sin(angle_one)], axis=1).astype(
        jnp.bfloat16
    )
    column_group = jnp.arange(MGRP, dtype=jnp.int32)
    sample = jnp.arange(low_len, dtype=jnp.int32)
    m_value = MSTART + RES * column_group[:, None, None] + residue[None, None, :]
    turn_two = m_value * sample[None, :, None] % cycle_len
    angle_two = 2.0 * math.pi / cycle_len * turn_two.astype(jnp.float32)
    twiddle_re = jnp.cos(angle_two).astype(jnp.bfloat16)
    twiddle_im = (-jnp.sin(angle_two)).astype(jnp.bfloat16)
    return (first_table, twiddle_re, twiddle_im)


def cycle_transform(cycle_rows, parity, tables):
    first_table, twiddle_re, twiddle_im = tables
    cycle_count, maps_count, cycle_len = cycle_rows.shape
    low_len = cycle_len // RES
    folded = cycle_rows.reshape(cycle_count, maps_count, RES, low_len)
    section_one = jnp.einsum(
        "rnaj,ak->rnjk", folded, first_table, preferred_element_type=jnp.float32
    )
    section_one = section_one.astype(jnp.bfloat16)
    part_re = section_one[..., :RES]
    part_im = section_one[..., RES:]
    real_sum = jnp.einsum(
        "rnjk,cjk->rnck", part_re, twiddle_re, preferred_element_type=jnp.float32
    ) - jnp.einsum("rnjk,cjk->rnck", part_im, twiddle_im, preferred_element_type=jnp.float32)
    imag_sum = jnp.einsum(
        "rnjk,cjk->rnck", part_im, twiddle_re, preferred_element_type=jnp.float32
    ) + jnp.einsum("rnjk,cjk->rnck", part_re, twiddle_im, preferred_element_type=jnp.float32)
    column_group = jnp.arange(MGRP, dtype=jnp.int32)
    residue = jnp.arange(RES, dtype=jnp.int32)
    m_value = MSTART + RES * column_group[:, None] + residue[None, :]
    shifted = m_value[None, :, :] * parity[:, None, None] % (2 * cycle_len)
    phase_angle = math.pi / cycle_len * shifted.astype(jnp.float32)
    cos_part = jnp.cos(phase_angle)[:, None]
    sin_part = jnp.sin(phase_angle)[:, None]
    factor = 1.0 / math.sqrt(cycle_len)
    out_re = factor * (cos_part * real_sum + sin_part * imag_sum)
    out_im = factor * (cos_part * imag_sum - sin_part * real_sum)
    return jnp.stack([out_re, out_im], axis=1).astype(jnp.bfloat16)


def legendre_rows(start_pair, height, m_float, first_l):
    m_column = m_float[:, None]

    def recur_coef(degree):
        return jnp.sqrt((4.0 * degree * degree - 1.0) / ((degree - m_column) * (degree + m_column)))

    base_l = first_l.astype(jnp.float32)
    value_older = start_pair[0]
    value_newer = start_pair[1]
    prior_coef = recur_coef(base_l - 1.0)
    height_row = height[None, :]
    stacked_rows = []
    for offset in range(LBLK):
        present_coef = recur_coef(base_l + offset)
        value_now = present_coef * (height_row * value_newer - value_older / prior_coef)
        stacked_rows.append(value_now)
        value_older = value_newer
        value_newer = value_now
        prior_coef = present_coef
    return jnp.stack(stacked_rows, axis=1)


STEP_LANES = 1024
KDIM = 256
GAP = 8
RUN = 64
PACK = 8
WIDE = 256
START_GAP = 8


def sky_modes(totals, number_ref, sky_ref, first_ref, twice_ref, wave_ref, phase_ref, lhs_ref,
              rest_ref, rows_ref, me):
    maps, factor = totals
    low_len = wave_ref.shape[1]
    more = maps - 8
    for a in range(RES):
        values = sky_ref[0, :, a * low_len : (a + 1) * low_len].astype(jnp.float32)
        lhs_ref[a * 8 : a * 8 + 8, :] = values[:8]
        rest_ref[a * more : (a + 1) * more, :] = values[8:]
    rows_ref[...] = jnp.zeros_like(rows_ref)
    parity = (number_ref[me] - NSIDE + 1) % 2
    odd = jnp.full((MGRP, RES), parity, jnp.int32) == 1
    cosines = jnp.where(odd, phase_ref[:MGRP], 1.0)
    sines = jnp.where(odd, phase_ref[MGRP:], 0.0)
    none = jnp.zeros((8, RES), jnp.float32)
    for c in range(MGRP):
        real, imag, real_more, imag_more = none, none, none, none
        out = jnp.dot(
            lhs_ref[...].astype(jnp.bfloat16), wave_ref[c], preferred_element_type=jnp.float32
        )
        for a in range(RES):
            e_re, e_im = first_ref[a : a + 1, :RES], first_ref[a : a + 1, RES:]
            w_re, w_im = out[a * 8 : a * 8 + 8, :RES], out[a * 8 : a * 8 + 8, RES:]
            real = real + (e_re * w_re - e_im * w_im)
            imag = imag + (e_re * w_im + e_im * w_re)
        out = jnp.dot(
            rest_ref[...].astype(jnp.bfloat16), wave_ref[c], preferred_element_type=jnp.float32
        )
        for a in range(RES * more // 8):
            rows = slice(a * 8, a * 8 + 8)
            e_re, e_im = twice_ref[rows, :RES], twice_ref[rows, RES:]
            w_re, w_im = out[rows, :RES], out[rows, RES:]
            real_more = real_more + (e_re * w_re - e_im * w_im)
            imag_more = imag_more + (e_re * w_im + e_im * w_re)
        cos, sin = cosines[c : c + 1], sines[c : c + 1]
        row = c * 2 * maps
        for re, im, at, size in ((real, imag, 0, 8), (real_more, imag_more, 8, more)):
            if size != 8:
                re = sum(re[i : i + size] for i in range(0, 8, size))
                im = sum(im[i : i + size] for i in range(0, 8, size))
            first = row + at
            rows_ref[first : first + size, :] = factor * (cos * re + sin * im)
            rows_ref[first + maps : first + maps + size, :] = factor * (cos * im - sin * re)


def heights(number_ref, z_ref):
    lane = lax.broadcasted_iota(jnp.int32, z_ref.shape, 1) % number_ref.shape[0]
    numbers = jnp.zeros(z_ref.shape, jnp.int32)
    for r in range(number_ref.shape[0]):
        numbers = jnp.where(lane == r, number_ref[r], numbers)
    z_ref[...] = cycle_height(numbers)


def prepare(blk_total, blocks, pieces_ref, p_ref):
    local_cols = MGRP * RES // blk_total
    lane = lax.broadcasted_iota(jnp.int32, (blocks, 128), 1)
    column = lax.axis_index("blk") * local_cols + lane % local_cols
    m_row = (MSTART + RES * (column % MGRP) + column // MGRP).astype(jnp.float32)
    block = lax.broadcasted_iota(jnp.int32, (blocks, 128), 0)
    base = LSTART + (lax.axis_index("map") * blocks + block) * LBLK

    def setup(j, carry):
        p_prev, q_prev = carry
        degree = (base + j).astype(jnp.float32)
        num = 4.0 * degree * degree - 1.0
        den = (degree - m_row) * (degree + m_row)
        root = lax.rsqrt(num * den)
        kappa = p_prev * p_prev
        high = kappa.astype(jnp.bfloat16).astype(jnp.float32)
        rest = kappa - high
        mid = rest.astype(jnp.bfloat16).astype(jnp.float32)
        low = rest - mid
        rows = pl.ds(pl.multiple_of(j * blocks, blocks), blocks)
        pieces_ref[rows, :128] = jnp.where(lane < local_cols, high, mid).astype(jnp.bfloat16)
        pieces_ref[rows, 128:] = low.astype(jnp.bfloat16)
        p_now = num * root * q_prev
        q_now = den * root * p_prev
        for half in range(blocks // 8):
            p_ref[pl.ds(half * 8 * (LBLK + GAP) + j, 8, stride=LBLK + GAP), :] = p_now[
                half * 8 : half * 8 + 8
            ]
        return p_now, q_now

    one = jnp.ones((blocks, 128), jnp.float32)
    lax.fori_loop(0, LBLK, setup, (one, one), unroll=4)


def turn_factors(scale, scales_ref, p_ref):
    blocks, local_cols, _ = scales_ref.shape

    def turn(t, _):
        turned = p_ref[pl.ds(pl.multiple_of(t * (LBLK + GAP), 8), LBLK), :].T
        scales_ref[t] = turned[:local_cols] * scale
        return 0

    lax.fori_loop(0, blocks, turn, 0, unroll=4)


def start_values(starts_ref, turn_ref, init_ref):
    _, blocks, cycles, local_cols = starts_ref.shape
    lane = lax.broadcasted_iota(jnp.int32, (blocks, local_cols), 1)
    column = lax.axis_index("blk") * local_cols + lane
    m_row = (MSTART + RES * (column % MGRP) + column // MGRP).astype(jnp.float32)
    block = lax.broadcasted_iota(jnp.int32, (blocks, local_cols), 0)
    degree = (LSTART + (lax.axis_index("map") * blocks + block) * LBLK - 1).astype(jnp.float32)
    inverse = jnp.sqrt(((degree - m_row) * (degree + m_row)) / (4.0 * degree * degree - 1.0))
    pitch = local_cols + START_GAP
    for kind in range(2):
        for t in range(blocks):
            values = starts_ref[kind, t]
            if kind == 0:
                values = values * inverse[t : t + 1]
            turn_ref[kind, t * pitch : t * pitch + local_cols, :cycles] = values.T
    per_tile = 128 // cycles
    slot = lax.broadcasted_iota(jnp.int32, (8, 128), 1) // cycles
    for kind in range(2):
        for half in range(blocks // 8):
            for tile in range(local_cols // per_tile):
                row = None
                for i in range(per_tile):
                    first = half * 8 * pitch + tile * per_tile + i
                    part = turn_ref[kind, pl.ds(first, 8, stride=pitch), :]
                    if i == 0:
                        row = part
                    else:
                        row = jnp.where(slot == i, pltpu.roll(part, i * cycles, 1), row)
                init_ref[kind, half * 8 : half * 8 + 8, tile * 128 : tile * 128 + 128] = row


def recurrence(part, cycles, z_ref, pieces_ref, init_ref, leg_ref):
    blocks = init_ref.shape[1]
    halves = STEP_LANES // 128
    q_row = lax.broadcasted_iota(jnp.int32, (256, STEP_LANES), 0)
    q_lane = lax.broadcasted_iota(jnp.int32, (256, STEP_LANES), 1) // cycles + part * (
        STEP_LANES // cycles
    )
    spread = jnp.where((q_row % 64 == q_lane) & (q_row < 192), 1.0, 0.0).astype(jnp.bfloat16)

    def recur(i, carry):
        older, newer = carry
        rows = pl.ds(pl.multiple_of(i * RUN * blocks, RUN * blocks), RUN * blocks)
        kap = jnp.dot(pieces_ref[rows, :], spread, preferred_element_type=jnp.float32)
        for j in range(RUN):
            now = (kap[j * blocks : (j + 1) * blocks] * z_ref[...]) * newer - older
            for half in range(blocks // 8):
                at = pl.ds(half * 8 * (LBLK + GAP) + i * RUN + j, 8, stride=LBLK + GAP)
                for g in range(halves):
                    leg_ref[part * halves + g, at, :] = now[
                        half * 8 : half * 8 + 8, g * 128 : g * 128 + 128
                    ]
            older, newer = newer, now
        return older, newer

    lanes = slice(part * STEP_LANES, (part + 1) * STEP_LANES)
    lax.fori_loop(0, LBLK // RUN, recur, (init_ref[0, :, lanes], init_ref[1, :, lanes]))


def block_weights(maps, held_ref, weight_ref):
    groups, rows_all, _ = weight_ref.shape
    cycles, _, _ = held_ref.shape
    parts = 2 * maps
    q_group = rows_all // parts
    per_group = q_group // MGRP
    row = lax.broadcasted_iota(jnp.int32, (rows_all, per_group * 128), 0)
    lane = lax.broadcasted_iota(jnp.int32, (rows_all, per_group * 128), 1)
    q = row % q_group
    wanted = q // MGRP * 128 + (q % MGRP) * parts + row // q_group
    pick = jnp.where(lane == wanted, 1.0, 0.0).astype(jnp.bfloat16)
    row = lax.broadcasted_iota(jnp.int32, (rows_all, KDIM), 0)
    lane = lax.broadcasted_iota(jnp.int32, (rows_all, KDIM), 1)
    same_q = row % q_group == lane // cycles
    modes = jnp.swapaxes(held_ref[...].astype(jnp.float32), 0, 1).astype(jnp.bfloat16)
    for g in range(groups):
        own = jnp.concatenate([modes[g * per_group + k] for k in range(per_group)], axis=1)
        wide = lax.dot_general(
            pick, jnp.concatenate([own] * q_group, axis=0), (((1,), (1,)), ((), ())),
            preferred_element_type=jnp.float32,
        )
        weight_ref[g] = jnp.where(same_q, wide, 0.0).astype(jnp.bfloat16)


def project_tiles(u, maps, share, leg_ref, scales_ref, weight_ref, harm_ref, near_ref):
    groups, rows_all, _ = weight_ref.shape
    parts = 2 * maps
    q_group = rows_all // parts
    width = 2 * LBLK

    def tile(piece, g):
        first_t = u * (share // LBLK) + 2 * piece
        cols = pl.ds(pl.multiple_of(u * share + piece * width, width), width)
        sources = [
            pl.ds(pl.multiple_of((first_t + x) * (LBLK + GAP), 8), LBLK) for x in range(2)
        ]
        rows = slice(g * q_group, (g + 1) * q_group)
        p_rows = jnp.concatenate([scales_ref[first_t + x, rows, :] for x in range(2)], axis=1)
        leg = jnp.concatenate(
            [
                jnp.concatenate(
                    [leg_ref[g * (KDIM // 128) + h, src, :] for h in range(KDIM // 128)], axis=1
                )
                for src in sources
            ],
            axis=0,
        ).astype(jnp.bfloat16)
        out = lax.dot_general(
            weight_ref[g], leg, (((1,), (1,)), ((), ())), preferred_element_type=jnp.float32
        )
        crossed = (out.reshape(parts, q_group, width) * p_rows[None]).astype(jnp.bfloat16)
        harm_ref[:, rows, cols] = crossed
        near_ref[:, rows, piece * width : (piece + 1) * width] = crossed

    return [
        functools.partial(tile, piece, g) for piece in range(share // width) for g in range(groups)
    ]


def product_steps(maps, share, near_ref, sums_ref):
    local_cols = near_ref.shape[1]
    pairs = [(i, k) for i in range(maps) for k in range(i, maps)]
    middle = maps // 2
    sets = [
        [p for p, (i, k) in enumerate(pairs) if k < middle],
        [p for p, (i, k) in enumerate(pairs) if i >= middle],
        [p for p, (i, k) in enumerate(pairs) if i < middle <= k and i % 2 == 0],
        [p for p, (i, k) in enumerate(pairs) if i < middle <= k and i % 2 == 1],
    ]

    def some(piece, chosen):
        cols = slice(piece * WIDE, (piece + 1) * WIDE)
        total = {}
        for h in range(2):
            for t in range(local_cols // PACK):
                x = {}
                for n in sorted({v for p in chosen for v in pairs[p]}):
                    x[n] = near_ref[h * maps + n, t * PACK : (t + 1) * PACK, cols]
                for p in chosen:
                    i, k = pairs[p]
                    term = x[i] * x[k]
                    total[p] = term if p not in total else total[p] + term
        for p in chosen:
            sums_ref[p * PACK : (p + 1) * PACK, cols] = total[p]

    return [
        functools.partial(some, piece, chosen)
        for piece in range(share // WIDE)
        for chosen in sets
    ]


def interleave(one, other):
    for i in range(max(len(one), len(other))):
        for steps in (one, other):
            if i < len(steps):
                steps[i]()


def wrapped(index, total):
    return jnp.where(index >= total, index - total, index)


def visit(me_blk, i, inner, blk_total):
    half = blk_total // 2
    outer, side = me_blk // 2, lax.rem(me_blk, 2)
    if isinstance(i, int):
        sign = i % 2 * 2 - 1
    else:
        sign = lax.rem(i, 2) * 2 - 1
    other = lax.rem(outer * sign + (half - 1) - i + 2 * half, half)
    return other * 2 + (side if inner else 1 - side)


def whole_kernel(
    dims, number_hbm, sky_hbm, starts_hbm, first_hbm, twice_hbm, wave_hbm, phase_hbm,
    harm_ref, out_ref,
    number_ref, sky_ref, starts_ref, first_ref, twice_ref, wave_ref, phase_ref,
    lhs_ref, rest_ref, rows_ref, turned_ref, held_ref, pieces_ref, scales_ref, z_ref, p_ref,
    turn_ref, init_ref, leg_ref, weight_ref, near_a, near_b, sums_ref, part_ref, other_ref, relay_ref,
    load_sem, send_sem, recv_sem, part_send, part_recv, relay_sem,
):
    blk_total, map_total, maps, factor, scale = dims
    count = blk_total * map_total
    cycles = number_hbm.shape[0]
    share = out_ref.shape[1]
    me_blk, me_map = lax.axis_index("blk"), lax.axis_index("map")
    me = me_blk * map_total + me_map
    k_share = RES // blk_total
    fetched = [
        pltpu.make_async_copy(source, target, load_sem.at[i])
        for i, (source, target) in enumerate(
            [
                (sky_hbm, sky_ref), (wave_hbm, wave_ref), (first_hbm, first_ref),
                (twice_hbm, twice_ref),
                (phase_hbm, phase_ref), (number_hbm, number_ref), (starts_hbm, starts_ref),
            ]
        )
    ]
    for copy in fetched:
        copy.start()
    barrier = pltpu.get_barrier_semaphore()
    blk_at = [me_blk] + [wrapped(me_blk + i, blk_total) for i in range(1, blk_total)]
    map_at = [me_map] + [wrapped(me_map + i, map_total) for i in range(1, map_total)]
    away = [(b, m) for b in range(blk_total) for m in range(map_total) if b or m]
    for b, m in away:
        pl.semaphore_signal(
            barrier, inc=1, device_id={"blk": blk_at[b], "map": map_at[m]},
            device_id_type=pl.DeviceIdType.MESH,
        )
    prepare(blk_total, scales_ref.shape[0], pieces_ref, p_ref)
    turn_factors(scale, scales_ref, p_ref)
    for copy in fetched[:-1]:
        copy.wait()
    heights(number_ref, z_ref)
    sky_modes(
        (maps, factor), number_ref, sky_ref, first_ref, twice_ref, wave_ref, phase_ref, lhs_ref,
        rest_ref, rows_ref, me,
    )
    turned_ref[...] = rows_ref[...].T.astype(jnp.bfloat16)
    pl.semaphore_wait(barrier, count - 1)

    def modes_to(target_blk, target_map, source):
        peer = target_blk * map_total + target_map
        return pltpu.make_async_remote_copy(
            src_ref=turned_ref.at[pl.ds(pl.multiple_of(target_blk * k_share, k_share), k_share)],
            dst_ref=held_ref.at[source],
            send_sem=send_sem.at[peer],
            recv_sem=recv_sem.at[source],
            device_id={"blk": target_blk, "map": target_map},
            device_id_type=pl.DeviceIdType.MESH,
        )

    half = blk_total // 2
    for b, m in away:
        modes_to(blk_at[b], map_at[m], me).start()
    held_ref[me] = turned_ref[pl.ds(pl.multiple_of(me_blk * k_share, k_share), k_share), :]

    fetched[-1].wait()
    start_values(starts_ref, turn_ref, init_ref)
    for part in range(init_ref.shape[2] // STEP_LANES):
        recurrence(part, cycles, z_ref, pieces_ref, init_ref, leg_ref)

    for b, m in away:
        modes_to(blk_at[b], map_at[m], blk_at[b] * map_total + map_at[m]).wait_recv()
    block_weights(maps, held_ref, weight_ref)

    pairs = maps * (maps + 1) // 2
    pair_rows = part_ref.shape[1]
    row = lax.broadcasted_iota(jnp.int32, (pair_rows, pair_rows * PACK), 0)
    lane = lax.broadcasted_iota(jnp.int32, (pair_rows, pair_rows * PACK), 1)
    gather = jnp.where(lane // PACK == row, 1.0, 0.0).astype(jnp.bfloat16)
    for p in range(pairs, pair_rows):
        sums_ref[p * PACK : (p + 1) * PACK, :] = jnp.zeros((PACK, share), jnp.bfloat16)

    def part_to(peer, source):
        return pltpu.make_async_remote_copy(
            src_ref=part_ref.at[peer],
            dst_ref=other_ref.at[source],
            send_sem=part_send.at[peer],
            recv_sem=part_recv.at[source],
            device_id={"blk": peer},
            device_id_type=pl.DeviceIdType.MESH,
        )

    def place(i, inner):
        return visit(me_blk, i, inner, blk_total)

    def project(u, near_ref):
        return project_tiles(u, maps, share, leg_ref, scales_ref, weight_ref, harm_ref, near_ref)

    def finish(u):
        part_ref[u] = jnp.dot(
            gather, sums_ref[...], preferred_element_type=jnp.float32
        ).astype(jnp.bfloat16)
        return u

    beside = place(half - 1, 0)
    firsts = (place(1, 0), place(0, 1), place(2, 0), beside)
    seconds = (place(0, 0), place(1, 1), place(2, 1))
    relay = pltpu.make_async_remote_copy(
        src_ref=part_ref.at[firsts[0]],
        dst_ref=relay_ref,
        send_sem=relay_sem.at[0],
        recv_sem=relay_sem.at[1],
        device_id={"blk": beside},
        device_id_type=pl.DeviceIdType.MESH,
    )

    def chosen(i, options):
        value = options[-1]
        for at in range(len(options) - 1):
            value = jnp.where(i == at, options[at], value)
        return value

    def two_shares(i, _):
        first, second = chosen(i, firsts[:3]), chosen(i, seconds)
        third = chosen(i, firsts[1:])
        interleave(product_steps(maps, share, near_a, sums_ref), project(second, near_b))
        finish(first)

        @pl.when(i == 0)
        def _():
            relay.start()

        @pl.when(i > 0)
        def _():
            part_to(first, me_blk).start()

        interleave(product_steps(maps, share, near_b, sums_ref), project(third, near_a))
        finish(second)

        @pl.when(i != 1)
        def _():
            part_to(second, me_blk).start()

        return 0

    interleave(project(firsts[0], near_a), [])
    lax.fori_loop(0, 3, two_shares, 0)
    relay.wait_recv()
    both = part_ref[seconds[1]].astype(jnp.float32) + relay_ref[...].astype(jnp.float32)
    part_ref[seconds[1]] = both.astype(jnp.bfloat16)
    part_to(seconds[1], me_blk).start()
    interleave(product_steps(maps, share, near_a, sums_ref), [])
    finish(beside)
    part_to(beside, me_blk).start()
    interleave(project(me_blk, near_b), [])
    interleave(product_steps(maps, share, near_b, sums_ref), [])
    finish(me_blk)
    direct = (seconds[0], firsts[1], firsts[2], seconds[2], beside, seconds[1])
    out_rows = maps * maps
    row = lax.broadcasted_iota(jnp.int32, (out_rows, pair_rows), 0)
    lane = lax.broadcasted_iota(jnp.int32, (out_rows, pair_rows), 1)
    low = jnp.minimum(row // maps, row % maps)
    high = jnp.maximum(row // maps, row % maps)
    pair_at = low * maps - low * (low - 1) // 2 + high - low
    unfold = jnp.where(lane == pair_at, 1.0, 0.0).astype(jnp.bfloat16)
    unfolded = lambda x: jnp.dot(unfold, x, preferred_element_type=jnp.float32)
    total = unfolded(part_ref[me_blk])
    for peer in direct:
        part_to(peer, peer).wait_recv()
        total = total + unfolded(other_ref[peer])
    out_ref[...] = total * (1.0 / (MGRP * RES))
    for b, m in away:
        modes_to(blk_at[b], map_at[m], me).wait_send()
    for peer in direct:
        part_to(peer, me_blk).wait_send()
    relay.wait_send()


def constant_tables(cycle_len, maps):
    low_len = cycle_len // RES
    residue = np.arange(RES)
    angle = np.float32(2.0 * math.pi / RES) * (
        residue[:, None] * residue[None, :] % RES
    ).astype(np.float32)
    first = np.concatenate([np.cos(angle), -np.sin(angle)], axis=1)
    first = first.astype(jnp.bfloat16).astype(np.float32)
    m_value = MSTART + RES * np.arange(MGRP)[:, None, None] + residue[None, None, :]
    turn = m_value * np.arange(low_len)[None, :, None] % cycle_len
    angle = np.float32(2.0 * math.pi / cycle_len) * turn.astype(np.float32)
    wave = np.concatenate([np.cos(angle), -np.sin(angle)], axis=2).astype(jnp.bfloat16)
    m_value = MSTART + np.arange(MGRP)[:, None] * RES + np.arange(RES)[None, :]
    angle = np.float32(math.pi / cycle_len) * (m_value % (2 * cycle_len)).astype(np.float32)
    phase = np.concatenate([np.cos(angle), np.sin(angle)], axis=0)
    twice = np.repeat(first, maps - 8, axis=0)
    return jnp.asarray(first), jnp.asarray(twice), jnp.asarray(wave), jnp.asarray(phase)


def kernel_fits(own_cycles, blk_total, cycles, maps_count, block_count):
    local_cols = MGRP * RES // blk_total
    return (
        own_cycles == 1
        and blk_total == 8
        and maps_count in (9, 10, 12)
        and local_cols == 64
        and KDIM % cycles == 0
        and KDIM // cycles == 8
        and 2 * maps_count * MGRP <= 128
        and block_count % 8 == 0
        and block_count % blk_total == 0
        and (block_count * LBLK // blk_total) % (2 * LBLK) == 0
    )


def fast_body(sky_maps, cycle_number, legendre_starts):
    _, maps, cycle_len = sky_maps.shape
    map_total = lax.axis_size("map")
    blk_total = lax.axis_size("blk")
    local_cols, blocks, cycles = legendre_starts.shape[1:]
    count = blk_total * map_total
    local_len = blocks * LBLK
    share = local_len // blk_total
    parts = 2 * maps
    q_group = KDIM // cycles
    lanes = local_cols * cycles
    pair_rows = -(-(maps * (maps + 1) // 2) // 8) * 8
    tables = constant_tables(cycle_len, maps)
    starts = jnp.transpose(legendre_starts, (0, 2, 3, 1))
    dims = (blk_total, map_total, maps, 1.0 / math.sqrt(cycle_len), 1.0 / math.sqrt(cycles))
    vmem = pl.BlockSpec(memory_space=pltpu.VMEM)
    pitch = LBLK + GAP
    harmonics, spectra = pl.pallas_call(
        functools.partial(whole_kernel, dims),
        out_shape=(
            pltpu.VMEM((parts, local_cols, local_len), jnp.bfloat16),
            pltpu.VMEM((maps * maps, share), jnp.float32),
        ),
        in_specs=[pl.BlockSpec(memory_space=pl.ANY)] * 7,
        out_specs=(vmem, vmem),
        scratch_shapes=[pltpu.SMEM(cycle_number.shape, jnp.int32)]
        + [pltpu.VMEM(x.shape, x.dtype) for x in (sky_maps, starts, *tables)]
        + [
            pltpu.VMEM((RES * 8, cycle_len // RES), jnp.float32),
            pltpu.VMEM((RES * (maps - 8), cycle_len // RES), jnp.float32),
            pltpu.VMEM((128, RES), jnp.float32),
            pltpu.VMEM((RES, 128), jnp.bfloat16),
            pltpu.VMEM((count, RES // blk_total, 128), jnp.bfloat16),
            pltpu.VMEM((local_len, 256), jnp.bfloat16),
            pltpu.VMEM((blocks, local_cols, LBLK), jnp.float32),
            pltpu.VMEM((1, STEP_LANES), jnp.float32),
            pltpu.VMEM((blocks * pitch, 128), jnp.float32),
            pltpu.VMEM((2, blocks * (local_cols + START_GAP), 128), jnp.float32),
            pltpu.VMEM((2, blocks, lanes), jnp.float32),
            pltpu.VMEM((lanes // 128, blocks * pitch, 128), jnp.float32),
            pltpu.VMEM((local_cols // q_group, parts * q_group, KDIM), jnp.bfloat16),
            pltpu.VMEM((parts, local_cols, share), jnp.bfloat16),
            pltpu.VMEM((parts, local_cols, share), jnp.bfloat16),
            pltpu.VMEM((pair_rows * PACK, share), jnp.bfloat16),
            pltpu.VMEM((blk_total, pair_rows, share), jnp.bfloat16),
            pltpu.VMEM((blk_total, pair_rows, share), jnp.bfloat16),
            pltpu.VMEM((pair_rows, share), jnp.bfloat16),
            pltpu.SemaphoreType.DMA((7,)),
            pltpu.SemaphoreType.DMA((count,)),
            pltpu.SemaphoreType.DMA((count,)),
            pltpu.SemaphoreType.DMA((blk_total,)),
            pltpu.SemaphoreType.DMA((blk_total,)),
            pltpu.SemaphoreType.DMA((2,)),
        ],
        compiler_params=pltpu.CompilerParams(
            collective_id=0, has_side_effects=True, vmem_limit_bytes=48 * 1024 * 1024
        ),
    )(
        *(
            pltpu.with_memory_space_constraint(x, pltpu.HBM)
            for x in (cycle_number, sky_maps, starts, *tables)
        )
    )
    harmonics, spectra = write_out(harmonics, spectra, maps)
    return (jnp.transpose(harmonics, (1, 0, 2)), jnp.transpose(spectra, (2, 0, 1, 3)))


def write_kernel(maps, harm_ref, sums_ref, harm_out, spectra_out, spectra_ref, sem, spectra_sem):
    pieces = sem.shape[0]
    rows = harm_ref.shape[0] // pieces
    copies = [
        pltpu.make_async_copy(
            harm_ref.at[pl.ds(i * rows, rows)], harm_out.at[pl.ds(i * rows, rows)], sem.at[i]
        )
        for i in range(pieces)
    ]
    for copy in copies:
        copy.start()
    for i in range(maps):
        for k in range(maps):
            spectra_ref[i, k] = sums_ref[i * maps + k : i * maps + k + 1]
    last = pltpu.make_async_copy(spectra_ref, spectra_out, spectra_sem)
    last.start()
    for copy in copies:
        copy.wait()
    last.wait()


def write_out(harmonics, spectra, maps):
    vmem = pl.BlockSpec(memory_space=pltpu.VMEM)
    shape = (maps, maps, 1, spectra.shape[1])
    return pl.pallas_call(
        functools.partial(write_kernel, maps),
        out_shape=(
            jax.ShapeDtypeStruct(harmonics.shape, harmonics.dtype),
            jax.ShapeDtypeStruct(shape, jnp.float32),
        ),
        in_specs=[vmem, vmem],
        out_specs=(pl.BlockSpec(memory_space=pl.ANY),) * 2,
        scratch_shapes=[
            pltpu.VMEM(shape, jnp.float32),
            pltpu.SemaphoreType.DMA((2,)),
            pltpu.SemaphoreType.DMA,
        ],
        compiler_params=pltpu.CompilerParams(vmem_limit_bytes=8 * 1024 * 1024),
    )(harmonics, spectra)


def body(sky_maps, cycle_number, legendre_starts):
    own_cycles, maps_count, cycle_len = sky_maps.shape
    map_total = lax.axis_size("map")
    blk_total = lax.axis_size("blk")
    cycles, block_count = cycle_number.shape[0], legendre_starts.shape[2]
    if kernel_fits(own_cycles, blk_total, cycles, maps_count, block_count):
        return fast_body(sky_maps, cycle_number, legendre_starts)
    tables = dft_tables(cycle_len)
    first_row = (lax.axis_index("blk") * map_total + lax.axis_index("map")) * own_cycles
    own_numbers = lax.dynamic_slice_in_dim(cycle_number, first_row, own_cycles)
    parity = (own_numbers - NSIDE + 1) % 2
    local_modes = cycle_transform(sky_maps, parity, tables)
    grouped = lax.all_gather(local_modes, "map", axis=0, tiled=True)
    regrouped = lax.all_to_all(grouped, "blk", split_axis=4, concat_axis=0, tiled=True)
    ordered = jnp.transpose(regrouped, (4, 3, 1, 2, 0))
    local_cols = ordered.shape[0] * ordered.shape[1]
    cycle_modes = ordered.reshape(local_cols, 2 * maps_count, -1)
    heights = cycle_height(cycle_number)
    column = lax.axis_index("blk") * local_cols + jnp.arange(local_cols, dtype=jnp.int32)
    m_float = (MSTART + RES * (column % MGRP) + column // MGRP).astype(jnp.float32)
    block_count = legendre_starts.shape[2]
    local_len = block_count * LBLK
    first_l = LSTART + lax.axis_index("map") * local_len
    cycle_scale = 1.0 / math.sqrt(cycle_modes.shape[-1])

    def one_block(block_index):
        start_pair = lax.dynamic_index_in_dim(legendre_starts, block_index, 2, keepdims=False)
        legendre_tile = legendre_rows(
            start_pair, heights, m_float, first_l + block_index * LBLK
        ).astype(jnp.bfloat16)
        projected = (
            jnp.einsum(
                "qlr,qnr->qnl", legendre_tile, cycle_modes, preferred_element_type=jnp.float32
            )
            * cycle_scale
        )
        return projected.astype(jnp.bfloat16)

    blocks_out = lax.map(one_block, jnp.arange(block_count, dtype=jnp.int32))
    harmonics = jnp.transpose(blocks_out, (1, 2, 0, 3)).reshape(
        local_cols, 2 * maps_count, local_len
    )
    total_cols = MGRP * RES
    spread = harmonics.reshape(local_cols, 2 * maps_count, blk_total, local_len // blk_total)
    spread = jnp.transpose(spread, (2, 3, 1, 0))
    received = lax.all_to_all(
        shortened(spread), "blk", split_axis=0, concat_axis=3, tiled=True
    ).astype(spread.dtype)
    item_count = received.shape[1]
    split_piece = received.reshape(item_count, 2, maps_count, received.shape[3])
    cross_sum = jnp.einsum(
        "gciq,gcjq->ijg", split_piece, split_piece, preferred_element_type=jnp.float32
    )
    owned = (cross_sum / total_cols)[None]
    return (harmonics, owned)


def solution(mesh):
    return jax.shard_map(
        body,
        mesh=mesh,
        in_specs=(P(("blk", "map"), None, None), P(), P(None, "blk", "map", None)),
        out_specs=(P("blk", None, "map"), P("map", None, None, "blk")),
        check_vma=False,
    )
```
